256 devices in a mesh: seq: 64 (over x, z, core), ch: 4 (over y).
Axes of the slice: x: 4, y: 4, z: 8, core: 2. Of those that a mesh axis runs over, the one named last changes fastest.
Arguments:
- proj: bfloat16 [3, 128, 65536], P(None, 'ch', 'seq'), may hold values from -6 to 6
- cotangent: bfloat16 [128, 65536], P('ch', 'seq'), may hold values from -6 to 6
- short_w: float32 [3, 128, 3], P(None, 'ch'), may hold values from -3.5 to 3.5
- filter_in: float32 [32, 64], replicated, may hold values from -5 to 5
- filter_out: float32 [64, 128], P(None, 'ch'), may hold values from -0.75 to 0.75
- rates: float32 [128], P('ch'), may hold values from 0.25 to 2184
Outputs:
- grad_proj: bfloat16 [3, 128, 65536], P(None, 'ch', 'seq')
- grad_short: float32 [3, 128, 3], P(None, 'ch')
- grad_filter_out: float32 [64, 128], P(None, 'ch')
- grad_filter_in: float32 [32, 64], replicated
The draws below stay inside these ranges and needn't reach their ends.
All inputs are finite; a program needn't handle non-finite values.
Results may differ from the reference program's by a relative error of at most 0.0013.
Values may be sent and summed in bfloat16 or wider, within the bound.
A program may use at most 64 MiB of HBM per device.

```python
import math
import jax
import jax.numpy as jnp
from jax import lax

CH = 128
ORDER = 64
FEAT = 32
TAPS = 3
SEQ_LEN = 65536


def draw_rates(key, part):
    key_choose, key_slow, key_fast = jax.random.split(key, 3)
    slow_share = 0.5
    slow_mask = jax.random.uniform(key_choose, (CH,), jnp.float32) < slow_share
    low_log = math.log(0.25)
    mid_log = math.log(2.3)
    top_log = math.log(SEQ_LEN // 30)
    slow_rate = jnp.exp(low_log + (mid_log - low_log) * jax.random.uniform(key_slow, (CH,), jnp.float32))
    fast_rate = jnp.exp(mid_log + (top_log - mid_log) * jax.random.uniform(key_fast, (CH,), jnp.float32))
    picked = jnp.where(slow_mask, slow_rate, fast_rate)
    return jnp.clip(picked, 0.25, SEQ_LEN // 30).astype(jnp.float32)


def steps_of(stream_key, extent, pieces, least, high):
    level, own = 1.0, jax.random.fold_in(stream_key, 6)
    for axis_at, blocks in pieces:
        heights = jnp.exp(jax.random.uniform(jax.random.fold_in(own, axis_at), (blocks,), jnp.float32, least / len(pieces), high / len(pieces)))
        level = level * jnp.repeat(heights, extent[axis_at] // blocks).reshape([-1 if axis == axis_at else 1 for axis in range(len(extent))])
    return level


def scatter_about(stream_key, dims, scale, reach, pieces=(), kind=jnp.bfloat16):
    array = jax.random.normal(stream_key, dims, jnp.float32) * scale
    if len(pieces) > 0:
        array = steps_of(stream_key, dims, pieces, -0.22, 0.18) * array
    return jnp.clip(array, min=-reach, max=reach).astype(kind)


def setup_inputs(seed: int = 0) -> dict:
    key_list = jax.random.split(jax.random.key(seed), 7)
    return {
        "proj": scatter_about(key_list[0], (3, CH, SEQ_LEN), 1.0, 6.0, ((1, 4), (2, 64))),
        "cotangent": scatter_about(key_list[1], (CH, SEQ_LEN), 1.0, 6.0, ((0, 4), (1, 64))),
        "short_w": scatter_about(key_list[2], (3, CH, TAPS), TAPS ** -0.5, 3.5, ((1, 4),), jnp.float32),
        "filter_in": scatter_about(key_list[3], (FEAT, ORDER), 1.0, 5.0, (), jnp.float32),
        "filter_out": scatter_about(key_list[4], (ORDER, CH), ORDER ** -0.5, 0.75, ((1, 4),), jnp.float32),
        "rates": draw_rates(jax.random.fold_in(key_list[6], 71), 0),
    }


PRECISE = lax.Precision.HIGHEST

def position_features(positions, length, feature_count):
    feature_index = jnp.arange(feature_count, dtype=jnp.int32)
    multiplier = (1 + feature_index // 2 * 499) % length
    upper = positions // 1024
    lower = positions % 1024
    phases = (upper[:, None] * (multiplier * 1024 % length)[None, :] + lower[:, None] * multiplier[None, :]) % length
    angles = phases.astype(jnp.float32) * (2.0 * math.pi / length)
    return jnp.where((feature_index % 2 == 0)[None, :], jnp.cos(angles), jnp.sin(angles))

def reference(proj, cotangent, short_w, filter_in, filter_out, rates):
    length = SEQ_LEN
    tap_count = TAPS
    norm_scale = 1.0 / math.sqrt(length)
    positions = jnp.arange(length, dtype=jnp.int32)
    features = position_features(positions, length, FEAT)
    preact = jnp.dot(features, filter_in, precision=PRECISE, preferred_element_type=jnp.float32)
    hidden = jnp.sin(preact)
    relative = positions.astype(jnp.float32) / length
    block = min(CH, 32)
    blocks = CH // block
    proj_blocks = proj.reshape(3, blocks, block, length).transpose(1, 0, 2, 3)
    cot_blocks = cotangent.reshape(blocks, block, length)
    short_blocks = short_w.reshape(3, blocks, block, tap_count).transpose(1, 0, 2, 3)
    out_blocks = filter_out.reshape(ORDER, blocks, block).transpose(1, 0, 2)
    rate_blocks = rates.reshape(blocks, block)

    def one_block(items):
        proj_part, cot_part, short_part, out_part, rate_part = items
        padded = jnp.pad(proj_part.astype(jnp.float32), ((0, 0), (0, 0), (tap_count - 1, 0)))

        def delayed(offset):
            return padded[:, :, tap_count - 1 - offset:tap_count - 1 - offset + length]
        mixed_all = short_part[:, :, 0, None] * delayed(0)
        for offset in range(1, tap_count):
            mixed_all = mixed_all + short_part[:, :, offset, None] * delayed(offset)
        query_part, key_part, value_part = (mixed_all[0], mixed_all[1], mixed_all[2])
        gated_prod = key_part * value_part
        modulated = jnp.einsum('to,oc->ct', hidden, out_part, precision=PRECISE)
        spread = jnp.sqrt(jnp.expm1(-2.0 * rate_part) / jnp.expm1(-2.0 * rate_part / length))
        envelope = jnp.exp(-rate_part[:, None] * relative[None, :]) / spread[:, None]
        kernel = envelope * modulated
        cotangent_full = cot_part.astype(jnp.float32)
        grad_conv = cotangent_full * query_part
        points = 2 * length
        gated_spec = jnp.fft.rfft(gated_prod, n=points, axis=-1)
        kernel_spec = jnp.fft.rfft(kernel, n=points, axis=-1)
        grad_spec = jnp.fft.rfft(grad_conv, n=points, axis=-1)
        conv_out = jnp.fft.irfft(gated_spec * kernel_spec, n=points, axis=-1)[:, :length].astype(jnp.float32)
        grad_gated = jnp.fft.irfft(grad_spec * jnp.conj(kernel_spec), n=points, axis=-1)[:, :length].astype(jnp.float32)
        grad_kernel = jnp.fft.irfft(grad_spec * jnp.conj(gated_spec), n=points, axis=-1)[:, :length].astype(jnp.float32)
        grad_mixed = jnp.stack([cotangent_full * conv_out, grad_gated * value_part, grad_gated * key_part])
        tail_padded = jnp.pad(grad_mixed, ((0, 0), (0, 0), (0, tap_count - 1)))
        result = short_part[:, :, 0, None] * tail_padded[:, :, 0:length]
        for offset in range(1, tap_count):
            result = result + short_part[:, :, offset, None] * tail_padded[:, :, offset:offset + length]
        grad_proj = result.astype(jnp.bfloat16)
        grad_short = jnp.stack([lax.optimization_barrier(jnp.sum(grad_mixed * delayed(offset), axis=2)) for offset in range(tap_count)], axis=2) * norm_scale
        weighted = envelope * grad_kernel
        grad_out = jnp.einsum('to,ct->oc', hidden, weighted, precision=PRECISE) * norm_scale
        grad_hidden = jnp.einsum('ct,oc->to', weighted, out_part, precision=PRECISE)
        grad_in = jnp.einsum('tf,to->fo', features, grad_hidden * jnp.cos(preact), precision=PRECISE)
        return (grad_proj, grad_short, grad_out, grad_in)
    results = lax.map(one_block, (proj_blocks, cot_blocks, short_blocks, out_blocks, rate_blocks))
    grad_proj = results[0].transpose(1, 0, 2, 3).reshape(3, CH, length)
    grad_short = results[1].transpose(1, 0, 2, 3).reshape(3, CH, tap_count)
    grad_filter_out = results[2].transpose(1, 0, 2).reshape(ORDER, CH)
    grad_filter_in = lax.optimization_barrier(jnp.sum(results[3], axis=0)) * norm_scale
    return (grad_proj, grad_short, grad_filter_out, grad_filter_in)
```

```python
import functools
import math

import jax
import jax.numpy as jnp
import ml_dtypes
import numpy as np
from jax import lax
from jax.experimental import pallas as pl
from jax.experimental.pallas import tpu as pltpu
from jax.sharding import PartitionSpec as P

MESH = pl.DeviceIdType.MESH
F32 = jnp.float32
BF16 = jnp.bfloat16
PRECISE = lax.Precision.HIGHEST
LANES = 128
ROWS = 8
TOKENS = ROWS * LANES
Z_SIZE = 8


def bf16_pair(table):
    high = table.astype(ml_dtypes.bfloat16)
    low = (table - high.astype(np.float64)).astype(ml_dtypes.bfloat16)
    return np.stack([high, low])


def make_tables(devices):
    outer = devices * ROWS
    length = outer * LANES
    half = outer // 2
    block = np.arange(devices // 2)
    within = np.arange(ROWS)
    fwd, back, twiddle = [], [], []
    for core in range(2):
        own = ((2 * block[:, None] + core) * ROWS + within[None, :]).reshape(-1)
        other = ((2 * block[:, None] + 1 - core) * ROWS + within[None, :]).reshape(-1)
        a = np.concatenate([own, other])
        k1 = core * half + np.arange(half)
        num = (a[None, :] * (4 * k1[:, None] + 1)) % (4 * outer)
        angle = num * (2.0 * np.pi / (4 * outer))
        matrix = np.concatenate([np.cos(angle), -np.sin(angle)], 0)
        fwd.append(bf16_pair(matrix))
        back.append(bf16_pair(np.ascontiguousarray(matrix.T)))
        num = (np.arange(LANES)[None, :] * (4 * k1[:, None] + 1)) % (4 * length)
        angle = num * (2.0 * np.pi / (4 * length))
        twiddle.append(np.stack([np.cos(angle), -np.sin(angle)]).astype(np.float32))
    b = np.arange(LANES)
    angle = (b[:, None] * b[None, :] % LANES) * (2.0 * np.pi / LANES)
    c, s = np.cos(angle), np.sin(angle)
    inner = np.block([[c, -s], [s, c]])
    return (
        np.stack(fwd),
        np.stack(back),
        np.stack(twiddle),
        bf16_pair(inner),
        bf16_pair(np.ascontiguousarray(inner.T)),
    )


def sin_small(x):
    y = x * x
    p = 1.0 / 6227020800.0
    p = p * y - 1.0 / 39916800.0
    p = p * y + 1.0 / 362880.0
    p = p * y - 1.0 / 5040.0
    p = p * y + 1.0 / 120.0
    p = p * y - 1.0 / 6.0
    return x + x * y * p


def minus_pi_times(x, n):
    return ((x - n * 3.140625) - n * 9.67502593994140625e-4) - n * 1.509957990978376e-7


def parity_sign(n):
    return 1.0 - 2.0 * (n - 2.0 * jnp.floor(n * 0.5))


def sin_cos(x):
    scaled = x * (1.0 / math.pi)
    n = jnp.floor(scaled + 0.5)
    sine = parity_sign(n) * sin_small(minus_pi_times(x, n))
    m = jnp.floor(scaled) + 1.0
    cosine = parity_sign(m) * sin_small(minus_pi_times(x, m - 0.5))
    return sine, cosine


def split(x):
    high = x.astype(BF16)
    return high, (x - high.astype(F32)).astype(BF16)


def dot_one(a, b):
    return lax.dot_general(a, b, (((1,), (0,)), ((), ())), preferred_element_type=F32)


def dot3(a, b):
    return dot_one(a[0], b[0]) + (dot_one(a[0], b[1]) + dot_one(a[1], b[0]))


def dot_exact(a, b, dims):
    return lax.dot_general(a, b, (dims, ((), ())), precision=PRECISE, preferred_element_type=F32)


def kernel(
    devices, y_size,
    proj, cot, sw, fin, fout, env_in, f1_hbm, f1t_hbm, tw_hbm, f2, f2t,
    gp_out, r1_out, r2_out,
    f1, f1t, tw, feat, hid, hcos, env, ext, kv, halo, sendb, abuf, spec, own, sx, xb, outb, retb,
    gm, halo_gm, r_own, r_core, r_x, r_z, r_y,
    tab_sem, halo_sem, in_send, in_recv, fwd_send, fwd_recv, x_send, x_recv, out_send, out_recv,
    hg_sem, red_send, red_recv,
):
    chips = devices // 2
    channels = cot.shape[0]
    length = devices * TOKENS
    half = devices * ROWS // 2
    blocks = channels // 8
    me = lax.axis_index("seq")
    yi = lax.axis_index("ch")
    q = lax.div(me, 2)
    core = lax.rem(me, 2)
    sib = me + 1 - 2 * core
    nxt = lax.rem(me + 1, devices)
    prv = lax.rem(me + devices - 1, devices)
    x_size = chips // Z_SIZE
    zi = lax.rem(q, Z_SIZE)
    xi = lax.div(q, Z_SIZE)

    def seq_dev(chip):
        return {"seq": 2 * chip + core}

    barrier = pltpu.get_barrier_semaphore()

    def greet(r, carry):
        pl.semaphore_signal(barrier, inc=1, device_id=seq_dev(lax.rem(q + r, chips)), device_id_type=MESH)
        return carry

    lax.fori_loop(1, chips, greet, 0)
    pl.semaphore_signal(barrier, inc=1, device_id={"seq": nxt}, device_id_type=MESH)
    pl.semaphore_signal(barrier, inc=1, device_id={"seq": prv}, device_id_type=MESH)

    def greet_y(r, carry):
        pl.semaphore_signal(barrier, inc=1, device_id={"ch": lax.rem(yi + r, y_size)}, device_id_type=MESH)
        return carry

    lax.fori_loop(1, y_size, greet_y, 0)

    tables = [
        pltpu.make_async_copy(f1_hbm.at[core], f1, tab_sem.at[0]),
        pltpu.make_async_copy(f1t_hbm.at[core], f1t, tab_sem.at[1]),
        pltpu.make_async_copy(tw_hbm.at[core], tw, tab_sem.at[2]),
    ]
    for copy in tables:
        copy.start()

    row = lax.broadcasted_iota(jnp.int32, feat.shape, 0)
    position = me * TOKENS + lax.broadcasted_iota(jnp.int32, feat.shape, 1)
    odd = row & 1
    phase = position * (1 + (row >> 1) * 499) - odd * (length // 4) + length // 2
    phase = (phase & (length - 1)) - length // 2
    feat[...] = sin_small((length // 4 - jnp.abs(phase)).astype(F32) * (2.0 * math.pi / length))
    preact = dot_exact(fin[...], feat[...], ((0,), (0,)))
    sine, cosine = sin_cos(preact)
    hid[...] = sine
    hcos[...] = cosine
    relative = (me * TOKENS + lax.broadcasted_iota(jnp.int32, env.shape, 1)).astype(F32) * (1.0 / length)
    env[...] = jnp.exp(env_in[:, 0:1] * relative) * env_in[:, 1:2]

    pl.semaphore_wait(barrier, chips - 1 + 2 + y_size - 1)

    halo_copy = pltpu.make_async_remote_copy(
        proj.at[:, :, TOKENS - LANES :], halo, halo_sem.at[0], halo_sem.at[1],
        device_id={"seq": nxt}, device_id_type=MESH,
    )
    halo_copy.start()

    def scatter_rows(slot, value, cb):
        for j in range(ROWS):
            sendb[slot, pl.ds(cb * 64 + j, 8, stride=8), :] = value[:, j * LANES : (j + 1) * LANES]

    def gather_rows(slot, cb):
        return jnp.concatenate(
            [retb[slot, pl.ds(cb * 64 + j, 8, stride=8), :] for j in range(ROWS)], 1
        )

    my_rows = pl.ds(pl.multiple_of(q * ROWS, ROWS), ROWS)

    def exchange(src, dst, lo, hi, send_sem, recv_sem):
        def one(r, carry):
            chip = lax.rem(q + r, chips)
            rows = pl.ds(pl.multiple_of(chip * ROWS, ROWS), ROWS)
            pltpu.make_async_remote_copy(
                src.at[lo:hi, rows], dst.at[lo:hi, my_rows], send_sem, recv_sem,
                device_id=seq_dev(chip), device_id_type=MESH,
            ).start()
            return carry

        lax.fori_loop(1, chips, one, 0)
        dst[lo:hi, my_rows] = src[lo:hi, my_rows]

    def wait_bytes(src, lo, hi, sem):
        part = src.at[lo:hi, pl.ds(0, (chips - 1) * ROWS)]
        pltpu.make_async_copy(part, part, sem).wait()

    modulated = dot_exact(fout[...], hid[...], ((0,), (0,)))
    filt = env[...] * modulated
    for cb in range(blocks):
        scatter_rows(0, filt[cb * 8 : cb * 8 + 8], cb)
    exchange(sendb, abuf, 0, 1, in_send.at[0], in_recv.at[0])

    halo_copy.wait()
    first = (me > 0).astype(F32)
    cot32 = cot[...].astype(F32)
    mixed = []
    for s in range(3):
        ext[s, :, LANES:] = proj[s].astype(F32)
        ext[s, :, :LANES] = halo[s].astype(F32) * first
        full = ext[s]
        total = sw[s, :, 0:1] * full[:, LANES:]
        for j in range(1, 3):
            total = total + sw[s, :, j : j + 1] * pltpu.roll(full, j, 1)[:, LANES:]
        mixed.append(total)
    kv[0] = mixed[1]
    kv[1] = mixed[2]
    gated = mixed[1] * mixed[2]
    grad_conv = cot32 * mixed[0]
    for cb in range(blocks):
        scatter_rows(1, gated[cb * 8 : cb * 8 + 8], cb)
        scatter_rows(2, grad_conv[cb * 8 : cb * 8 + 8], cb)
    exchange(sendb, abuf, 1, 3, in_send.at[1], in_recv.at[1])

    for copy in tables:
        copy.wait()

    def to_sibling(src, dst, slot):
        return pltpu.make_async_remote_copy(
            src, dst, fwd_send.at[slot], fwd_recv.at[slot], device_id={"seq": sib}, device_id_type=MESH
        )

    def forward(signals):
        a = jnp.concatenate([abuf[s] for s in signals], 1)
        u = dot3((f1[0], f1[1]), split(a))
        for at, s in enumerate(signals):
            ur = u[:half, at * LANES : (at + 1) * LANES]
            ui = u[half:, at * LANES : (at + 1) * LANES]
            v = jnp.concatenate([ur * tw[0] - ui * tw[1], ur * tw[1] + ui * tw[0]], 1)
            spec[s] = dot3(split(v), (f2[0], f2[1]))

    wait_bytes(abuf, 0, 1, in_recv.at[0])
    send_k = to_sibling(abuf.at[0:1, 0:half], abuf.at[0:1, half:], 0)
    send_k.start()
    send_k.wait()
    forward([0])
    wait_bytes(abuf, 1, 3, in_recv.at[1])
    send_gd = to_sibling(abuf.at[1:3, 0:half], abuf.at[1:3, half:], 1)
    send_gd.start()
    send_gd.wait()
    forward([1, 2])

    def parts(s):
        return spec[s, :, :LANES], spec[s, :, LANES:]

    def inverse_rows(re, im):
        z = dot3(split(jnp.concatenate([re, im], 1)), (f2t[0], f2t[1]))
        zr, zi_ = z[:, :LANES], z[:, LANES:]
        return jnp.concatenate([zr * tw[0] + zi_ * tw[1], zi_ * tw[0] - zr * tw[1]], 0)

    kr, ki = parts(0)
    gr, gi = parts(1)
    dr, di = parts(2)

    def finish(signals, rows_of):
        y = dot3((f1t[0], f1t[1]), split(jnp.concatenate(rows_of, 1)))
        for at, s in enumerate(signals):
            own[s] = y[:half, at * LANES : (at + 1) * LANES]
            sx[s] = y[half:, at * LANES : (at + 1) * LANES]

    def swap(lo, hi, slot):
        return pltpu.make_async_remote_copy(
            sx.at[lo:hi], xb.at[lo:hi], x_send.at[slot], x_recv.at[slot],
            device_id={"seq": sib}, device_id_type=MESH,
        )

    finish([0], [inverse_rows(dr * gr + di * gi, di * gr - dr * gi)])
    swap_k = swap(0, 1, 0)
    swap_k.start()
    conv_rows = inverse_rows(gr * kr - gi * ki, gr * ki + gi * kr)
    back_rows = inverse_rows(dr * kr + di * ki, di * kr - dr * ki)
    swap_k.wait()
    outb[0] = (own[0] + xb[0]) * (1.0 / length)
    exchange(outb, retb, 0, 1, out_send.at[0], out_recv.at[0])
    finish([1, 2], [conv_rows, back_rows])
    swap_c = swap(1, 3, 1)
    swap_c.start()
    swap_c.wait()
    for s in (1, 2):
        outb[s] = (own[s] + xb[s]) * (1.0 / length)
    exchange(outb, retb, 1, 3, out_send.at[1], out_recv.at[1])

    wait_bytes(retb, 0, 1, out_recv.at[0])
    weighted = env[...] * jnp.concatenate([gather_rows(0, cb) for cb in range(blocks)], 0)
    out_part = dot_exact(weighted, hid[...], ((1,), (1,)))
    grad_hidden = dot_exact(fout[...], weighted, ((1,), (0,))) * hcos[...]
    in_part = dot_exact(feat[...], grad_hidden, ((1,), (1,)))
    half_in = in_part.shape[0] // 2

    wait_bytes(retb, 1, 3, out_recv.at[1])
    conv_out = jnp.concatenate([gather_rows(1, cb) for cb in range(blocks)], 0)
    grad_gated = jnp.concatenate([gather_rows(2, cb) for cb in range(blocks)], 0)
    gm[0] = cot[...].astype(F32) * conv_out
    gm[1] = grad_gated * kv[1]
    gm[2] = grad_gated * kv[0]
    halo_back = pltpu.make_async_remote_copy(
        gm.at[:, :, 0:LANES], halo_gm, hg_sem.at[0], hg_sem.at[1],
        device_id={"seq": prv}, device_id_type=MESH,
    )
    halo_back.start()

    lane = lax.broadcasted_iota(jnp.int32, (channels, LANES - out_part.shape[1]), 1)
    short = jnp.zeros((channels, LANES - out_part.shape[1]), F32)
    for s in range(3):
        full = ext[s]
        for j in range(3):
            shifted = full[:, LANES:] if j == 0 else pltpu.roll(full, j, 1)[:, LANES:]
            total = jnp.sum(gm[s] * shifted, axis=1, keepdims=True)
            short = jnp.where(lane == s * 3 + j, total, short)
    r_own[0:channels] = jnp.concatenate([out_part, short], 1)
    r_own[channels:] = jnp.concatenate([in_part[:half_in], in_part[half_in:]], 1)

    red_core = pltpu.make_async_remote_copy(
        r_own, r_core, red_send.at[0], red_recv.at[0], device_id={"seq": sib}, device_id_type=MESH
    )
    red_core.start()

    halo_back.wait()
    last = (me < devices - 1).astype(F32)
    for s in range(3):
        full = jnp.concatenate([gm[s], halo_gm[s] * last], 1)
        total = sw[s, :, 0:1] * full[:, :TOKENS]
        for j in range(1, 3):
            total = total + sw[s, :, j : j + 1] * pltpu.roll(full, TOKENS + LANES - j, 1)[:, :TOKENS]
        gp_out[s] = total.astype(BF16)

    red_core.wait()

    def group_sum(buf, index, size, device_of, slot):
        def one(r, carry):
            pltpu.make_async_remote_copy(
                buf.at[index], buf.at[index], red_send.at[slot], red_recv.at[slot],
                device_id=device_of(lax.rem(index + r, size)), device_id_type=MESH,
            ).start()
            return carry

        lax.fori_loop(1, size, one, 0)
        rest = buf.at[pl.ds(0, size - 1)]
        pltpu.make_async_copy(rest, rest, red_recv.at[slot]).wait()
        pltpu.make_async_copy(rest, rest, red_send.at[slot]).wait()
        total = buf[0]
        for i in range(1, size):
            total = total + buf[i]
        return total

    r_x[xi] = r_own[...] + r_core[...]
    r_z[zi] = group_sum(r_x, xi, x_size, lambda i: seq_dev(i * Z_SIZE + zi), 1)
    total = group_sum(r_z, zi, Z_SIZE, lambda i: seq_dev(xi * Z_SIZE + i), 2)
    scale = 1.0 / math.sqrt(length)
    r1_out[...] = total[:channels] * scale
    r_y[yi] = total[channels:]
    r2_out[...] = group_sum(r_y, yi, y_size, lambda i: {"ch": i}, 3) * scale

    wait_bytes(sendb, 0, 1, in_send.at[0])
    wait_bytes(sendb, 1, 3, in_send.at[1])
    wait_bytes(outb, 0, 1, out_send.at[0])
    wait_bytes(outb, 1, 3, out_send.at[1])


def shards(devices, y_size, tables, proj, cotangent, short_w, filter_in, filter_out, rates):
    channels = cotangent.shape[0]
    feats, order = filter_in.shape
    length = devices * TOKENS
    chips = devices // 2
    half = devices * ROWS // 2
    outer = devices * ROWS
    spread = jnp.sqrt(jnp.expm1(-2.0 * rates) / jnp.expm1(-2.0 * rates / length))
    env_in = jnp.stack([-rates, 1.0 / spread], 1)
    r_rows = channels + feats // 2
    vmem = pl.BlockSpec(memory_space=pltpu.VMEM)
    anywhere = pl.BlockSpec(memory_space=pl.ANY)
    dma = pltpu.SemaphoreType.DMA
    grad_proj, r1, r2 = pl.pallas_call(
        functools.partial(kernel, devices, y_size),
        out_shape=(
            jax.ShapeDtypeStruct(proj.shape, BF16),
            jax.ShapeDtypeStruct((channels, LANES), F32),
            jax.ShapeDtypeStruct((feats // 2, LANES), F32),
        ),
        in_specs=[vmem] * 6 + [anywhere] * 3 + [vmem] * 2,
        out_specs=(vmem, vmem, vmem),
        scratch_shapes=[
            pltpu.VMEM((2, outer, outer), BF16),
            pltpu.VMEM((2, outer, outer), BF16),
            pltpu.VMEM((2, half, LANES), F32),
            pltpu.VMEM((feats, TOKENS), F32),
            pltpu.VMEM((order, TOKENS), F32),
            pltpu.VMEM((order, TOKENS), F32),
            pltpu.VMEM((channels, TOKENS), F32),
            pltpu.VMEM((3, channels, LANES + TOKENS), F32),
            pltpu.VMEM((2, channels, TOKENS), F32),
            pltpu.VMEM((3, channels, LANES), BF16),
            pltpu.VMEM((3, chips * ROWS, LANES), F32),
            pltpu.VMEM((3, outer, LANES), F32),
            pltpu.VMEM((3, half, 2 * LANES), F32),
            pltpu.VMEM((3, half, LANES), F32),
            pltpu.VMEM((3, half, LANES), F32),
            pltpu.VMEM((3, half, LANES), F32),
            pltpu.VMEM((3, half, LANES), F32),
            pltpu.VMEM((3, half, LANES), F32),
            pltpu.VMEM((3, channels, TOKENS), F32),
            pltpu.VMEM((3, channels, LANES), F32),
            pltpu.VMEM((r_rows, LANES), F32),
            pltpu.VMEM((r_rows, LANES), F32),
            pltpu.VMEM((chips // Z_SIZE, r_rows, LANES), F32),
            pltpu.VMEM((Z_SIZE, r_rows, LANES), F32),
            pltpu.VMEM((y_size, feats // 2, LANES), F32),
            dma((3,)), dma((2,)), dma((2,)), dma((2,)), dma((2,)), dma((2,)), dma((2,)), dma((2,)),
            dma((2,)), dma((2,)), dma((2,)), dma((4,)), dma((4,)),
        ],
        compiler_params=pltpu.CompilerParams(
            collective_id=0, has_side_effects=True, vmem_limit_bytes=40 << 20
        ),
    )(proj, cotangent, short_w, filter_in, filter_out, env_in, *tables)
    grad_out = r1[:, :order].T
    grad_short = r1[:, order : order + 9].reshape(channels, 3, 3).transpose(1, 0, 2)
    grad_in = jnp.concatenate([r2[:, :order], r2[:, order:]], 0)
    return grad_proj, grad_short, grad_out, grad_in


def solution(mesh):
    devices, y_size = mesh.shape["seq"], mesh.shape["ch"]
    tables = make_tables(devices)

    def run(*args):
        return shards(devices, y_size, [jnp.asarray(t) for t in tables], *args)

    return jax.shard_map(
        run,
        mesh=mesh,
        in_specs=(
            P(None, "ch", "seq"),
            P("ch", "seq"),
            P(None, "ch", None),
            P(),
            P(None, "ch"),
            P("ch"),
        ),
        out_specs=(P(None, "ch", "seq"), P(None, "ch", None), P(None, "ch"), P()),
        check_vma=False,
    )
```

```python
import functools
import math

import jax
import jax.numpy as jnp
import ml_dtypes
import numpy as np
from jax import lax
from jax.experimental import pallas as pl
from jax.experimental.pallas import tpu as pltpu
from jax.sharding import PartitionSpec as P

MESH = pl.DeviceIdType.MESH
F32 = jnp.float32
BF16 = jnp.bfloat16
PRECISE = lax.Precision.HIGHEST
LANES = 128
ROWS = 8
TOKENS = ROWS * LANES
Z_SIZE = 8


def bf16_pair(table):
    high = table.astype(ml_dtypes.bfloat16)
    low = (table - high.astype(np.float64)).astype(ml_dtypes.bfloat16)
    return np.stack([high, low])


def make_tables(devices):
    outer = devices * ROWS
    length = outer * LANES
    half = outer // 2
    block = np.arange(devices // 2)
    within = np.arange(ROWS)
    fwd, back, twiddle = [], [], []
    for core in range(2):
        own = ((2 * block[:, None] + core) * ROWS + within[None, :]).reshape(-1)
        other = ((2 * block[:, None] + 1 - core) * ROWS + within[None, :]).reshape(-1)
        a = np.concatenate([own, other])
        k1 = core * half + np.arange(half)
        num = (a[None, :] * (4 * k1[:, None] + 1)) % (4 * outer)
        angle = num * (2.0 * np.pi / (4 * outer))
        matrix = np.concatenate([np.cos(angle), -np.sin(angle)], 0)
        fwd.append(bf16_pair(matrix))
        back.append(bf16_pair(np.ascontiguousarray(matrix.T)))
        num = (np.arange(LANES)[None, :] * (4 * k1[:, None] + 1)) % (4 * length)
        angle = num * (2.0 * np.pi / (4 * length))
        twiddle.append(np.stack([np.cos(angle), -np.sin(angle)]).astype(np.float32))
    b = np.arange(LANES)
    angle = (b[:, None] * b[None, :] % LANES) * (2.0 * np.pi / LANES)
    c, s = np.cos(angle), np.sin(angle)
    inner = np.block([[c, -s], [s, c]])
    return (
        np.stack(fwd),
        np.stack(back),
        np.stack(twiddle),
        bf16_pair(inner),
        bf16_pair(np.ascontiguousarray(inner.T)),
    )


def sin_small(x):
    y = x * x
    p = 1.0 / 6227020800.0
    p = p * y - 1.0 / 39916800.0
    p = p * y + 1.0 / 362880.0
    p = p * y - 1.0 / 5040.0
    p = p * y + 1.0 / 120.0
    p = p * y - 1.0 / 6.0
    return x + x * y * p


def minus_pi_times(x, n):
    return ((x - n * 3.140625) - n * 9.67502593994140625e-4) - n * 1.509957990978376e-7


def parity_sign(n):
    return 1.0 - 2.0 * (n - 2.0 * jnp.floor(n * 0.5))


def sin_cos(x):
    scaled = x * (1.0 / math.pi)
    n = jnp.floor(scaled + 0.5)
    sine = parity_sign(n) * sin_small(minus_pi_times(x, n))
    m = jnp.floor(scaled) + 1.0
    cosine = parity_sign(m) * sin_small(minus_pi_times(x, m - 0.5))
    return sine, cosine


def diagonal(n):
    return lax.broadcasted_iota(jnp.int32, (n, n), 0) == lax.broadcasted_iota(jnp.int32, (n, n), 1)


def column(row):
    return jnp.sum(jnp.where(diagonal(row.shape[1]), row, 0.0), axis=1, keepdims=True)


def as_row(col):
    return jnp.sum(jnp.where(diagonal(col.shape[0]), col, 0.0), axis=0, keepdims=True)


def inverse_spread(rate, length):
    y = rate * (2.0 / length)
    p = 1.0 / 5040.0
    for k in (720.0, 120.0, 24.0, 6.0, 2.0, 1.0):
        p = 1.0 / k - y * p
    return jnp.sqrt(y * p / (1.0 - jnp.exp(-2.0 * rate)))


def split(x):
    high = x.astype(BF16)
    return high, (x - high.astype(F32)).astype(BF16)


def dot_one(a, b):
    return lax.dot_general(a, b, (((1,), (0,)), ((), ())), preferred_element_type=F32)


def dot3(a, b):
    return dot_one(a[0], b[0]) + (dot_one(a[0], b[1]) + dot_one(a[1], b[0]))


def dot_exact(a, b, dims):
    return lax.dot_general(a, b, (dims, ((), ())), precision=PRECISE, preferred_element_type=F32)


def kernel(
    devices, y_size,
    proj_hbm, cot_hbm, sw_hbm, fin_hbm, fout_hbm, rates_hbm, f1_hbm, f1t_hbm, tw_hbm, f2_hbm, f2t_hbm,
    gp_out, short_out, fout_out, fin_out,
    proj, cot, sw, fin, fout, rates, f1, f1t, tw, f2, f2t, feat, hid, hcos, env, ext, kv, halo, sendb, abuf, spec, own, sx, xb, outb, retb,
    gm, halo_gm, r_own, r_core, r_x, r_z, r_y,
    tab_sem, halo_sem, in_send, in_recv, fwd_send, fwd_recv, x_send, x_recv, out_send, out_recv,
    hg_sem, red_send, red_recv,
):
    chips = devices // 2
    channels = cot.shape[0]
    length = devices * TOKENS
    half = devices * ROWS // 2
    blocks = channels // 8
    me = lax.axis_index("seq")
    yi = lax.axis_index("ch")
    q = lax.div(me, 2)
    core = lax.rem(me, 2)
    sib = me + 1 - 2 * core
    nxt = lax.rem(me + 1, devices)
    prv = lax.rem(me + devices - 1, devices)
    x_size = chips // Z_SIZE
    zi = lax.rem(q, Z_SIZE)
    xi = lax.div(q, Z_SIZE)

    def seq_dev(chip):
        return {"seq": 2 * chip + core}

    moves = (
        (fin_hbm, fin), (rates_hbm, rates), (fout_hbm, fout), (sw_hbm, sw), (proj_hbm, proj), (cot_hbm, cot),
        (f1_hbm.at[core], f1), (tw_hbm.at[core], tw), (f2_hbm, f2), (f2t_hbm, f2t), (f1t_hbm.at[core], f1t),
    )
    loads = [pltpu.make_async_copy(src, dst, tab_sem.at[i]) for i, (src, dst) in enumerate(moves)]
    for copy in loads:
        copy.start()
    barrier = pltpu.get_barrier_semaphore()

    def greet(r, carry):
        pl.semaphore_signal(barrier, inc=1, device_id=seq_dev(lax.rem(q + r, chips)), device_id_type=MESH)
        return carry

    lax.fori_loop(1, chips, greet, 0)
    pl.semaphore_signal(barrier, inc=1, device_id={"seq": nxt}, device_id_type=MESH)
    pl.semaphore_signal(barrier, inc=1, device_id={"seq": prv}, device_id_type=MESH)

    def greet_y(r, carry):
        pl.semaphore_signal(barrier, inc=1, device_id={"ch": lax.rem(yi + r, y_size)}, device_id_type=MESH)
        return carry

    lax.fori_loop(1, y_size, greet_y, 0)


    row = lax.broadcasted_iota(jnp.int32, feat.shape, 0)
    position = me * TOKENS + lax.broadcasted_iota(jnp.int32, feat.shape, 1)
    odd = row & 1
    phase = position * (1 + (row >> 1) * 499) - odd * (length // 4) + length // 2
    phase = (phase & (length - 1)) - length // 2
    feat[...] = sin_small((length // 4 - jnp.abs(phase)).astype(F32) * (2.0 * math.pi / length))
    for copy in loads[:4]:
        copy.wait()
    preact = dot_exact(fin[...], feat[...], ((0,), (0,)))
    sine, cosine = sin_cos(preact)
    hid[...] = sine
    hcos[...] = cosine
    relative = (me * TOKENS + lax.broadcasted_iota(jnp.int32, env.shape, 1)).astype(F32) * (1.0 / length)
    rate = column(rates[...])
    env[...] = jnp.exp(-rate * relative) * inverse_spread(rate, length)

    pl.semaphore_wait(barrier, chips - 1 + 2 + y_size - 1)

    halo_copy = pltpu.make_async_remote_copy(
        proj_hbm.at[:, :, TOKENS - LANES :], halo, halo_sem.at[0], halo_sem.at[1],
        device_id={"seq": nxt}, device_id_type=MESH,
    )
    halo_copy.start()

    def scatter_rows(slot, value, cb):
        for j in range(ROWS):
            sendb[slot, pl.ds(cb * 64 + j, 8, stride=8), :] = value[:, j * LANES : (j + 1) * LANES]

    def gather_rows(slot, cb):
        return jnp.concatenate(
            [retb[slot, pl.ds(cb * 64 + j, 8, stride=8), :] for j in range(ROWS)], 1
        )

    my_rows = pl.ds(pl.multiple_of(q * ROWS, ROWS), ROWS)

    def exchange(src, dst, lo, hi, send_sem, recv_sem):
        def one(r, carry):
            chip = lax.rem(q + r, chips)
            rows = pl.ds(pl.multiple_of(chip * ROWS, ROWS), ROWS)
            pltpu.make_async_remote_copy(
                src.at[lo:hi, rows], dst.at[lo:hi, my_rows], send_sem, recv_sem,
                device_id=seq_dev(chip), device_id_type=MESH,
            ).start()
            return carry

        lax.fori_loop(1, chips, one, 0)
        dst[lo:hi, my_rows] = src[lo:hi, my_rows]

    def wait_bytes(src, lo, hi, sem):
        part = src.at[lo:hi, pl.ds(0, (chips - 1) * ROWS)]
        pltpu.make_async_copy(part, part, sem).wait()

    modulated = dot_exact(fout[...], hid[...], ((1,), (0,)))
    filt = env[...] * modulated
    for cb in range(blocks):
        scatter_rows(0, filt[cb * 8 : cb * 8 + 8], cb)
    exchange(sendb, abuf, 0, 1, in_send.at[0], in_recv.at[0])

    for copy in loads[4:6]:
        copy.wait()
    taps = [[column(sw[s, j : j + 1, :]) for j in range(3)] for s in range(3)]
    halo_copy.wait()
    first = (me > 0).astype(F32)
    cot32 = cot[...].astype(F32)
    mixed = []
    for s in range(3):
        ext[s, :, LANES:] = proj[s].astype(F32)
        ext[s, :, :LANES] = halo[s].astype(F32) * first
        full = ext[s]
        total = taps[s][0] * full[:, LANES:]
        for j in range(1, 3):
            total = total + taps[s][j] * pltpu.roll(full, j, 1)[:, LANES:]
        mixed.append(total)
    kv[0] = mixed[1]
    kv[1] = mixed[2]
    gated = mixed[1] * mixed[2]
    grad_conv = cot32 * mixed[0]
    for cb in range(blocks):
        scatter_rows(1, gated[cb * 8 : cb * 8 + 8], cb)
        scatter_rows(2, grad_conv[cb * 8 : cb * 8 + 8], cb)
    exchange(sendb, abuf, 1, 3, in_send.at[1], in_recv.at[1])

    for copy in loads[6:]:
        copy.wait()

    def to_sibling(src, dst, slot):
        return pltpu.make_async_remote_copy(
            src, dst, fwd_send.at[slot], fwd_recv.at[slot], device_id={"seq": sib}, device_id_type=MESH
        )

    def forward(signals):
        a = jnp.concatenate([abuf[s] for s in signals], 1)
        u = dot3((f1[0], f1[1]), split(a))
        for at, s in enumerate(signals):
            ur = u[:half, at * LANES : (at + 1) * LANES]
            ui = u[half:, at * LANES : (at + 1) * LANES]
            v = jnp.concatenate([ur * tw[0] - ui * tw[1], ur * tw[1] + ui * tw[0]], 1)
            spec[s] = dot3(split(v), (f2[0], f2[1]))

    wait_bytes(abuf, 0, 1, in_recv.at[0])
    send_k = to_sibling(abuf.at[0:1, 0:half], abuf.at[0:1, half:], 0)
    send_k.start()
    send_k.wait()
    forward([0])
    wait_bytes(abuf, 1, 3, in_recv.at[1])
    send_gd = to_sibling(abuf.at[1:3, 0:half], abuf.at[1:3, half:], 1)
    send_gd.start()
    send_gd.wait()
    forward([1, 2])

    def parts(s):
        return spec[s, :, :LANES], spec[s, :, LANES:]

    def inverse_rows(re, im):
        z = dot3(split(jnp.concatenate([re, im], 1)), (f2t[0], f2t[1]))
        zr, zi_ = z[:, :LANES], z[:, LANES:]
        return jnp.concatenate([zr * tw[0] + zi_ * tw[1], zi_ * tw[0] - zr * tw[1]], 0)

    kr, ki = parts(0)
    gr, gi = parts(1)
    dr, di = parts(2)

    def finish(signals, rows_of):
        y = dot3((f1t[0], f1t[1]), split(jnp.concatenate(rows_of, 1)))
        for at, s in enumerate(signals):
            own[s] = y[:half, at * LANES : (at + 1) * LANES]
            sx[s] = y[half:, at * LANES : (at + 1) * LANES]

    def swap(lo, hi, slot):
        return pltpu.make_async_remote_copy(
            sx.at[lo:hi], xb.at[lo:hi], x_send.at[slot], x_recv.at[slot],
            device_id={"seq": sib}, device_id_type=MESH,
        )

    finish([0], [inverse_rows(dr * gr + di * gi, di * gr - dr * gi)])
    swap_k = swap(0, 1, 0)
    swap_k.start()
    conv_rows = inverse_rows(gr * kr - gi * ki, gr * ki + gi * kr)
    back_rows = inverse_rows(dr * kr + di * ki, di * kr - dr * ki)
    swap_k.wait()
    outb[0] = (own[0] + xb[0]) * (1.0 / length)
    exchange(outb, retb, 0, 1, out_send.at[0], out_recv.at[0])
    finish([1, 2], [conv_rows, back_rows])
    swap_c = swap(1, 3, 1)
    swap_c.start()
    swap_c.wait()
    for s in (1, 2):
        outb[s] = (own[s] + xb[s]) * (1.0 / length)
    exchange(outb, retb, 1, 3, out_send.at[1], out_recv.at[1])

    wait_bytes(retb, 0, 1, out_recv.at[0])
    weighted = env[...] * jnp.concatenate([gather_rows(0, cb) for cb in range(blocks)], 0)
    out_part = dot_exact(weighted, hid[...], ((1,), (1,)))
    grad_hidden = dot_exact(fout[...], weighted, ((0,), (0,))) * hcos[...]
    in_part = dot_exact(feat[...], grad_hidden, ((1,), (1,)))
    half_in = in_part.shape[0] // 2

    wait_bytes(retb, 1, 3, out_recv.at[1])
    conv_out = jnp.concatenate([gather_rows(1, cb) for cb in range(blocks)], 0)
    grad_gated = jnp.concatenate([gather_rows(2, cb) for cb in range(blocks)], 0)
    gm[0] = cot[...].astype(F32) * conv_out
    gm[1] = grad_gated * kv[1]
    gm[2] = grad_gated * kv[0]
    halo_back = pltpu.make_async_remote_copy(
        gm.at[:, :, 0:LANES], halo_gm, hg_sem.at[0], hg_sem.at[1],
        device_id={"seq": prv}, device_id_type=MESH,
    )
    halo_back.start()

    lane = lax.broadcasted_iota(jnp.int32, (channels, LANES - out_part.shape[1]), 1)
    short = jnp.zeros((channels, LANES - out_part.shape[1]), F32)
    for s in range(3):
        full = ext[s]
        for j in range(3):
            shifted = full[:, LANES:] if j == 0 else pltpu.roll(full, j, 1)[:, LANES:]
            total = jnp.sum(gm[s] * shifted, axis=1, keepdims=True)
            short = jnp.where(lane == s * 3 + j, total, short)
    r_own[0:channels] = jnp.concatenate([out_part, short], 1)
    r_own[channels:] = jnp.concatenate([in_part[:half_in], in_part[half_in:]], 1)

    red_core = pltpu.make_async_remote_copy(
        r_own, r_core, red_send.at[0], red_recv.at[0], device_id={"seq": sib}, device_id_type=MESH
    )
    red_core.start()

    halo_back.wait()
    last = (me < devices - 1).astype(F32)
    for s in range(3):
        full = jnp.concatenate([gm[s], halo_gm[s] * last], 1)
        total = taps[s][0] * full[:, :TOKENS]
        for j in range(1, 3):
            total = total + taps[s][j] * pltpu.roll(full, TOKENS + LANES - j, 1)[:, :TOKENS]
        gp_out[s] = total.astype(BF16)

    red_core.wait()

    def group_sum(buf, index, size, device_of, slot):
        def one(r, carry):
            pltpu.make_async_remote_copy(
                buf.at[index], buf.at[index], red_send.at[slot], red_recv.at[slot],
                device_id=device_of(lax.rem(index + r, size)), device_id_type=MESH,
            ).start()
            return carry

        lax.fori_loop(1, size, one, 0)
        rest = buf.at[pl.ds(0, size - 1)]
        pltpu.make_async_copy(rest, rest, red_recv.at[slot]).wait()
        pltpu.make_async_copy(rest, rest, red_send.at[slot]).wait()
        total = buf[0]
        for i in range(1, size):
            total = total + buf[i]
        return total

    r_x[xi] = r_own[...] + r_core[...]
    r_z[zi] = group_sum(r_x, xi, x_size, lambda i: seq_dev(i * Z_SIZE + zi), 1)
    total = group_sum(r_z, zi, Z_SIZE, lambda i: seq_dev(xi * Z_SIZE + i), 2)
    scale = 1.0 / math.sqrt(length)
    units = hid.shape[0]
    fout_out[...] = total[:channels, :units] * scale
    for s in range(3):
        short_out[s] = jnp.concatenate(
            [as_row(total[:channels, units + 3 * s + j : units + 3 * s + j + 1]) for j in range(3)], 0
        ) * scale
    r_y[yi] = total[channels:]
    in_total = group_sum(r_y, yi, y_size, lambda i: {"ch": i}, 3) * scale
    fin_out[0:half_in] = in_total[:, :units]
    fin_out[half_in:] = in_total[:, units:]

    wait_bytes(sendb, 0, 1, in_send.at[0])
    wait_bytes(sendb, 1, 3, in_send.at[1])
    wait_bytes(outb, 0, 1, out_send.at[0])
    wait_bytes(outb, 1, 3, out_send.at[1])


def shards(devices, y_size, tables, proj, cotangent, short_w, filter_in, filter_out, rates):
    channels = cotangent.shape[0]
    feats, order = filter_in.shape
    length = devices * TOKENS
    chips = devices // 2
    half = devices * ROWS // 2
    outer = devices * ROWS
    r_rows = channels + feats // 2
    vmem = pl.BlockSpec(memory_space=pltpu.VMEM)
    hbm = pl.BlockSpec(memory_space=pltpu.HBM)
    dma = pltpu.SemaphoreType.DMA
    grad_proj, grad_short, grad_out, grad_in = pl.pallas_call(
        functools.partial(kernel, devices, y_size),
        out_shape=(
            jax.ShapeDtypeStruct(proj.shape, BF16),
            jax.ShapeDtypeStruct((3, 3, channels), F32),
            jax.ShapeDtypeStruct((channels, order), F32),
            jax.ShapeDtypeStruct((feats, order), F32),
        ),
        in_specs=[hbm] * 11,
        out_specs=(vmem,) * 4,
        scratch_shapes=[
            pltpu.VMEM(proj.shape, BF16),
            pltpu.VMEM(cotangent.shape, BF16),
            pltpu.VMEM((3, 3, channels), F32),
            pltpu.VMEM((feats, order), F32),
            pltpu.VMEM((channels, order), F32),
            pltpu.VMEM((1, channels), F32),
            pltpu.VMEM((2, outer, outer), BF16),
            pltpu.VMEM((2, outer, outer), BF16),
            pltpu.VMEM((2, half, LANES), F32),
            pltpu.VMEM((2, 2 * LANES, 2 * LANES), BF16),
            pltpu.VMEM((2, 2 * LANES, 2 * LANES), BF16),
            pltpu.VMEM((feats, TOKENS), F32),
            pltpu.VMEM((order, TOKENS), F32),
            pltpu.VMEM((order, TOKENS), F32),
            pltpu.VMEM((channels, TOKENS), F32),
            pltpu.VMEM((3, channels, LANES + TOKENS), F32),
            pltpu.VMEM((2, channels, TOKENS), F32),
            pltpu.VMEM((3, channels, LANES), BF16),
            pltpu.VMEM((3, chips * ROWS, LANES), F32),
            pltpu.VMEM((3, outer, LANES), F32),
            pltpu.VMEM((3, half, 2 * LANES), F32),
            pltpu.VMEM((3, half, LANES), F32),
            pltpu.VMEM((3, half, LANES), F32),
            pltpu.VMEM((3, half, LANES), F32),
            pltpu.VMEM((3, half, LANES), F32),
            pltpu.VMEM((3, half, LANES), F32),
            pltpu.VMEM((3, channels, TOKENS), F32),
            pltpu.VMEM((3, channels, LANES), F32),
            pltpu.VMEM((r_rows, LANES), F32),
            pltpu.VMEM((r_rows, LANES), F32),
            pltpu.VMEM((chips // Z_SIZE, r_rows, LANES), F32),
            pltpu.VMEM((Z_SIZE, r_rows, LANES), F32),
            pltpu.VMEM((y_size, feats // 2, LANES), F32),
            dma((11,)), dma((2,)), dma((2,)), dma((2,)), dma((2,)), dma((2,)), dma((2,)), dma((2,)),
            dma((2,)), dma((2,)), dma((2,)), dma((4,)), dma((4,)),
        ],
        compiler_params=pltpu.CompilerParams(
            collective_id=0, has_side_effects=True, vmem_limit_bytes=56 << 20
        ),
    )(proj, cotangent, short_w.transpose(0, 2, 1), filter_in, filter_out.T, rates.reshape(1, channels), *tables)
    return grad_proj, grad_short.transpose(0, 2, 1), grad_out.T, grad_in


def solution(mesh):
    devices, y_size = mesh.shape["seq"], mesh.shape["ch"]
    tables = make_tables(devices)

    def run(*args):
        return shards(devices, y_size, [jnp.asarray(t) for t in tables], *args)

    return jax.shard_map(
        run,
        mesh=mesh,
        in_specs=(
            P(None, "ch", "seq"),
            P("ch", "seq"),
            P(None, "ch", None),
            P(),
            P(None, "ch"),
            P("ch"),
        ),
        out_specs=(P(None, "ch", "seq"), P(None, "ch", None), P(None, "ch"), P()),
        check_vma=False,
    )
```

```python
import functools
import math

import jax
import jax.numpy as jnp
import ml_dtypes
import numpy as np
from jax import lax
from jax.experimental import pallas as pl
from jax.experimental.pallas import tpu as pltpu
from jax.sharding import PartitionSpec as P

MESH = pl.DeviceIdType.MESH
F32 = jnp.float32
BF16 = jnp.bfloat16
PRECISE = lax.Precision.HIGHEST
LANES = 128
ROWS = 8
TOKENS = ROWS * LANES


def bf16_pair(table):
    high = table.astype(ml_dtypes.bfloat16)
    low = (table - high.astype(np.float64)).astype(ml_dtypes.bfloat16)
    return np.stack([high, low])


def make_tables(devices):
    outer = devices * ROWS
    length = outer * LANES
    half = outer // 2
    a = np.arange(outer)
    fwd, back, twiddle = [], [], []
    for core in range(2):
        k1 = core * half + np.arange(half)
        num = (a[None, :] * (4 * k1[:, None] + 1)) % (4 * outer)
        angle = num * (2.0 * np.pi / (4 * outer))
        matrix = np.concatenate([np.cos(angle), -np.sin(angle)], 0)
        fwd.append(bf16_pair(matrix))
        back.append(bf16_pair(np.ascontiguousarray(matrix.T)))
        num = (np.arange(LANES)[None, :] * (4 * k1[:, None] + 1)) % (4 * length)
        angle = num * (2.0 * np.pi / (4 * length))
        twiddle.append(np.stack([np.cos(angle), -np.sin(angle)]).astype(np.float32))
    b = np.arange(LANES)
    angle = (b[:, None] * b[None, :] % LANES) * (2.0 * np.pi / LANES)
    c, s = np.cos(angle), np.sin(angle)
    inner = np.block([[c, -s], [s, c]])
    return (
        np.stack(fwd),
        np.stack(back),
        np.stack(twiddle),
        bf16_pair(inner),
        bf16_pair(np.ascontiguousarray(inner.T)),
    )


def sin_small(x):
    y = x * x
    p = 1.0 / 6227020800.0
    p = p * y - 1.0 / 39916800.0
    p = p * y + 1.0 / 362880.0
    p = p * y - 1.0 / 5040.0
    p = p * y + 1.0 / 120.0
    p = p * y - 1.0 / 6.0
    return x + x * y * p


def minus_pi_times(x, n):
    return ((x - n * 3.140625) - n * 9.67502593994140625e-4) - n * 1.509957990978376e-7


def parity_sign(n):
    return 1.0 - 2.0 * (n - 2.0 * jnp.floor(n * 0.5))


def sin_cos(x):
    scaled = x * (1.0 / math.pi)
    n = jnp.floor(scaled + 0.5)
    sine = parity_sign(n) * sin_small(minus_pi_times(x, n))
    m = jnp.floor(scaled) + 1.0
    cosine = parity_sign(m) * sin_small(minus_pi_times(x, m - 0.5))
    return sine, cosine


def diagonal(n):
    return lax.broadcasted_iota(jnp.int32, (n, n), 0) == lax.broadcasted_iota(jnp.int32, (n, n), 1)


def column(row):
    return jnp.sum(jnp.where(diagonal(row.shape[1]), row, 0.0), axis=1, keepdims=True)


def as_row(col):
    return jnp.sum(jnp.where(diagonal(col.shape[0]), col, 0.0), axis=0, keepdims=True)


def inverse_spread(rate, length):
    y = rate * (2.0 / length)
    p = 1.0 / 5040.0
    for k in (720.0, 120.0, 24.0, 6.0, 2.0, 1.0):
        p = 1.0 / k - y * p
    return jnp.sqrt(y * p / (1.0 - jnp.exp(-2.0 * rate)))


def split(x):
    high = x.astype(BF16)
    return high, (x - high.astype(F32)).astype(BF16)


def dot_one(a, b):
    return lax.dot_general(a, b, (((1,), (0,)), ((), ())), preferred_element_type=F32)


def dot3(a, b):
    return dot_one(a[0], b[0]) + (dot_one(a[0], b[1]) + dot_one(a[1], b[0]))


def dot_exact(a, b, dims):
    return lax.dot_general(a, b, (dims, ((), ())), precision=PRECISE, preferred_element_type=F32)


def kernel(
    devices, y_size,
    proj_hbm, cot_hbm, sw_hbm, fin_hbm, fout_hbm, rates_hbm, f1_hbm, f1t_hbm, tw_hbm, f2_hbm, f2t_hbm,
    gp_out, short_out, fout_out, fin_out,
    proj, cot, sw, fin, fout, rates, f1, f1t, tw, f2, f2t,
    feat, hid, hcos, env, raw32, raw_send, raw, k_send, kbuf, shifts, kv, spec, ybuf, xb, kg_send, kg_ret,
    res, gp_send, gp_ret, gp32, gp, row_send, row_in, row_mid, row_all, s_own, s_sib, s_all, small, short_rows,
    load_sem, in_send, in_recv, sib_send, sib_recv, x_send, x_recv, ret_send, ret_recv,
    red_send, red_recv, store_sem,
):
    chips = devices // 2
    channels = cot.shape[0]
    length = devices * TOKENS
    outer = devices * ROWS
    half = outer // 2
    local = half + ROWS
    blocks = channels // 8
    units = hid.shape[0]
    me = lax.axis_index("seq")
    yi = lax.axis_index("ch")
    q = lax.div(me, 2)
    core = lax.rem(me, 2)
    sib = me + 1 - 2 * core

    def seq_dev(chip):
        return {"seq": 2 * chip + core}

    barrier = pltpu.get_barrier_semaphore()

    def greet(r, carry):
        pl.semaphore_signal(barrier, inc=1, device_id={"seq": lax.rem(me + r, devices)}, device_id_type=MESH)
        return carry

    lax.fori_loop(1, devices, greet, 0)

    def cross(r):
        y = lax.rem(yi + lax.div(r, 2), y_size)
        return {"ch": y, "seq": 2 * q + lax.rem(core + r, 2)}

    def greet_y(r, carry):
        pl.semaphore_signal(barrier, inc=1, device_id=cross(r), device_id_type=MESH)
        return carry

    lax.fori_loop(2, 2 * y_size, greet_y, 0)

    moves = (
        (fin_hbm, fin), (rates_hbm, rates), (fout_hbm, fout), (proj_hbm, proj), (cot_hbm, cot), (sw_hbm, sw),
        (f1_hbm.at[core], f1), (tw_hbm.at[core], tw), (f2_hbm, f2), (f2t_hbm, f2t), (f1t_hbm.at[core], f1t),
    )
    loads = [pltpu.make_async_copy(src, dst, load_sem.at[i]) for i, (src, dst) in enumerate(moves)]
    for copy in loads:
        copy.start()

    def remote(src, dst, send_sem, recv_sem, device):
        return pltpu.make_async_remote_copy(
            src, dst, send_sem, recv_sem, device_id=device, device_id_type=MESH
        )

    def wait_bytes(part, sem):
        pltpu.make_async_copy(part, part, sem).wait()

    row = lax.broadcasted_iota(jnp.int32, feat.shape, 0)
    position = me * TOKENS + lax.broadcasted_iota(jnp.int32, feat.shape, 1)
    odd = row & 1
    phase = position * (1 + (row >> 1) * 499) - odd * (length // 4) + length // 2
    phase = (phase & (length - 1)) - length // 2
    feat[...] = sin_small((length // 4 - jnp.abs(phase)).astype(F32) * (2.0 * math.pi / length))
    for copy in loads[:5]:
        copy.wait()

    for s in range(4):
        value = cot[...].astype(F32) if s == 3 else proj[s].astype(F32)
        for cb in range(blocks):
            for j in range(ROWS):
                rows = pl.ds(cb * 8 * 4 * ROWS + s * ROWS + j, 8, stride=4 * ROWS)
                raw32[rows, :] = value[cb * 8 : cb * 8 + 8, j * LANES : (j + 1) * LANES]
    raw_send[...] = raw32[...].reshape(raw_send.shape).astype(BF16)

    preact = dot_exact(fin[...], feat[...], ((0,), (0,)))
    sine, cosine = sin_cos(preact)
    hid[...] = sine
    hcos[...] = cosine
    relative = (me * TOKENS + lax.broadcasted_iota(jnp.int32, env.shape, 1)).astype(F32) * (1.0 / length)
    rate = column(rates[...])
    env[...] = jnp.exp(-rate * relative) * inverse_spread(rate, length)
    filt = env[...] * dot_exact(fout[...], hid[...], ((1,), (0,)))
    for cb in range(blocks):
        for j in range(ROWS):
            k_send[pl.ds(cb * 64 + j, 8, stride=8), :] = filt[cb * 8 : cb * 8 + 8, j * LANES : (j + 1) * LANES]

    pl.semaphore_wait(barrier, devices - 1 + 2 * y_size - 2)

    def rows_of(chip):
        return pl.ds(pl.multiple_of(chip * ROWS, ROWS), ROWS)

    def to_chips(start):
        def one(r, carry):
            start(lax.rem(q + r, chips))
            return carry

        lax.fori_loop(1, chips, one, 0)

    to_chips(
        lambda chip: remote(
            raw_send.at[chip], raw.at[q, core], in_send.at[0], in_recv.at[0], seq_dev(chip)
        ).start()
    )
    raw[q, core] = raw_send[q]
    to_chips(
        lambda chip: remote(
            k_send.at[rows_of(chip)], kbuf.at[q, core], in_send.at[1], in_recv.at[1], seq_dev(chip)
        ).start()
    )
    kbuf[q, core] = k_send[rows_of(q)]

    for copy in loads[5:]:
        copy.wait()
    lane9 = lax.broadcasted_iota(jnp.int32, (1, channels), 1)
    taps = [
        [jnp.sum(jnp.where(lane9 == q, sw[s, j : j + 1, :], 0.0), axis=1, keepdims=True) for j in range(3)]
        for s in range(3)
    ]

    wait_bytes(raw_send.at[pl.ds(0, chips - 1)], in_recv.at[0])
    sib_raw = remote(raw.at[:, core], raw.at[:, core], sib_send.at[0], sib_recv.at[0], {"seq": sib})
    sib_raw.start()
    sib_raw.wait()

    lane = lax.broadcasted_iota(jnp.int32, (outer, LANES), 1)
    line = lax.broadcasted_iota(jnp.int32, (outer, LANES), 0)
    mixed = []
    for s in range(3):
        x = raw[:, :, s].astype(F32).reshape(outer, LANES)
        total = taps[s][0] * x
        for j in range(1, 3):
            turned = pltpu.roll(x, j, 1)
            before = jnp.where(line == 0, 0.0, pltpu.roll(turned, 1, 0))
            moved = jnp.where(lane < j, before, turned)
            shifts[s, j - 1] = moved
            total = total + taps[s][j] * moved
        mixed.append(total)
    kv[0] = mixed[1]
    kv[1] = mixed[2]
    gated = mixed[1] * mixed[2]
    grad_conv = raw[:, :, 3].astype(F32).reshape(outer, LANES) * mixed[0]

    def forward(values, slots):
        u = dot3((f1[0], f1[1]), split(jnp.concatenate(values, 1) if len(values) > 1 else values[0]))
        for at, s in enumerate(slots):
            ur = u[:half, at * LANES : (at + 1) * LANES]
            ui = u[half:, at * LANES : (at + 1) * LANES]
            v = jnp.concatenate([ur * tw[0] - ui * tw[1], ur * tw[1] + ui * tw[0]], 1)
            spec[s] = dot3(split(v), (f2[0], f2[1]))

    def parts(s):
        return spec[s, :, :LANES], spec[s, :, LANES:]

    def inverse_rows(re, im):
        z = dot3(split(jnp.concatenate([re, im], 1)), (f2t[0], f2t[1]))
        zr, zi = z[:, :LANES], z[:, LANES:]
        return jnp.concatenate([zr * tw[0] + zi * tw[1], zi * tw[0] - zr * tw[1]], 0)

    def finish(slots, columns):
        y = dot3((f1t[0], f1t[1]), split(jnp.concatenate(columns, 1) if len(columns) > 1 else columns[0]))
        for at, s in enumerate(slots):
            ybuf[s] = y[:, at * LANES : (at + 1) * LANES]

    mine = pl.ds(pl.multiple_of(core * (half - ROWS), ROWS), local)
    theirs = pl.ds(pl.multiple_of((1 - core) * (half - ROWS), ROWS), local)

    def swap(lo, hi, slot):
        return remote(
            ybuf.at[lo:hi, theirs], xb.at[lo:hi], x_send.at[slot], x_recv.at[slot], {"seq": sib}
        )

    forward([gated, grad_conv], [1, 2])
    gr, gi = parts(1)
    dr, di = parts(2)
    finish([0], [inverse_rows(dr * gr + di * gi, di * gr - dr * gi)])
    swap_k = swap(0, 1, 0)
    swap_k.start()

    wait_bytes(k_send.at[pl.ds(0, (chips - 1) * ROWS)], in_recv.at[1])
    sib_k = remote(kbuf.at[:, core], kbuf.at[:, core], sib_send.at[1], sib_recv.at[1], {"seq": sib})
    sib_k.start()

    def send_half(src, dst, slot):
        def one(r, carry):
            d = lax.rem(q + r, chips)
            target = core * chips + d

            @pl.when(target != me)
            def _():
                remote(src.at[d], dst.at[q], ret_send.at[slot], ret_recv.at[slot], {"seq": target}).start()

            @pl.when(target == me)
            def _():
                pltpu.make_async_copy(src.at[d], dst.at[q], ret_recv.at[slot]).start()

            return carry

        lax.fori_loop(0, chips, one, 0)

    swap_k.wait()
    own_rows = pl.ds(pl.multiple_of(core * ROWS, ROWS), half)
    kg = (ybuf[0, pl.ds(pl.multiple_of(core * half, ROWS), half), :] + xb[0, own_rows, :]) * (1.0 / length)
    kg_send[...] = kg.reshape(kg_send.shape)
    send_half(kg_send, kg_ret, 0)

    sib_k.wait()
    forward([kbuf[...].reshape(outer, LANES)], [0])
    kr, ki = parts(0)
    finish(
        [1, 2],
        [
            inverse_rows(gr * kr - gi * ki, gr * ki + gi * kr),
            inverse_rows(dr * kr + di * ki, di * kr - dr * ki),
        ],
    )
    swap_c = swap(1, 3, 1)
    swap_c.start()
    swap_c.wait()

    conv_out = (ybuf[1, mine, :] + xb[1]) * (1.0 / length)
    grad_gated = (ybuf[2, mine, :] + xb[2]) * (1.0 / length)
    lane = lax.broadcasted_iota(jnp.int32, (local, LANES), 1)
    line = lax.broadcasted_iota(jnp.int32, (local, LANES), 0)
    is_mine = (line >= core * ROWS) & (line < core * ROWS + half)
    cot_all = raw[:, :, 3].astype(F32).reshape(outer, LANES)
    gp32[0:outer, :] = cot_all
    cot_mine = gp32[mine, :]
    grad_mixed = [cot_mine * conv_out, grad_gated * kv[1, mine, :], grad_gated * kv[0, mine, :]]
    for s in range(3):
        g = grad_mixed[s]
        total = taps[s][0] * g
        for j in range(1, 3):
            turned = pltpu.roll(g, LANES - j, 1)
            after = jnp.where(line == local - 1, 0.0, pltpu.roll(turned, local - 1, 0))
            total = total + taps[s][j] * jnp.where(lane >= LANES - j, after, turned)
        res[s] = total
        gp_send[:, s] = res[s, own_rows, :].reshape(chips, ROWS, LANES).astype(BF16)
    send_half(gp_send, gp_ret, 1)

    lane1 = lax.broadcasted_iota(jnp.int32, (1, LANES), 1)
    short = jnp.zeros((1, LANES), F32)
    for s in range(3):
        g = jnp.where(is_mine, grad_mixed[s], 0.0)
        gp32[0:outer, :] = raw[:, :, s].astype(F32).reshape(outer, LANES)
        for j in range(3):
            x = gp32[mine, :] if j == 0 else shifts[s, j - 1, mine, :]
            total = jnp.sum(jnp.sum(g * x, axis=0, keepdims=True), axis=1, keepdims=True)
            short = jnp.where(lane1 == s * 3 + j, total, short)
    s_own[...] = short
    sib_short = remote(s_own, s_sib, sib_send.at[2], sib_recv.at[2], {"seq": sib})
    sib_short.start()

    wait_bytes(kg_send, ret_recv.at[0])
    weighted = env[...] * jnp.concatenate(
        [
            jnp.concatenate(
                [
                    kg_ret.at[pl.ds(cb * 8, 8)][:, j, :] for j in range(ROWS)
                ], 1,
            )
            for cb in range(blocks)
        ], 0,
    )
    out_part = dot_exact(weighted, hid[...], ((1,), (1,)))
    grad_hidden = dot_exact(fout[...], weighted, ((0,), (0,))) * hcos[...]
    in_part = dot_exact(feat[...], grad_hidden, ((1,), (1,)))
    row_send[...] = jnp.concatenate([out_part, in_part], 1).reshape(row_send.shape)
    to_chips(
        lambda chip: remote(
            row_send.at[chip], row_in.at[q], red_send.at[0], red_recv.at[0], seq_dev(chip)
        ).start()
    )
    row_in[q] = row_send[q]

    sib_short.wait()
    s_all[q] = s_own[...] + s_sib[...]
    to_chips(
        lambda chip: remote(s_all.at[q], s_all.at[q], red_send.at[3], red_recv.at[3], seq_dev(chip)).start()
    )

    wait_bytes(row_send.at[pl.ds(0, chips - 1)], red_recv.at[0])
    row_mid[yi, core] = jnp.sum(row_in[...], axis=0)

    def to_cross(r, carry):
        remote(
            row_mid.at[yi, core], row_mid.at[yi, core], red_send.at[1], red_recv.at[1], cross(r)
        ).start()
        return carry

    lax.fori_loop(1, 2 * y_size, to_cross, 0)

    wait_bytes(gp_send, ret_recv.at[1])
    gp32[...] = gp_ret[...].astype(F32).reshape(gp32.shape)
    for s in range(3):
        for cb in range(blocks):
            for j in range(ROWS):
                rows = pl.ds(cb * 8 * 3 * ROWS + s * ROWS + j, 8, stride=3 * ROWS)
                gp[s, cb * 8 : cb * 8 + 8, j * LANES : (j + 1) * LANES] = gp32[rows, :].astype(BF16)
    store_gp = pltpu.make_async_copy(gp, gp_out, store_sem.at[0])
    store_gp.start()

    mid_rest = row_in.at[pl.ds(0, 2 * y_size - 1)]
    wait_bytes(mid_rest, red_recv.at[1])
    pair = row_mid[yi, 0] + row_mid[yi, 1]
    every = row_mid[0, 0] + row_mid[0, 1]
    for y in range(1, y_size):
        every = every + (row_mid[y, 0] + row_mid[y, 1])
    scale = 1.0 / math.sqrt(length)
    row_all[q] = jnp.where(lane1 < units, pair, every) * scale
    to_chips(
        lambda chip: remote(row_all.at[q], row_all.at[q], red_send.at[2], red_recv.at[2], seq_dev(chip)).start()
    )
    wait_bytes(row_send.at[pl.ds(0, chips - 1)], red_recv.at[3])
    shorts = s_all[...].reshape(channels, LANES) * scale
    for s in range(3):
        short_rows[s] = jnp.concatenate(
            [as_row(shorts[:, 3 * s + j : 3 * s + j + 1]) for j in range(3)], 0
        )
    wait_bytes(row_send.at[pl.ds(0, chips - 1)], red_recv.at[2])
    rows = row_all[...].reshape(channels, LANES)
    small[0] = rows[:, :units]
    small[1] = rows[:, units:]
    stores = [
        pltpu.make_async_copy(small.at[0], fout_out, store_sem.at[1]),
        pltpu.make_async_copy(small.at[1], fin_out, store_sem.at[2]),
        pltpu.make_async_copy(short_rows, short_out, store_sem.at[3]),
    ]
    for copy in stores:
        copy.start()

    wait_bytes(raw_send.at[pl.ds(0, chips - 1)], in_send.at[0])
    wait_bytes(k_send.at[pl.ds(0, (chips - 1) * ROWS)], in_send.at[1])
    for slot, buf in ((0, kg_send), (1, gp_send)):
        wait_bytes(buf.at[pl.ds(0, chips - 1)], ret_send.at[slot])

        @pl.when(lax.div(me, chips) != core)
        def _():
            wait_bytes(buf.at[0], ret_send.at[slot])

    for slot in (0, 2, 3):
        wait_bytes(row_send.at[pl.ds(0, chips - 1)], red_send.at[slot])
    wait_bytes(mid_rest, red_send.at[1])
    store_gp.wait()
    for copy in stores:
        copy.wait()


def move_outputs(*refs):
    count = (len(refs) - 1) // 2
    copies = [pltpu.make_async_copy(refs[i], refs[count + i], refs[-1].at[i]) for i in range(count)]
    for copy in copies:
        copy.start()
    for copy in copies:
        copy.wait()


def shards(devices, y_size, tables, proj, cotangent, short_w, filter_in, filter_out, rates):
    channels = cotangent.shape[0]
    feats, order = filter_in.shape
    chips = devices // 2
    outer = devices * ROWS
    half = outer // 2
    hbm = pl.BlockSpec(memory_space=pltpu.HBM)
    dma = pltpu.SemaphoreType.DMA

    def f32(*shape):
        return pltpu.VMEM(shape, F32)

    def bf16(*shape):
        return pltpu.VMEM(shape, BF16)

    shapes = (
        jax.ShapeDtypeStruct(proj.shape, BF16),
        jax.ShapeDtypeStruct((3, 3, channels), F32),
        jax.ShapeDtypeStruct((channels, order), F32),
        jax.ShapeDtypeStruct((feats, order), F32),
    )
    results = pl.pallas_call(
        functools.partial(kernel, devices, y_size),
        out_shape=shapes,
        in_specs=[hbm] * 11,
        out_specs=(hbm,) * 4,
        scratch_shapes=[
            bf16(*proj.shape),
            bf16(*cotangent.shape),
            f32(3, 3, channels),
            f32(feats, order),
            f32(channels, order),
            f32(1, channels),
            bf16(2, outer, outer),
            bf16(2, outer, outer),
            f32(2, half, LANES),
            bf16(2, 2 * LANES, 2 * LANES),
            bf16(2, 2 * LANES, 2 * LANES),
            f32(feats, TOKENS),
            f32(order, TOKENS),
            f32(order, TOKENS),
            f32(channels, TOKENS),
            f32(chips * 4 * ROWS, LANES),
            bf16(chips, 4, ROWS, LANES),
            bf16(chips, 2, 4, ROWS, LANES),
            f32(chips * ROWS, LANES),
            f32(chips, 2, ROWS, LANES),
            f32(3, 2, outer, LANES),
            f32(2, outer, LANES),
            f32(3, half, 2 * LANES),
            f32(3, outer, LANES),
            f32(3, half + ROWS, LANES),
            f32(chips, ROWS, LANES),
            f32(chips, ROWS, LANES),
            f32(3, half + ROWS, LANES),
            bf16(chips, 3, ROWS, LANES),
            bf16(chips, 3, ROWS, LANES),
            f32(chips * 3 * ROWS, LANES),
            bf16(*proj.shape),
            f32(chips, 1, LANES),
            f32(chips, 1, LANES),
            f32(y_size, 2, 1, LANES),
            f32(chips, 1, LANES),
            f32(1, LANES),
            f32(1, LANES),
            f32(chips, 1, LANES),
            f32(2, channels, order),
            f32(3, 3, channels),
            dma((11,)), dma((2,)), dma((2,)), dma((3,)), dma((3,)), dma((2,)), dma((2,)), dma((2,)), dma((2,)),
            dma((4,)), dma((4,)), dma((4,)),
        ],
        compiler_params=pltpu.CompilerParams(
            collective_id=0, has_side_effects=True, vmem_limit_bytes=56 << 20
        ),
    )(proj, cotangent, short_w.transpose(0, 2, 1), filter_in, filter_out.T, rates.reshape(1, channels), *tables)
    grad_proj, grad_short, grad_out, grad_in = pl.pallas_call(
        move_outputs,
        out_shape=shapes,
        in_specs=[hbm] * 4,
        out_specs=(hbm,) * 4,
        scratch_shapes=[dma((4,))],
        compiler_params=pltpu.CompilerParams(vmem_limit_bytes=56 << 20),
    )(*results)
    return grad_proj, grad_short.transpose(0, 2, 1), grad_out.T, grad_in


def solution(mesh):
    devices, y_size = mesh.shape["seq"], mesh.shape["ch"]
    tables = make_tables(devices)

    def run(*args):
        return shards(devices, y_size, [jnp.asarray(t) for t in tables], *args)

    return jax.shard_map(
        run,
        mesh=mesh,
        in_specs=(
            P(None, "ch", "seq"),
            P("ch", "seq"),
            P(None, "ch", None),
            P(),
            P(None, "ch"),
            P("ch"),
        ),
        out_specs=(P(None, "ch", "seq"), P(None, "ch", None), P(None, "ch"), P()),
        check_vma=False,
    )
```

```python
import functools
import math

import jax
import jax.numpy as jnp
import ml_dtypes
import numpy as np
from jax import lax
from jax.experimental import pallas as pl
from jax.experimental.pallas import tpu as pltpu
from jax.sharding import PartitionSpec as P

MESH = pl.DeviceIdType.MESH
F32 = jnp.float32
BF16 = jnp.bfloat16
PRECISE = lax.Precision.HIGHEST
LANES = 128
ROWS = 8
TOKENS = ROWS * LANES
Z_SIZE = 8


def bf16_pair(table):
    high = table.astype(ml_dtypes.bfloat16)
    low = (table - high.astype(np.float64)).astype(ml_dtypes.bfloat16)
    return np.stack([high, low])


def make_tables(devices):
    outer = devices * ROWS
    length = outer * LANES
    half = outer // 2
    a = np.arange(outer)
    fwd, back, twiddle = [], [], []
    for core in range(2):
        k1 = core * half + np.arange(half)
        num = (a[None, :] * (4 * k1[:, None] + 1)) % (4 * outer)
        angle = num * (2.0 * np.pi / (4 * outer))
        matrix = np.concatenate([np.cos(angle), -np.sin(angle)], 0)
        fwd.append(bf16_pair(matrix))
        back.append(bf16_pair(np.ascontiguousarray(matrix.T)))
        num = (np.arange(LANES)[None, :] * (4 * k1[:, None] + 1)) % (4 * length)
        angle = num * (2.0 * np.pi / (4 * length))
        twiddle.append(np.stack([np.cos(angle), -np.sin(angle)]).astype(np.float32))
    b = np.arange(LANES)
    angle = (b[:, None] * b[None, :] % LANES) * (2.0 * np.pi / LANES)
    c, s = np.cos(angle), np.sin(angle)
    inner = np.block([[c, -s], [s, c]])
    return (
        np.stack(fwd),
        np.stack(back),
        np.stack(twiddle),
        bf16_pair(inner),
        bf16_pair(np.ascontiguousarray(inner.T)),
    )


def sin_small(x):
    y = x * x
    p = 1.0 / 6227020800.0
    p = p * y - 1.0 / 39916800.0
    p = p * y + 1.0 / 362880.0
    p = p * y - 1.0 / 5040.0
    p = p * y + 1.0 / 120.0
    p = p * y - 1.0 / 6.0
    return x + x * y * p


def minus_pi_times(x, n):
    return ((x - n * 3.140625) - n * 9.67502593994140625e-4) - n * 1.509957990978376e-7


def parity_sign(n):
    return 1.0 - 2.0 * (n - 2.0 * jnp.floor(n * 0.5))


def sin_cos(x):
    scaled = x * (1.0 / math.pi)
    n = jnp.floor(scaled + 0.5)
    sine = parity_sign(n) * sin_small(minus_pi_times(x, n))
    m = jnp.floor(scaled) + 1.0
    cosine = parity_sign(m) * sin_small(minus_pi_times(x, m - 0.5))
    return sine, cosine


def diagonal(n):
    return lax.broadcasted_iota(jnp.int32, (n, n), 0) == lax.broadcasted_iota(jnp.int32, (n, n), 1)


def column(row):
    return jnp.sum(jnp.where(diagonal(row.shape[1]), row, 0.0), axis=1, keepdims=True)


def as_row(col):
    return jnp.sum(jnp.where(diagonal(col.shape[0]), col, 0.0), axis=0, keepdims=True)


def inverse_spread(rate, length):
    y = rate * (2.0 / length)
    p = 1.0 / 5040.0
    for k in (720.0, 120.0, 24.0, 6.0, 2.0, 1.0):
        p = 1.0 / k - y * p
    return jnp.sqrt(y * p / (1.0 - jnp.exp(-2.0 * rate)))


def split(x):
    high = x.astype(BF16)
    return high, (x - high.astype(F32)).astype(BF16)


def dot_one(a, b, da=1, db=0):
    return lax.dot_general(a, b, (((da,), (db,)), ((), ())), preferred_element_type=F32)


def dot3(a, b, da=1, db=0):
    return dot_one(a[0], b[0], da, db) + (dot_one(a[0], b[1], da, db) + dot_one(a[1], b[0], da, db))


def dot_exact(a, b, dims):
    return lax.dot_general(a, b, (dims, ((), ())), precision=PRECISE, preferred_element_type=F32)


def kernel(
    devices, y_size,
    proj_hbm, cot_hbm, sw_hbm, fin_hbm, fout_hbm, rates_hbm, f1_hbm, f1t_hbm, tw_hbm, f2_hbm, f2t_hbm,
    gp, small,
    proj, cot, sw, fin, fout, rates, f1, f1t, tw, f2, f2t,
    feat, hcos, env, raw32, raw_send, raw, k_send, kbuf, shifts, kv, spec, ybuf, xb, kg_send, kg_ret,
    res, gp_send, gp_ret, gp32, hid2, feat2, r_own, r_sib, r_z, r_xy, r_all, s_own, s_sib, s_all,
    load_sem, in_send, in_recv, raw_recv, sib_send, sib_recv, x_send, x_recv, ret_send, ret_recv,
    red_send, red_recv,
):
    chips = devices // 2
    channels = cot.shape[0]
    length = devices * TOKENS
    outer = devices * ROWS
    half = outer // 2
    local = half + ROWS
    blocks = channels // 8
    units = hcos.shape[0]
    me = lax.axis_index("seq")
    yi = lax.axis_index("ch")
    q = lax.div(me, 2)
    core = lax.rem(me, 2)
    sib = me + 1 - 2 * core

    def seq_dev(chip):
        return {"seq": 2 * chip + core}

    barrier = pltpu.get_barrier_semaphore()

    order = (3, 4, 0, 1, 2, 5, 6, 7, 8, 9, 10)
    moves = (
        (fin_hbm, fin), (rates_hbm, rates), (fout_hbm, fout), (proj_hbm, proj), (cot_hbm, cot), (sw_hbm, sw),
        (f1_hbm.at[core], f1), (tw_hbm.at[core], tw), (f2_hbm, f2), (f2t_hbm, f2t), (f1t_hbm.at[core], f1t),
    )
    loads = [pltpu.make_async_copy(src, dst, load_sem.at[i]) for i, (src, dst) in enumerate(moves)]
    for i in order[:2]:
        loads[i].start()

    x_size = chips // Z_SIZE
    xi = lax.div(q, Z_SIZE)
    zi = lax.rem(q, Z_SIZE)

    def cross(r):
        x = lax.rem(xi + lax.div(r, y_size), x_size)
        return {"ch": lax.rem(yi + lax.rem(r, y_size), y_size), "seq": 2 * (x * Z_SIZE + zi) + core}

    def greet(r, carry):
        pl.semaphore_signal(barrier, inc=1, device_id=seq_dev(lax.rem(q + r, chips)), device_id_type=MESH)
        return carry

    def greet_cross(r, carry):
        pl.semaphore_signal(barrier, inc=1, device_id=cross(r), device_id_type=MESH)
        return carry

    lax.fori_loop(1, chips, greet, 0)
    pl.semaphore_signal(barrier, inc=1, device_id={"seq": sib}, device_id_type=MESH)
    lax.fori_loop(1, x_size * y_size, greet_cross, 0)
    for i in order[2:]:
        loads[i].start()

    def remote(src, dst, send_sem, recv_sem, device):
        return pltpu.make_async_remote_copy(
            src, dst, send_sem, recv_sem, device_id=device, device_id_type=MESH
        )

    def wait_bytes(part, sem):
        pltpu.make_async_copy(part, part, sem).wait()

    for copy in loads[3:5]:
        copy.wait()

    for s in range(4):
        value = cot[...].astype(F32) if s == 3 else proj[s].astype(F32)
        for cb in range(blocks):
            for j in range(ROWS):
                rows = pl.ds(cb * 8 * 4 * ROWS + s * ROWS + j, 8, stride=4 * ROWS)
                raw32[rows, :] = value[cb * 8 : cb * 8 + 8, j * LANES : (j + 1) * LANES]
    raw_send[...] = raw32[...].reshape(raw_send.shape).astype(BF16)

    pl.semaphore_wait(barrier, chips + x_size * y_size - 1)

    def rows_of(chip):
        return pl.ds(pl.multiple_of(chip * ROWS, ROWS), ROWS)

    def to_chips(start):
        def one(r, carry):
            start(lax.rem(q + r, chips))
            return carry

        lax.fori_loop(1, chips, one, 0)

    to_chips(
        lambda chip: remote(
            raw_send.at[chip], raw.at[q, core], in_send.at[0], raw_recv.at[q], seq_dev(chip)
        ).start()
    )
    raw[q, core] = raw_send[q]

    row = lax.broadcasted_iota(jnp.int32, feat.shape, 0)
    position = me * TOKENS + lax.broadcasted_iota(jnp.int32, feat.shape, 1)
    odd = row & 1
    phase = position * (1 + (row >> 1) * 499) - odd * (length // 4) + length // 2
    phase = (phase & (length - 1)) - length // 2
    feat[...] = sin_small((length // 4 - jnp.abs(phase)).astype(F32) * (2.0 * math.pi / length))
    for copy in loads[:3]:
        copy.wait()

    preact = dot_exact(fin[...], feat[...], ((0,), (0,)))
    sine, cosine = sin_cos(preact)
    hid2[0], hid2[1] = split(sine)
    feat2[0], feat2[1] = split(feat[...])
    hcos[...] = cosine
    relative = (me * TOKENS + lax.broadcasted_iota(jnp.int32, env.shape, 1)).astype(F32) * (1.0 / length)
    rate = column(rates[...])
    env[...] = jnp.exp(-rate * relative) * inverse_spread(rate, length)
    filt = env[...] * dot3(split(fout[...]), (hid2[0], hid2[1]))
    for cb in range(blocks):
        for j in range(ROWS):
            k_send[pl.ds(cb * 64 + j, 8, stride=8), :] = filt[cb * 8 : cb * 8 + 8, j * LANES : (j + 1) * LANES]

    for copy in loads[5:]:
        copy.wait()
    lane9 = lax.broadcasted_iota(jnp.int32, (1, channels), 1)
    taps = [
        [jnp.sum(jnp.where(lane9 == q, sw[s, j : j + 1, :], 0.0), axis=1, keepdims=True) for j in range(3)]
        for s in range(3)
    ]

    def hand_on(chip):
        remote(raw.at[chip, core], raw.at[chip, core], sib_send.at[0], sib_recv.at[0], {"seq": sib}).start()

    def arrived(r, carry):
        chip = lax.rem(q + chips - r, chips)
        pltpu.make_async_copy(raw.at[chip, core], raw.at[chip, core], raw_recv.at[chip]).wait()
        hand_on(chip)
        return carry

    hand_on(q)
    lax.fori_loop(1, chips // 2, arrived, 0)
    to_chips(
        lambda chip: remote(
            k_send.at[rows_of(chip)], kbuf.at[q, core], in_send.at[1], in_recv.at[1], seq_dev(chip)
        ).start()
    )
    kbuf[q, core] = k_send[rows_of(q)]
    lax.fori_loop(chips // 2, chips, arrived, 0)
    wait_bytes(raw_send, sib_recv.at[0])

    lane = lax.broadcasted_iota(jnp.int32, (outer, LANES), 1)
    line = lax.broadcasted_iota(jnp.int32, (outer, LANES), 0)
    mixed = []
    for s in range(3):
        x = raw[:, :, s].astype(F32).reshape(outer, LANES)
        total = taps[s][0] * x
        for j in range(1, 3):
            turned = pltpu.roll(x, j, 1)
            before = jnp.where(line == 0, 0.0, pltpu.roll(turned, 1, 0))
            moved = jnp.where(lane < j, before, turned)
            shifts[s, j - 1] = moved
            total = total + taps[s][j] * moved
        mixed.append(total)
    kv[0] = mixed[1]
    kv[1] = mixed[2]
    gated = mixed[1] * mixed[2]
    grad_conv = raw[:, :, 3].astype(F32).reshape(outer, LANES) * mixed[0]

    def forward(values, slots):
        u = dot3((f1[0], f1[1]), split(jnp.concatenate(values, 1) if len(values) > 1 else values[0]))
        for at, s in enumerate(slots):
            ur = u[:half, at * LANES : (at + 1) * LANES]
            ui = u[half:, at * LANES : (at + 1) * LANES]
            v = jnp.concatenate([ur * tw[0] - ui * tw[1], ur * tw[1] + ui * tw[0]], 1)
            spec[s] = dot3(split(v), (f2[0], f2[1]))

    def parts(s):
        return spec[s, :, :LANES], spec[s, :, LANES:]

    def inverse_rows(re, im):
        z = dot3(split(jnp.concatenate([re, im], 1)), (f2t[0], f2t[1]))
        zr, zi = z[:, :LANES], z[:, LANES:]
        return jnp.concatenate([zr * tw[0] + zi * tw[1], zi * tw[0] - zr * tw[1]], 0)

    def finish(slots, columns):
        y = dot3((f1t[0], f1t[1]), split(jnp.concatenate(columns, 1) if len(columns) > 1 else columns[0]))
        for at, s in enumerate(slots):
            ybuf[s] = y[:, at * LANES : (at + 1) * LANES]

    mine = pl.ds(pl.multiple_of(core * (half - ROWS), ROWS), local)
    theirs = pl.ds(pl.multiple_of((1 - core) * (half - ROWS), ROWS), local)

    def swap(lo, hi, slot):
        return remote(
            ybuf.at[lo:hi, theirs], xb.at[lo:hi], x_send.at[slot], x_recv.at[slot], {"seq": sib}
        )

    forward([gated, grad_conv], [1, 2])
    gr, gi = parts(1)
    dr, di = parts(2)
    finish([0], [inverse_rows(dr * gr + di * gi, di * gr - dr * gi)])
    swap_k = swap(0, 1, 0)
    swap_k.start()

    wait_bytes(k_send.at[pl.ds(0, (chips - 1) * ROWS)], in_recv.at[1])
    sib_k = remote(kbuf.at[:, core], kbuf.at[:, core], sib_send.at[1], sib_recv.at[1], {"seq": sib})
    sib_k.start()

    def send_half(src, dst, slot):
        def one(r, carry):
            d = lax.rem(q + r, chips)
            target = core * chips + d

            @pl.when(target != me)
            def _():
                remote(src.at[d], dst.at[q], ret_send.at[slot], ret_recv.at[slot], {"seq": target}).start()

            @pl.when(target == me)
            def _():
                pltpu.make_async_copy(src.at[d], dst.at[q], ret_recv.at[slot]).start()

            return carry

        lax.fori_loop(0, chips, one, 0)

    swap_k.wait()
    own_rows = pl.ds(pl.multiple_of(core * ROWS, ROWS), half)
    kg = (ybuf[0, pl.ds(pl.multiple_of(core * half, ROWS), half), :] + xb[0, own_rows, :]) * (1.0 / length)
    kg_send[...] = kg.reshape(kg_send.shape)
    send_half(kg_send, kg_ret, 0)

    sib_k.wait()
    forward([kbuf[...].reshape(outer, LANES)], [0])
    kr, ki = parts(0)
    finish(
        [1, 2],
        [
            inverse_rows(gr * kr - gi * ki, gr * ki + gi * kr),
            inverse_rows(dr * kr + di * ki, di * kr - dr * ki),
        ],
    )
    swap_c = swap(1, 3, 1)
    swap_c.start()
    swap_c.wait()

    conv_out = (ybuf[1, mine, :] + xb[1]) * (1.0 / length)
    grad_gated = (ybuf[2, mine, :] + xb[2]) * (1.0 / length)
    lane = lax.broadcasted_iota(jnp.int32, (local, LANES), 1)
    line = lax.broadcasted_iota(jnp.int32, (local, LANES), 0)
    is_mine = (line >= core * ROWS) & (line < core * ROWS + half)
    cot_all = raw[:, :, 3].astype(F32).reshape(outer, LANES)
    gp32[0:outer, :] = cot_all
    cot_mine = gp32[mine, :]
    grad_mixed = [cot_mine * conv_out, grad_gated * kv[1, mine, :], grad_gated * kv[0, mine, :]]
    for s in range(3):
        g = grad_mixed[s]
        total = taps[s][0] * g
        for j in range(1, 3):
            turned = pltpu.roll(g, LANES - j, 1)
            after = jnp.where(line == local - 1, 0.0, pltpu.roll(turned, local - 1, 0))
            total = total + taps[s][j] * jnp.where(lane >= LANES - j, after, turned)
        res[s] = total
        gp_send[:, s] = res[s, own_rows, :].reshape(chips, ROWS, LANES).astype(BF16)
    send_half(gp_send, gp_ret, 1)

    lane1 = lax.broadcasted_iota(jnp.int32, (1, LANES), 1)
    short = jnp.zeros((1, LANES), F32)
    for s in range(3):
        g = jnp.where(is_mine, grad_mixed[s], 0.0)
        gp32[0:outer, :] = raw[:, :, s].astype(F32).reshape(outer, LANES)
        for j in range(3):
            x = gp32[mine, :] if j == 0 else shifts[s, j - 1, mine, :]
            total = jnp.sum(jnp.sum(g * x, axis=0, keepdims=True), axis=1, keepdims=True)
            short = jnp.where(lane1 == s * 3 + j, total, short)
    s_own[...] = short
    sib_short = remote(s_own, s_sib, sib_send.at[2], sib_recv.at[2], {"seq": sib})
    sib_short.start()

    sib_short.wait()
    s_all[q] = s_own[...] + s_sib[...]
    to_chips(
        lambda chip: remote(s_all.at[q], s_all.at[q], red_send.at[4], red_recv.at[4], seq_dev(chip)).start()
    )

    wait_bytes(kg_send, ret_recv.at[0])
    weighted = env[...] * jnp.concatenate(
        [
            jnp.concatenate(
                [
                    kg_ret.at[pl.ds(cb * 8, 8)][:, j, :] for j in range(ROWS)
                ], 1,
            )
            for cb in range(blocks)
        ], 0,
    )
    pair = split(weighted)
    out_part = dot3(pair, (hid2[0], hid2[1]), 1, 1)
    grad_hidden = dot3(split(fout[...]), pair, 0, 0) * hcos[...]
    in_part = dot3((feat2[0], feat2[1]), split(grad_hidden), 1, 1)
    r_own[...] = jnp.concatenate([out_part, in_part], 1).reshape(r_own.shape)
    red_core = remote(r_own.at[1 - core], r_sib, red_send.at[0], red_recv.at[0], {"seq": sib})
    red_core.start()
    red_core.wait()
    r_z[zi] = r_own[core] + r_sib[...]

    def to_z(r, carry):
        device = seq_dev(xi * Z_SIZE + lax.rem(zi + r, Z_SIZE))
        remote(r_z.at[zi], r_z.at[zi], red_send.at[1], red_recv.at[1], device).start()
        return carry

    lax.fori_loop(1, Z_SIZE, to_z, 0)

    wait_bytes(gp_send, ret_recv.at[1])
    gp32[...] = gp_ret[...].astype(F32).reshape(gp32.shape)
    for s in range(3):
        for cb in range(blocks):
            for j in range(ROWS):
                rows = pl.ds(cb * 8 * 3 * ROWS + s * ROWS + j, 8, stride=3 * ROWS)
                gp[s, cb * 8 : cb * 8 + 8, j * LANES : (j + 1) * LANES] = gp32[rows, :].astype(BF16)

    z_rest = r_z.at[pl.ds(0, Z_SIZE - 1)]
    wait_bytes(z_rest, red_recv.at[1])
    total = r_z[0]
    for i in range(1, Z_SIZE):
        total = total + r_z[i]
    here = xi * y_size + yi
    r_xy[here] = total

    def to_cross(r, carry):
        remote(r_xy.at[here], r_xy.at[here], red_send.at[2], red_recv.at[2], cross(r)).start()
        return carry

    lax.fori_loop(1, x_size * y_size, to_cross, 0)

    scale = 1.0 / math.sqrt(length)
    wait_bytes(s_all.at[pl.ds(0, chips - 1)], red_recv.at[4])
    shorts = s_all[...].reshape(channels, LANES) * scale
    for at in range(9):
        small[channels + at : channels + at + 1, 0:channels] = as_row(shorts[:, at : at + 1])

    def wait_cross(sem):
        wait_bytes(r_xy.at[pl.ds(0, x_size * y_size - 1)], sem)

    wait_cross(red_recv.at[2])
    columns = []
    for y in [yi] + list(range(y_size)):
        column_sum = r_xy[y]
        for x in range(1, x_size):
            column_sum = column_sum + r_xy[x * y_size + y]
        columns.append(column_sum)
    every = columns[1]
    for y in range(1, y_size):
        every = every + columns[1 + y]
    lanes = lax.broadcasted_iota(jnp.int32, every.shape, 1)
    r_all[core] = jnp.where(lanes < units, columns[0], every) * scale
    red_back = remote(r_all.at[core], r_all.at[core], red_send.at[3], red_recv.at[3], {"seq": sib})
    red_back.start()
    red_back.wait()
    small[0:channels, :] = r_all[...].reshape(channels, LANES)

    wait_bytes(raw_send.at[pl.ds(0, chips - 1)], in_send.at[0])
    wait_bytes(k_send.at[pl.ds(0, (chips - 1) * ROWS)], in_send.at[1])
    for slot, buf in ((0, kg_send), (1, gp_send)):
        wait_bytes(buf.at[pl.ds(0, chips - 1)], ret_send.at[slot])

        @pl.when(lax.div(me, chips) != core)
        def _():
            wait_bytes(buf.at[0], ret_send.at[slot])

    wait_bytes(raw_send, sib_send.at[0])
    wait_bytes(z_rest, red_send.at[1])
    wait_cross(red_send.at[2])
    wait_bytes(s_all.at[pl.ds(0, chips - 1)], red_send.at[4])


def shards(devices, y_size, tables, proj, cotangent, short_w, filter_in, filter_out, rates):
    channels = cotangent.shape[0]
    feats, order = filter_in.shape
    chips = devices // 2
    outer = devices * ROWS
    half = outer // 2
    hbm = pl.BlockSpec(memory_space=pltpu.HBM)
    dma = pltpu.SemaphoreType.DMA

    def f32(*shape):
        return pltpu.VMEM(shape, F32)

    def bf16(*shape):
        return pltpu.VMEM(shape, BF16)

    operands = (
        proj, cotangent, short_w.transpose(0, 2, 1), filter_in, filter_out.T, rates.reshape(1, channels), *tables
    )
    grad_proj, small = pl.pallas_call(
        functools.partial(kernel, devices, y_size),
        out_shape=(
            jax.ShapeDtypeStruct(proj.shape, BF16),
            jax.ShapeDtypeStruct((channels + 16, LANES), F32),
        ),
        in_specs=[hbm] * 11,
        out_specs=(pl.BlockSpec(memory_space=pltpu.VMEM),) * 2,
        scratch_shapes=[
            bf16(*proj.shape),
            bf16(*cotangent.shape),
            f32(3, 3, channels),
            f32(feats, order),
            f32(channels, order),
            f32(1, channels),
            bf16(2, outer, outer),
            bf16(2, outer, outer),
            f32(2, half, LANES),
            bf16(2, 2 * LANES, 2 * LANES),
            bf16(2, 2 * LANES, 2 * LANES),
            f32(feats, TOKENS),
            f32(order, TOKENS),
            f32(channels, TOKENS),
            f32(chips * 4 * ROWS, LANES),
            bf16(chips, 4, ROWS, LANES),
            bf16(chips, 2, 4, ROWS, LANES),
            f32(chips * ROWS, LANES),
            f32(chips, 2, ROWS, LANES),
            f32(3, 2, outer, LANES),
            f32(2, outer, LANES),
            f32(3, half, 2 * LANES),
            f32(3, outer, LANES),
            f32(3, half + ROWS, LANES),
            f32(chips, ROWS, LANES),
            f32(chips, ROWS, LANES),
            f32(3, half + ROWS, LANES),
            bf16(chips, 3, ROWS, LANES),
            bf16(chips, 3, ROWS, LANES),
            f32(chips * 3 * ROWS, LANES),
            bf16(2, order, TOKENS),
            bf16(2, feats, TOKENS),
            f32(2, channels // 2, LANES),
            f32(channels // 2, LANES),
            f32(Z_SIZE, channels // 2, LANES),
            f32(chips // Z_SIZE * y_size, channels // 2, LANES),
            f32(2, channels // 2, LANES),
            f32(1, LANES),
            f32(1, LANES),
            f32(chips, 1, LANES),
            dma((11,)), dma((2,)), dma((2,)), dma((chips,)), dma((3,)), dma((3,)), dma((2,)), dma((2,)),
            dma((2,)), dma((2,)), dma((5,)), dma((5,)),
        ],
        compiler_params=pltpu.CompilerParams(
            collective_id=0, has_side_effects=True, vmem_limit_bytes=32 << 20
        ),
    )(*[pltpu.with_memory_space_constraint(x, pltpu.HBM) for x in operands])
    grad_short = small[channels : channels + 9, :channels].reshape(3, 3, channels).transpose(0, 2, 1)
    return grad_proj, grad_short, small[:channels, :order].T, small[:feats, order:]


def solution(mesh):
    devices, y_size = mesh.shape["seq"], mesh.shape["ch"]
    tables = make_tables(devices)

    def run(*args):
        return shards(devices, y_size, [jnp.asarray(t) for t in tables], *args)

    return jax.shard_map(
        run,
        mesh=mesh,
        in_specs=(
            P(None, "ch", "seq"),
            P("ch", "seq"),
            P(None, "ch", None),
            P(),
            P(None, "ch"),
            P("ch"),
        ),
        out_specs=(P(None, "ch", "seq"), P(None, "ch", None), P(None, "ch"), P()),
        check_vma=False,
    )
```

```python
import functools
import math

import jax
import jax.numpy as jnp
import ml_dtypes
import numpy as np
from jax import lax
from jax.experimental import pallas as pl
from jax.experimental.pallas import tpu as pltpu
from jax.sharding import PartitionSpec as P

MESH = pl.DeviceIdType.MESH
F32 = jnp.float32
BF16 = jnp.bfloat16
PRECISE = lax.Precision.HIGHEST
LANES = 128
ROWS = 8
TOKENS = ROWS * LANES
Z_SIZE = 8
EXTRA = 16


def bf16_pair(table):
    high = table.astype(ml_dtypes.bfloat16)
    low = (table - high.astype(np.float64)).astype(ml_dtypes.bfloat16)
    return np.stack([high, low])


def make_tables(devices):
    outer = devices * ROWS
    length = outer * LANES
    half = outer // 2
    a = np.arange(outer)
    fwd, back, twiddle = [], [], []
    for core in range(2):
        k1 = core * half + np.arange(half)
        num = (a[None, :] * (4 * k1[:, None] + 1)) % (4 * outer)
        angle = num * (2.0 * np.pi / (4 * outer))
        matrix = np.concatenate([np.cos(angle), -np.sin(angle)], 0)
        fwd.append(bf16_pair(matrix))
        starts = [(1 - core) * (half - EXTRA), core * (half - EXTRA)]
        rows = np.concatenate([start + np.arange(half + EXTRA) for start in starts])
        back.append(bf16_pair(np.ascontiguousarray(matrix.T[rows])))
        num = (np.arange(LANES)[None, :] * (4 * k1[:, None] + 1)) % (4 * length)
        angle = num * (2.0 * np.pi / (4 * length))
        twiddle.append(np.stack([np.cos(angle), -np.sin(angle)]).astype(np.float32))
    b = np.arange(LANES)
    angle = (b[:, None] * b[None, :] % LANES) * (2.0 * np.pi / LANES)
    c, s = np.cos(angle), np.sin(angle)
    inner = np.block([[c, -s], [s, c]])
    return (
        np.stack(fwd),
        np.stack(back),
        np.stack(twiddle),
        bf16_pair(inner),
        bf16_pair(np.ascontiguousarray(inner.T)),
    )


def sin_small(x):
    y = x * x
    p = 1.0 / 6227020800.0
    p = p * y - 1.0 / 39916800.0
    p = p * y + 1.0 / 362880.0
    p = p * y - 1.0 / 5040.0
    p = p * y + 1.0 / 120.0
    p = p * y - 1.0 / 6.0
    return x + x * y * p


def minus_pi_times(x, n):
    return ((x - n * 3.140625) - n * 9.67502593994140625e-4) - n * 1.509957990978376e-7


def parity_sign(n):
    return 1.0 - 2.0 * (n - 2.0 * jnp.floor(n * 0.5))


def sin_cos(x):
    scaled = x * (1.0 / math.pi)
    n = jnp.floor(scaled + 0.5)
    sine = parity_sign(n) * sin_small(minus_pi_times(x, n))
    m = jnp.floor(scaled) + 1.0
    cosine = parity_sign(m) * sin_small(minus_pi_times(x, m - 0.5))
    return sine, cosine


def diagonal(n):
    return lax.broadcasted_iota(jnp.int32, (n, n), 0) == lax.broadcasted_iota(jnp.int32, (n, n), 1)


def column(row):
    return jnp.sum(jnp.where(diagonal(row.shape[1]), row, 0.0), axis=1, keepdims=True)


def as_row(col):
    return jnp.sum(jnp.where(diagonal(col.shape[0]), col, 0.0), axis=0, keepdims=True)


def inverse_spread(rate, length):
    y = rate * (2.0 / length)
    p = 1.0 / 5040.0
    for k in (720.0, 120.0, 24.0, 6.0, 2.0, 1.0):
        p = 1.0 / k - y * p
    return jnp.sqrt(y * p / (1.0 - jnp.exp(-2.0 * rate)))


def split(x):
    high = x.astype(BF16)
    return high, (x - high.astype(F32)).astype(BF16)


def dot_one(a, b, da=1, db=0):
    return lax.dot_general(a, b, (((da,), (db,)), ((), ())), preferred_element_type=F32)


def dot3(a, b, da=1, db=0):
    return dot_one(
        jnp.concatenate([a[0], a[0], a[1]], da), jnp.concatenate([b[0], b[1], b[0]], db), da, db
    )


def dot_exact(a, b, dims):
    return lax.dot_general(a, b, (dims, ((), ())), precision=PRECISE, preferred_element_type=F32)


def kernel(
    devices, y_size,
    proj_hbm, cot_hbm, sw_hbm, fin_hbm, fout_hbm, rates_hbm, f1_hbm, f1t_hbm, tw_hbm, f2_hbm, f2t_hbm,
    gp, short_rows, fout_out, fin_out,
    proj, cot, sw, fin, fout, rates, f1, f1t, tw, f2, f2t,
    feat, hcos, env, raw32, raw_send, raw, k_send, kbuf, shifts, kv, spec, ybuf, yown, xb, kg_send, kg_ret,
    res, gp_send, gp_ret, gp32, hid2, feat2, r_own, r_sib, r_z, r_x, r_xy, s_own, s_sib, s_all,
    load_sem, in_send, in_recv, raw_recv, sib_send, sib_recv, x_send, x_recv, ret_send, ret_recv,
    red_send, red_recv,
):
    chips = devices // 2
    channels = cot.shape[0]
    length = devices * TOKENS
    outer = devices * ROWS
    half = outer // 2
    local = half + EXTRA
    blocks = channels // 8
    units = hcos.shape[0]
    me = lax.axis_index("seq")
    yi = lax.axis_index("ch")
    q = lax.div(me, 2)
    core = lax.rem(me, 2)
    sib = me + 1 - 2 * core

    def seq_dev(chip):
        return {"seq": 2 * chip + core}

    barrier = pltpu.get_barrier_semaphore()

    order = (3, 4, 0, 1, 2, 5, 6, 7, 8, 9, 10)
    moves = (
        (fin_hbm, fin), (rates_hbm, rates), (fout_hbm, fout), (proj_hbm, proj), (cot_hbm, cot), (sw_hbm, sw),
        (f1_hbm.at[core], f1), (tw_hbm.at[core], tw), (f2_hbm, f2), (f2t_hbm, f2t), (f1t_hbm.at[core], f1t),
    )
    loads = [pltpu.make_async_copy(src, dst, load_sem.at[i]) for i, (src, dst) in enumerate(moves)]
    x_size = chips // Z_SIZE
    xi = lax.div(q, Z_SIZE)
    zi = lax.rem(q, Z_SIZE)

    def cross(r):
        x = lax.rem(xi + lax.rem(lax.div(r, y_size), x_size), x_size)
        other = lax.rem(core + lax.div(r, x_size * y_size), 2)
        return {"ch": lax.rem(yi + lax.rem(r, y_size), y_size), "seq": 2 * (x * Z_SIZE + zi) + other}

    def greet(r, carry):
        pl.semaphore_signal(barrier, inc=1, device_id=seq_dev(lax.rem(q + r, chips)), device_id_type=MESH)
        return carry

    def greet_cross(r, carry):
        pl.semaphore_signal(barrier, inc=1, device_id=cross(r), device_id_type=MESH)
        return carry

    lax.fori_loop(1, chips, greet, 0)
    lax.fori_loop(1, 2 * x_size * y_size, greet_cross, 0)
    for i in order:
        loads[i].start()

    def remote(src, dst, send_sem, recv_sem, device):
        return pltpu.make_async_remote_copy(
            src, dst, send_sem, recv_sem, device_id=device, device_id_type=MESH
        )

    def wait_bytes(part, sem):
        pltpu.make_async_copy(part, part, sem).wait()

    for copy in loads[3:5]:
        copy.wait()

    for s in range(4):
        value = cot[...].astype(F32) if s == 3 else proj[s].astype(F32)
        for cb in range(blocks):
            for j in range(ROWS):
                rows = pl.ds(cb * 8 * 4 * ROWS + s * ROWS + j, 8, stride=4 * ROWS)
                raw32[rows, :] = value[cb * 8 : cb * 8 + 8, j * LANES : (j + 1) * LANES]
    raw_send[...] = raw32[...].reshape(raw_send.shape).astype(BF16)

    pl.semaphore_wait(barrier, chips - 1 + 2 * x_size * y_size - 1)

    def rows_of(chip):
        return pl.ds(pl.multiple_of(chip * ROWS, ROWS), ROWS)

    def to_chips(start):
        def one(r, carry):
            start(lax.rem(q + r, chips))
            return carry

        lax.fori_loop(1, chips, one, 0)

    to_chips(
        lambda chip: remote(
            raw_send.at[chip], raw.at[q, core], in_send.at[0], raw_recv.at[q], seq_dev(chip)
        ).start()
    )
    raw[q, core] = raw_send[q]

    row = lax.broadcasted_iota(jnp.int32, feat.shape, 0)
    position = me * TOKENS + lax.broadcasted_iota(jnp.int32, feat.shape, 1)
    odd = row & 1
    phase = position * (1 + (row >> 1) * 499) - odd * (length // 4) + length // 2
    phase = (phase & (length - 1)) - length // 2
    feat[...] = sin_small((length // 4 - jnp.abs(phase)).astype(F32) * (2.0 * math.pi / length))
    for copy in loads[:3]:
        copy.wait()

    preact = dot_exact(fin[...], feat[...], ((0,), (0,)))
    sine, cosine = sin_cos(preact)
    hid2[0], hid2[1] = split(sine)
    feat2[0], feat2[1] = split(feat[...])
    hcos[...] = cosine
    relative = (me * TOKENS + lax.broadcasted_iota(jnp.int32, env.shape, 1)).astype(F32) * (1.0 / length)
    rate = column(rates[...])
    env[...] = jnp.exp(-rate * relative) * inverse_spread(rate, length)
    filt = env[...] * dot3(split(fout[...]), (hid2[0], hid2[1]))
    for cb in range(blocks):
        for j in range(ROWS):
            k_send[pl.ds(cb * 64 + j, 8, stride=8), :] = filt[cb * 8 : cb * 8 + 8, j * LANES : (j + 1) * LANES]

    for copy in loads[5:]:
        copy.wait()
    lane9 = lax.broadcasted_iota(jnp.int32, (1, channels), 1)
    taps = [
        [jnp.sum(jnp.where(lane9 == q, sw[s, j : j + 1, :], 0.0), axis=1, keepdims=True) for j in range(3)]
        for s in range(3)
    ]

    def hand_on(chip):
        remote(raw.at[chip, core], raw.at[chip, core], sib_send.at[0], sib_recv.at[0], {"seq": sib}).start()

    def arrived(r, carry):
        chip = lax.rem(q + chips - r, chips)
        pltpu.make_async_copy(raw.at[chip, core], raw.at[chip, core], raw_recv.at[chip]).wait()
        hand_on(chip)
        return carry

    hand_on(q)
    lax.fori_loop(1, chips // 2, arrived, 0)
    to_chips(
        lambda chip: remote(
            k_send.at[rows_of(chip)], kbuf.at[q, core], in_send.at[1], in_recv.at[1], seq_dev(chip)
        ).start()
    )
    kbuf[q, core] = k_send[rows_of(q)]
    lax.fori_loop(chips // 2, chips, arrived, 0)
    wait_bytes(raw_send, sib_recv.at[0])

    lane = lax.broadcasted_iota(jnp.int32, (outer, LANES), 1)
    line = lax.broadcasted_iota(jnp.int32, (outer, LANES), 0)
    mixed = []
    for s in range(3):
        x = raw[:, :, s].astype(F32).reshape(outer, LANES)
        total = taps[s][0] * x
        for j in range(1, 3):
            turned = pltpu.roll(x, j, 1)
            before = jnp.where(line == 0, 0.0, pltpu.roll(turned, 1, 0))
            moved = jnp.where(lane < j, before, turned)
            shifts[s, j - 1] = moved
            total = total + taps[s][j] * moved
        mixed.append(total)
    kv[0] = mixed[1]
    kv[1] = mixed[2]
    gated = mixed[1] * mixed[2]
    grad_conv = raw[:, :, 3].astype(F32).reshape(outer, LANES) * mixed[0]

    def forward(values, slots):
        u = dot3((f1[0], f1[1]), split(jnp.concatenate(values, 1) if len(values) > 1 else values[0]))
        for at, s in enumerate(slots):
            ur = u[:half, at * LANES : (at + 1) * LANES]
            ui = u[half:, at * LANES : (at + 1) * LANES]
            v = jnp.concatenate([ur * tw[0] - ui * tw[1], ur * tw[1] + ui * tw[0]], 1)
            spec[s] = dot3(split(v), (f2[0], f2[1]))

    def parts(s):
        return spec[s, :, :LANES], spec[s, :, LANES:]

    def inverse_rows(re, im):
        z = dot3(split(jnp.concatenate([re, im], 1)), (f2t[0], f2t[1]))
        zr, zi = z[:, :LANES], z[:, LANES:]
        return jnp.concatenate([zr * tw[0] + zi * tw[1], zi * tw[0] - zr * tw[1]], 0)

    mine = pl.ds(pl.multiple_of(core * (half - EXTRA), ROWS), local)

    def finish(slots, columns, exchange):
        right = split(jnp.concatenate(columns, 1) if len(columns) > 1 else columns[0])
        for own in (False, True):
            rows = slice(local, 2 * local) if own else slice(0, local)
            y = dot3((f1t[0, rows, :], f1t[1, rows, :]), right)
            for at, s in enumerate(slots):
                (yown if own else ybuf)[s] = y[:, at * LANES : (at + 1) * LANES]
            if not own:
                exchange.start()

    def swap(lo, hi, slot):
        return remote(
            ybuf.at[lo:hi], xb.at[lo:hi], x_send.at[slot], x_recv.at[slot], {"seq": sib}
        )

    forward([gated, grad_conv], [1, 2])
    gr, gi = parts(1)
    dr, di = parts(2)
    swap_k = swap(0, 1, 0)
    finish([0], [inverse_rows(dr * gr + di * gi, di * gr - dr * gi)], swap_k)

    is_local = lax.div(me, chips) == core

    def send_half(src, dst, slot, first, end):
        at = lax.rem(me, chips)

        def one(r, carry):
            d = lax.rem(at + r, chips)
            device = {"seq": core * chips + d}
            remote(src.at[d], dst.at[q], ret_send.at[slot], ret_recv.at[slot], device).start()
            return carry

        lax.fori_loop(max(first, 1), end, one, 0)
        if first == 0:

            @pl.when(is_local)
            def _():
                pltpu.make_async_copy(src.at[at], dst.at[q], ret_recv.at[slot]).start()

            @pl.when(jnp.logical_not(is_local))
            def _():
                one(0, 0)

    swap_k.wait()
    own_rows = pl.ds(pl.multiple_of(core * EXTRA, ROWS), half)
    kg = (yown[0, own_rows, :] + xb[0, own_rows, :]) * (1.0 / length)
    kg_send[...] = kg.reshape(kg_send.shape)
    send_half(kg_send, kg_ret, 0, 0, chips)

    wait_bytes(k_send.at[pl.ds(0, (chips - 1) * ROWS)], in_recv.at[1])
    sib_k = remote(kbuf.at[:, core], kbuf.at[:, core], sib_send.at[1], sib_recv.at[1], {"seq": sib})
    sib_k.start()

    sib_k.wait()
    forward([kbuf[...].reshape(outer, LANES)], [0])
    kr, ki = parts(0)
    swap_c = swap(1, 3, 1)
    finish(
        [1, 2],
        [
            inverse_rows(gr * kr - gi * ki, gr * ki + gi * kr),
            inverse_rows(dr * kr + di * ki, di * kr - dr * ki),
        ],
        swap_c,
    )
    swap_c.wait()

    conv_out = (yown[1] + xb[1]) * (1.0 / length)
    grad_gated = (yown[2] + xb[2]) * (1.0 / length)
    lane = lax.broadcasted_iota(jnp.int32, (local, LANES), 1)
    line = lax.broadcasted_iota(jnp.int32, (local, LANES), 0)
    is_mine = (line >= core * EXTRA) & (line < core * EXTRA + half)
    cot_all = raw[:, :, 3].astype(F32).reshape(outer, LANES)
    gp32[0:outer, :] = cot_all
    cot_mine = gp32[mine, :]
    grad_mixed = [cot_mine * conv_out, grad_gated * kv[1, mine, :], grad_gated * kv[0, mine, :]]
    for s in range(3):
        g = grad_mixed[s]
        total = taps[s][0] * g
        for j in range(1, 3):
            turned = pltpu.roll(g, LANES - j, 1)
            after = jnp.where(line == local - 1, 0.0, pltpu.roll(turned, local - 1, 0))
            total = total + taps[s][j] * jnp.where(lane >= LANES - j, after, turned)
        res[s] = total
        gp_send[:, s] = res[s, own_rows, :].reshape(chips, ROWS, LANES).astype(BF16)
    send_half(gp_send, gp_ret, 1, 0, chips // 2)

    wait_bytes(kg_send, ret_recv.at[0])
    weighted = env[...] * jnp.concatenate(
        [
            jnp.concatenate(
                [
                    kg_ret.at[pl.ds(cb * 8, 8)][:, j, :] for j in range(ROWS)
                ], 1,
            )
            for cb in range(blocks)
        ], 0,
    )
    pair = split(weighted)
    out_part = dot3(pair, (hid2[0], hid2[1]), 1, 1)
    grad_hidden = dot3(split(fout[...]), pair, 0, 0) * hcos[...]
    in_part = dot3((feat2[0], feat2[1]), split(grad_hidden), 1, 1)
    for half_at in range(2):
        for at, part in enumerate((out_part, in_part)):
            first = half_at * (channels // 2)
            middle, end = first + channels // 4, first + channels // 2
            r_own[half_at, at] = jnp.concatenate([part[first:middle], part[middle:end]], 1)
    red_core = remote(r_own.at[1 - core], r_sib, red_send.at[0], red_recv.at[0], {"seq": sib})
    red_core.start()
    lane1 = lax.broadcasted_iota(jnp.int32, (1, LANES), 1)
    short = jnp.zeros((1, LANES), F32)
    for s in range(3):
        g = jnp.where(is_mine, grad_mixed[s], 0.0)
        gp32[0:outer, :] = raw[:, :, s].astype(F32).reshape(outer, LANES)
        for j in range(3):
            x = gp32[mine, :] if j == 0 else shifts[s, j - 1, mine, :]
            total = jnp.sum(jnp.sum(g * x, axis=0, keepdims=True), axis=1, keepdims=True)
            short = jnp.where(lane1 == s * 3 + j, total, short)
    s_own[...] = short
    sib_short = remote(s_own, s_sib, sib_send.at[2], sib_recv.at[2], {"seq": sib})
    sib_short.start()

    red_core.wait()
    r_z[zi] = r_own[core] + r_sib[...]

    def to_z(r, carry):
        device = seq_dev(xi * Z_SIZE + lax.rem(zi + r, Z_SIZE))
        remote(r_z.at[zi], r_z.at[zi], red_send.at[1], red_recv.at[1], device).start()
        return carry

    lax.fori_loop(1, Z_SIZE, to_z, 0)


    sib_short.wait()
    s_all[q] = s_own[...] + s_sib[...]
    to_chips(
        lambda chip: remote(s_all.at[q], s_all.at[q], red_send.at[4], red_recv.at[4], seq_dev(chip)).start()
    )
    send_half(gp_send, gp_ret, 1, chips // 2, chips)

    z_rest = r_z.at[pl.ds(0, Z_SIZE - 1)]
    wait_bytes(z_rest, red_recv.at[1])
    total = r_z[0]
    for i in range(1, Z_SIZE):
        total = total + r_z[i]
    here = xi * y_size + yi
    r_x[core, xi] = total[0]
    r_xy[core, here] = total[1]

    def to_cross(r, carry):
        remote(r_xy.at[core, here], r_xy.at[core, here], red_send.at[2], red_recv.at[2], cross(r)).start()
        return carry

    def to_x(r, carry):
        remote(r_x.at[core, xi], r_x.at[core, xi], red_send.at[3], red_recv.at[3], cross(r * y_size)).start()
        return carry

    lax.fori_loop(1, 2 * x_size * y_size, to_cross, 0)
    lax.fori_loop(1, 2 * x_size, to_x, 0)

    wait_bytes(gp_send, ret_recv.at[1])
    gp32[...] = gp_ret[...].astype(F32).reshape(gp32.shape)
    for s in range(3):
        for cb in range(blocks):
            for j in range(ROWS):
                rows = pl.ds(cb * 8 * 3 * ROWS + s * ROWS + j, 8, stride=3 * ROWS)
                gp[s, cb * 8 : cb * 8 + 8, j * LANES : (j + 1) * LANES] = gp32[rows, :].astype(BF16)

    scale = 1.0 / math.sqrt(length)
    wait_bytes(s_all.at[pl.ds(0, chips - 1)], red_recv.at[4])
    shorts = s_all[...].reshape(channels, LANES) * scale
    for at in range(9):
        short_rows[at // 3, at % 3 : at % 3 + 1, :] = as_row(shorts[:, at : at + 1])

    group = 2 * x_size * y_size
    wait_bytes(gp32.at[pl.ds(0, (2 * x_size - 1) * (channels // 4))], red_recv.at[3])
    wait_bytes(gp32.at[pl.ds(0, (group - 1) * (channels // 4))], red_recv.at[2])
    for half_at in range(2):
        out_total = r_x[half_at, 0]
        for x in range(1, x_size):
            out_total = out_total + r_x[half_at, x]
        in_total = r_xy[half_at, 0]
        for at in range(1, x_size * y_size):
            in_total = in_total + r_xy[half_at, at]
        first = half_at * (channels // 2)
        middle, end = first + channels // 4, first + channels // 2
        for out, part in ((fout_out, out_total * scale), (fin_out, in_total * scale)):
            out[first:middle, :] = part[:, :units]
            out[middle:end, :] = part[:, units:]

    wait_bytes(raw_send.at[pl.ds(0, chips - 1)], in_send.at[0])
    wait_bytes(k_send.at[pl.ds(0, (chips - 1) * ROWS)], in_send.at[1])
    for slot, buf in ((0, kg_send), (1, gp_send)):
        wait_bytes(buf.at[pl.ds(0, chips - 1)], ret_send.at[slot])

        @pl.when(jnp.logical_not(is_local))
        def _():
            wait_bytes(buf.at[0], ret_send.at[slot])

    wait_bytes(raw_send, sib_send.at[0])
    wait_bytes(z_rest, red_send.at[1])
    wait_bytes(gp32.at[pl.ds(0, (2 * x_size - 1) * (channels // 4))], red_send.at[3])
    wait_bytes(gp32.at[pl.ds(0, (group - 1) * (channels // 4))], red_send.at[2])
    wait_bytes(s_all.at[pl.ds(0, chips - 1)], red_send.at[4])


def move_outputs(*refs):
    count = (len(refs) - 1) // 2
    copies = [pltpu.make_async_copy(refs[i], refs[count + i], refs[-1].at[i]) for i in range(count)]
    for copy in copies:
        copy.start()
    for copy in copies:
        copy.wait()


def shards(devices, y_size, tables, proj, cotangent, short_w, filter_in, filter_out, rates):
    channels = cotangent.shape[0]
    feats, order = filter_in.shape
    chips = devices // 2
    outer = devices * ROWS
    half = outer // 2
    hbm = pl.BlockSpec(memory_space=pltpu.HBM)
    dma = pltpu.SemaphoreType.DMA

    def f32(*shape):
        return pltpu.VMEM(shape, F32)

    def bf16(*shape):
        return pltpu.VMEM(shape, BF16)

    operands = (
        proj, cotangent, short_w.transpose(0, 2, 1), filter_in, filter_out.T, rates.reshape(1, channels), *tables
    )
    shapes = (
        jax.ShapeDtypeStruct(proj.shape, BF16),
        jax.ShapeDtypeStruct((3, 3, channels), F32),
        jax.ShapeDtypeStruct((channels, order), F32),
        jax.ShapeDtypeStruct((feats, order), F32),
    )
    results = pl.pallas_call(
        functools.partial(kernel, devices, y_size),
        out_shape=shapes,
        in_specs=[hbm] * 11,
        out_specs=(pl.BlockSpec(memory_space=pltpu.VMEM),) * 4,
        scratch_shapes=[
            bf16(*proj.shape),
            bf16(*cotangent.shape),
            f32(3, 3, channels),
            f32(feats, order),
            f32(channels, order),
            f32(1, channels),
            bf16(2, outer, outer),
            bf16(2, outer + 2 * EXTRA, outer),
            f32(2, half, LANES),
            bf16(2, 2 * LANES, 2 * LANES),
            bf16(2, 2 * LANES, 2 * LANES),
            f32(feats, TOKENS),
            f32(order, TOKENS),
            f32(channels, TOKENS),
            f32(chips * 4 * ROWS, LANES),
            bf16(chips, 4, ROWS, LANES),
            bf16(chips, 2, 4, ROWS, LANES),
            f32(chips * ROWS, LANES),
            f32(chips, 2, ROWS, LANES),
            f32(3, 2, outer, LANES),
            f32(2, outer, LANES),
            f32(3, half, 2 * LANES),
            f32(3, half + EXTRA, LANES),
            f32(3, half + EXTRA, LANES),
            f32(3, half + EXTRA, LANES),
            f32(chips, ROWS, LANES),
            f32(chips, ROWS, LANES),
            f32(3, half + EXTRA, LANES),
            bf16(chips, 3, ROWS, LANES),
            bf16(chips, 3, ROWS, LANES),
            f32(chips * 3 * ROWS, LANES),
            bf16(2, order, TOKENS),
            bf16(2, feats, TOKENS),
            f32(2, 2, channels // 4, LANES),
            f32(2, channels // 4, LANES),
            f32(Z_SIZE, 2, channels // 4, LANES),
            f32(2, chips // Z_SIZE, channels // 4, LANES),
            f32(2, chips // Z_SIZE * y_size, channels // 4, LANES),
            f32(1, LANES),
            f32(1, LANES),
            f32(chips, 1, LANES),
            dma((11,)), dma((2,)), dma((2,)), dma((chips,)), dma((3,)), dma((3,)), dma((2,)), dma((2,)),
            dma((2,)), dma((2,)), dma((5,)), dma((5,)),
        ],
        compiler_params=pltpu.CompilerParams(
            collective_id=0, has_side_effects=True, vmem_limit_bytes=32 << 20
        ),
    )(*[pltpu.with_memory_space_constraint(x, pltpu.HBM) for x in operands])
    grad_proj, grad_short, grad_out, grad_in = pl.pallas_call(
        move_outputs,
        out_shape=shapes,
        in_specs=[pl.BlockSpec(memory_space=pl.ANY)] * 4,
        out_specs=(hbm,) * 4,
        scratch_shapes=[dma((4,))],
        compiler_params=pltpu.CompilerParams(vmem_limit_bytes=1 << 20),
    )(*results)
    return grad_proj, grad_short.transpose(0, 2, 1), grad_out.T, grad_in


def solution(mesh):
    devices, y_size = mesh.shape["seq"], mesh.shape["ch"]
    tables = make_tables(devices)

    def run(*args):
        return shards(devices, y_size, [jnp.asarray(t) for t in tables], *args)

    return jax.shard_map(
        run,
        mesh=mesh,
        in_specs=(
            P(None, "ch", "seq"),
            P("ch", "seq"),
            P(None, "ch", None),
            P(),
            P(None, "ch"),
            P("ch"),
        ),
        out_specs=(P(None, "ch", "seq"), P(None, "ch", None), P(None, "ch"), P()),
        check_vma=False,
    )
```

```python
import functools
import math

import jax
import jax.numpy as jnp
import ml_dtypes
import numpy as np
from jax import lax
from jax.experimental import pallas as pl
from jax.experimental.pallas import tpu as pltpu
from jax.sharding import PartitionSpec as P

MESH = pl.DeviceIdType.MESH
F32 = jnp.float32
BF16 = jnp.bfloat16
PRECISE = lax.Precision.HIGHEST
LANES = 128
ROWS = 8
TOKENS = ROWS * LANES
Z_SIZE = 8
EXTRA = 16


def bf16_pair(table):
    high = table.astype(ml_dtypes.bfloat16)
    low = (table - high.astype(np.float64)).astype(ml_dtypes.bfloat16)
    return np.stack([high, low])


def make_tables(devices):
    outer = devices * ROWS
    length = outer * LANES
    half = outer // 2
    a = np.arange(outer)
    fwd, back, twiddle = [], [], []
    for core in range(2):
        k1 = core * half + np.arange(half)
        num = (a[None, :] * (4 * k1[:, None] + 1)) % (4 * outer)
        angle = num * (2.0 * np.pi / (4 * outer))
        matrix = np.concatenate([np.cos(angle), -np.sin(angle)], 0)
        fwd.append(bf16_pair(matrix))
        starts = [(1 - core) * (half - EXTRA), core * (half - EXTRA)]
        rows = np.concatenate([start + np.arange(half + EXTRA) for start in starts])
        back.append(bf16_pair(np.ascontiguousarray(matrix.T[rows])))
        num = (np.arange(LANES)[None, :] * (4 * k1[:, None] + 1)) % (4 * length)
        angle = num * (2.0 * np.pi / (4 * length))
        twiddle.append(np.stack([np.cos(angle), -np.sin(angle)]).astype(np.float32))
    b = np.arange(LANES)
    angle = (b[:, None] * b[None, :] % LANES) * (2.0 * np.pi / LANES)
    c, s = np.cos(angle), np.sin(angle)
    inner = np.block([[c, -s], [s, c]])
    return (
        np.stack(fwd),
        np.stack(back),
        np.stack(twiddle),
        bf16_pair(inner),
        bf16_pair(np.ascontiguousarray(inner.T)),
    )


def sin_small(x):
    y = x * x
    p = 1.0 / 6227020800.0
    p = p * y - 1.0 / 39916800.0
    p = p * y + 1.0 / 362880.0
    p = p * y - 1.0 / 5040.0
    p = p * y + 1.0 / 120.0
    p = p * y - 1.0 / 6.0
    return x + x * y * p


def minus_pi_times(x, n):
    return ((x - n * 3.140625) - n * 9.67502593994140625e-4) - n * 1.509957990978376e-7


def parity_sign(n):
    return 1.0 - 2.0 * (n - 2.0 * jnp.floor(n * 0.5))


def sin_cos(x):
    scaled = x * (1.0 / math.pi)
    n = jnp.floor(scaled + 0.5)
    sine = parity_sign(n) * sin_small(minus_pi_times(x, n))
    m = jnp.floor(scaled) + 1.0
    cosine = parity_sign(m) * sin_small(minus_pi_times(x, m - 0.5))
    return sine, cosine


def diagonal(n):
    return lax.broadcasted_iota(jnp.int32, (n, n), 0) == lax.broadcasted_iota(jnp.int32, (n, n), 1)


def column(row):
    return jnp.sum(jnp.where(diagonal(row.shape[1]), row, 0.0), axis=1, keepdims=True)


def as_row(col):
    return jnp.sum(jnp.where(diagonal(col.shape[0]), col, 0.0), axis=0, keepdims=True)


def inverse_spread(rate, length):
    y = rate * (2.0 / length)
    p = 1.0 / 5040.0
    for k in (720.0, 120.0, 24.0, 6.0, 2.0, 1.0):
        p = 1.0 / k - y * p
    return jnp.sqrt(y * p / (1.0 - jnp.exp(-2.0 * rate)))


def split(x):
    high = x.astype(BF16)
    return high, (x - high.astype(F32)).astype(BF16)


def dot_one(a, b, da=1, db=0):
    return lax.dot_general(a, b, (((da,), (db,)), ((), ())), preferred_element_type=F32)


def dot3(a, b, da=1, db=0):
    return dot_one(
        jnp.concatenate([a[0], a[0], a[1]], da), jnp.concatenate([b[0], b[1], b[0]], db), da, db
    )


def dot_exact(a, b, dims):
    return lax.dot_general(a, b, (dims, ((), ())), precision=PRECISE, preferred_element_type=F32)


def kernel(
    devices, y_size,
    proj_hbm, cot_hbm, sw_hbm, fin_hbm, fout_hbm, rates_hbm, f1_hbm, f1t_hbm, tw_hbm, f2_hbm, f2t_hbm,
    gp, short_rows, fout_out, fin_out,
    proj, cot, sw, fin, fout, rates, f1, f1t, tw, f2, f2t,
    feat, hcos, env, raw32, raw_send, raw, k_send, kbuf, shifts, kv, spec, ybuf, yown, xb, kg_send, kg_ret,
    res, gp_send, gp_ret, gp32, hid2, feat2, r_own, r_sib, r_z, r_x, r_xy, s_own, s_sib, s_all,
    load_sem, in_send, in_recv, raw_recv, sib_send, sib_recv, x_send, x_recv, ret_send, ret_recv,
    red_send, red_recv,
):
    chips = devices // 2
    channels = cot.shape[0]
    length = devices * TOKENS
    outer = devices * ROWS
    half = outer // 2
    local = half + EXTRA
    blocks = channels // 8
    units = hcos.shape[0]
    me = lax.axis_index("seq")
    yi = lax.axis_index("ch")
    q = lax.div(me, 2)
    core = lax.rem(me, 2)
    sib = me + 1 - 2 * core

    def seq_dev(chip):
        return {"seq": 2 * chip + core}

    barrier = pltpu.get_barrier_semaphore()

    order = (3, 4, 0, 1, 2, 5, 6, 7, 8, 9, 10)
    moves = (
        (fin_hbm, fin), (rates_hbm, rates), (fout_hbm, fout), (proj_hbm, proj), (cot_hbm, cot), (sw_hbm, sw),
        (f1_hbm.at[core], f1), (tw_hbm.at[core], tw), (f2_hbm, f2), (f2t_hbm, f2t), (f1t_hbm.at[core], f1t),
    )
    loads = [pltpu.make_async_copy(src, dst, load_sem.at[i]) for i, (src, dst) in enumerate(moves)]
    x_size = chips // Z_SIZE
    xi = lax.div(q, Z_SIZE)
    zi = lax.rem(q, Z_SIZE)

    def cross(r):
        x = lax.rem(xi + lax.rem(lax.div(r, y_size), x_size), x_size)
        other = lax.rem(core + lax.div(r, x_size * y_size), 2)
        return {"ch": lax.rem(yi + lax.rem(r, y_size), y_size), "seq": 2 * (x * Z_SIZE + zi) + other}

    def ring_offset(k):
        return Z_SIZE // 2 + jnp.where(lax.rem(k, 2) == 1, -lax.div(k + 1, 2), lax.div(k, 2))

    def greet_cross(r, carry):
        pl.semaphore_signal(barrier, inc=1, device_id=cross(r), device_id_type=MESH)
        return carry

    def greet_far(k, carry):
        z = lax.rem(zi + ring_offset(k), Z_SIZE)
        for dx in (2, 1, 3, 0):
            chip = lax.rem(xi + dx, x_size) * Z_SIZE + z
            pl.semaphore_signal(barrier, inc=1, device_id=seq_dev(chip), device_id_type=MESH)
        return carry

    lax.fori_loop(0, Z_SIZE - 1, greet_far, 0)
    for dx in range(1, x_size):
        chip = lax.rem(xi + dx, x_size) * Z_SIZE + zi
        pl.semaphore_signal(barrier, inc=1, device_id=seq_dev(chip), device_id_type=MESH)
    lax.fori_loop(1, 2 * x_size * y_size, greet_cross, 0)
    for i in order:
        loads[i].start()

    def remote(src, dst, send_sem, recv_sem, device):
        return pltpu.make_async_remote_copy(
            src, dst, send_sem, recv_sem, device_id=device, device_id_type=MESH
        )

    def wait_bytes(part, sem):
        pltpu.make_async_copy(part, part, sem).wait()

    for copy in loads[3:5]:
        copy.wait()

    for s in range(4):
        value = cot[...].astype(F32) if s == 3 else proj[s].astype(F32)
        for cb in range(blocks):
            for j in range(ROWS):
                rows = pl.ds(cb * 8 * 4 * ROWS + s * ROWS + j, 8, stride=4 * ROWS)
                raw32[rows, :] = value[cb * 8 : cb * 8 + 8, j * LANES : (j + 1) * LANES]
    raw_send[...] = raw32[...].reshape(raw_send.shape).astype(BF16)

    pl.semaphore_wait(barrier, chips - 1 + 2 * x_size * y_size - 1)

    def rows_of(chip):
        return pl.ds(pl.multiple_of(chip * ROWS, ROWS), ROWS)

    def to_chips(start):
        def one(r, carry):
            start(lax.rem(q + r, chips))
            return carry

        lax.fori_loop(1, chips, one, 0)

    to_chips(
        lambda chip: remote(
            raw_send.at[chip], raw.at[q, core], in_send.at[0], raw_recv.at[q], seq_dev(chip)
        ).start()
    )
    raw[q, core] = raw_send[q]

    row = lax.broadcasted_iota(jnp.int32, feat.shape, 0)
    position = me * TOKENS + lax.broadcasted_iota(jnp.int32, feat.shape, 1)
    odd = row & 1
    phase = position * (1 + (row >> 1) * 499) - odd * (length // 4) + length // 2
    phase = (phase & (length - 1)) - length // 2
    feat[...] = sin_small((length // 4 - jnp.abs(phase)).astype(F32) * (2.0 * math.pi / length))
    for copy in loads[:3]:
        copy.wait()

    preact = dot_exact(fin[...], feat[...], ((0,), (0,)))
    sine, cosine = sin_cos(preact)
    hid2[0], hid2[1] = split(sine)
    feat2[0], feat2[1] = split(feat[...])
    hcos[...] = cosine
    relative = (me * TOKENS + lax.broadcasted_iota(jnp.int32, env.shape, 1)).astype(F32) * (1.0 / length)
    rate = column(rates[...])
    env[...] = jnp.exp(-rate * relative) * inverse_spread(rate, length)
    filt = env[...] * dot3(split(fout[...]), (hid2[0], hid2[1]))
    for cb in range(blocks):
        for j in range(ROWS):
            k_send[pl.ds(cb * 64 + j, 8, stride=8), :] = filt[cb * 8 : cb * 8 + 8, j * LANES : (j + 1) * LANES]

    for copy in loads[5:]:
        copy.wait()
    lane9 = lax.broadcasted_iota(jnp.int32, (1, channels), 1)
    taps = [
        [jnp.sum(jnp.where(lane9 == q, sw[s, j : j + 1, :], 0.0), axis=1, keepdims=True) for j in range(3)]
        for s in range(3)
    ]

    def hand_on(chip):
        remote(raw.at[chip, core], raw.at[chip, core], sib_send.at[0], sib_recv.at[0], {"seq": sib}).start()

    def arrived(r, carry):
        chip = lax.rem(q + chips - r, chips)
        pltpu.make_async_copy(raw.at[chip, core], raw.at[chip, core], raw_recv.at[chip]).wait()
        hand_on(chip)
        return carry

    hand_on(q)
    lax.fori_loop(1, chips // 2, arrived, 0)
    to_chips(
        lambda chip: remote(
            k_send.at[rows_of(chip)], kbuf.at[q, core], in_send.at[1], in_recv.at[1], seq_dev(chip)
        ).start()
    )
    kbuf[q, core] = k_send[rows_of(q)]
    lax.fori_loop(chips // 2, chips, arrived, 0)
    wait_bytes(raw_send, sib_recv.at[0])

    lane = lax.broadcasted_iota(jnp.int32, (outer, LANES), 1)
    line = lax.broadcasted_iota(jnp.int32, (outer, LANES), 0)
    mixed = []
    for s in range(3):
        x = raw[:, :, s].astype(F32).reshape(outer, LANES)
        total = taps[s][0] * x
        for j in range(1, 3):
            turned = pltpu.roll(x, j, 1)
            before = jnp.where(line == 0, 0.0, pltpu.roll(turned, 1, 0))
            moved = jnp.where(lane < j, before, turned)
            shifts[s, j - 1] = moved
            total = total + taps[s][j] * moved
        mixed.append(total)
    kv[0] = mixed[1]
    kv[1] = mixed[2]
    gated = mixed[1] * mixed[2]
    grad_conv = raw[:, :, 3].astype(F32).reshape(outer, LANES) * mixed[0]

    def forward(values, slots):
        u = dot3((f1[0], f1[1]), split(jnp.concatenate(values, 1) if len(values) > 1 else values[0]))
        for at, s in enumerate(slots):
            ur = u[:half, at * LANES : (at + 1) * LANES]
            ui = u[half:, at * LANES : (at + 1) * LANES]
            v = jnp.concatenate([ur * tw[0] - ui * tw[1], ur * tw[1] + ui * tw[0]], 1)
            spec[s] = dot3(split(v), (f2[0], f2[1]))

    def parts(s):
        return spec[s, :, :LANES], spec[s, :, LANES:]

    def inverse_rows(re, im):
        z = dot3(split(jnp.concatenate([re, im], 1)), (f2t[0], f2t[1]))
        zr, zi = z[:, :LANES], z[:, LANES:]
        return jnp.concatenate([zr * tw[0] + zi * tw[1], zi * tw[0] - zr * tw[1]], 0)

    mine = pl.ds(pl.multiple_of(core * (half - EXTRA), ROWS), local)

    def finish(slots, columns, exchange):
        right = split(jnp.concatenate(columns, 1) if len(columns) > 1 else columns[0])
        for own in (False, True):
            rows = slice(local, 2 * local) if own else slice(0, local)
            y = dot3((f1t[0, rows, :], f1t[1, rows, :]), right)
            for at, s in enumerate(slots):
                (yown if own else ybuf)[s] = y[:, at * LANES : (at + 1) * LANES]
            if not own:
                exchange.start()

    def swap(lo, hi, slot):
        return remote(
            ybuf.at[lo:hi], xb.at[lo:hi], x_send.at[slot], x_recv.at[slot], {"seq": sib}
        )

    forward([gated, grad_conv], [1, 2])
    gr, gi = parts(1)
    dr, di = parts(2)
    swap_k = swap(0, 1, 0)
    finish([0], [inverse_rows(dr * gr + di * gi, di * gr - dr * gi)], swap_k)

    is_local = lax.div(me, chips) == core

    def send_half(src, dst, slot, first, end):
        at = lax.rem(me, chips)

        def one(r, carry):
            d = lax.rem(at + r, chips)
            device = {"seq": core * chips + d}
            remote(src.at[d], dst.at[q], ret_send.at[slot], ret_recv.at[slot], device).start()
            return carry

        lax.fori_loop(max(first, 1), end, one, 0)
        if first == 0:

            @pl.when(is_local)
            def _():
                pltpu.make_async_copy(src.at[at], dst.at[q], ret_recv.at[slot]).start()

            @pl.when(jnp.logical_not(is_local))
            def _():
                one(0, 0)

    swap_k.wait()
    own_rows = pl.ds(pl.multiple_of(core * EXTRA, ROWS), half)
    kg = (yown[0, own_rows, :] + xb[0, own_rows, :]) * (1.0 / length)
    kg_send[...] = kg.reshape(kg_send.shape)

    def kg_push(d):
        device = {"seq": core * chips + d}
        remote(kg_send.at[d], kg_ret.at[q], ret_send.at[0], ret_recv.at[0], device).start()

    def kg_blocks(k):
        z = lax.rem(zi + ring_offset(k), Z_SIZE)
        return [x * 2 * Z_SIZE + 2 * z + c for x in range(x_size // 2) for c in range(2)]

    def kg_far(k, carry):
        for d in kg_blocks(k):
            kg_push(d)
        return carry

    lax.fori_loop(0, Z_SIZE - 1, kg_far, 0)
    for d in kg_blocks(jnp.int32(Z_SIZE - 1)):
        is_me = core * chips + d == me

        @pl.when(is_me)
        def _():
            pltpu.make_async_copy(kg_send.at[d], kg_ret.at[q], ret_recv.at[0]).start()

        @pl.when(jnp.logical_not(is_me))
        def _():
            kg_push(d)


    wait_bytes(k_send.at[pl.ds(0, (chips - 1) * ROWS)], in_recv.at[1])
    sib_k = remote(kbuf.at[:, core], kbuf.at[:, core], sib_send.at[1], sib_recv.at[1], {"seq": sib})
    sib_k.start()

    sib_k.wait()
    forward([kbuf[...].reshape(outer, LANES)], [0])
    kr, ki = parts(0)
    swap_c = swap(1, 3, 1)
    finish(
        [1, 2],
        [
            inverse_rows(gr * kr - gi * ki, gr * ki + gi * kr),
            inverse_rows(dr * kr + di * ki, di * kr - dr * ki),
        ],
        swap_c,
    )
    swap_c.wait()

    conv_out = (yown[1] + xb[1]) * (1.0 / length)
    grad_gated = (yown[2] + xb[2]) * (1.0 / length)
    lane = lax.broadcasted_iota(jnp.int32, (local, LANES), 1)
    line = lax.broadcasted_iota(jnp.int32, (local, LANES), 0)
    is_mine = (line >= core * EXTRA) & (line < core * EXTRA + half)
    cot_all = raw[:, :, 3].astype(F32).reshape(outer, LANES)
    gp32[0:outer, :] = cot_all
    cot_mine = gp32[mine, :]
    grad_mixed = [cot_mine * conv_out, grad_gated * kv[1, mine, :], grad_gated * kv[0, mine, :]]
    for s in range(3):
        g = grad_mixed[s]
        total = taps[s][0] * g
        for j in range(1, 3):
            turned = pltpu.roll(g, LANES - j, 1)
            after = jnp.where(line == local - 1, 0.0, pltpu.roll(turned, local - 1, 0))
            total = total + taps[s][j] * jnp.where(lane >= LANES - j, after, turned)
        res[s] = total
        gp_send[:, s] = res[s, own_rows, :].reshape(chips, ROWS, LANES).astype(BF16)
    send_half(gp_send, gp_ret, 1, 0, chips // 2)

    wait_bytes(kg_send, ret_recv.at[0])
    weighted = env[...] * jnp.concatenate(
        [
            jnp.concatenate(
                [
                    kg_ret.at[pl.ds(cb * 8, 8)][:, j, :] for j in range(ROWS)
                ], 1,
            )
            for cb in range(blocks)
        ], 0,
    )
    pair = split(weighted)
    out_part = dot3(pair, (hid2[0], hid2[1]), 1, 1)
    grad_hidden = dot3(split(fout[...]), pair, 0, 0) * hcos[...]
    in_part = dot3((feat2[0], feat2[1]), split(grad_hidden), 1, 1)
    for half_at in range(2):
        for at, part in enumerate((out_part, in_part)):
            first = half_at * (channels // 2)
            middle, end = first + channels // 4, first + channels // 2
            r_own[half_at, at] = jnp.concatenate([part[first:middle], part[middle:end]], 1)
    red_core = remote(r_own.at[1 - core], r_sib, red_send.at[0], red_recv.at[0], {"seq": sib})
    red_core.start()
    lane1 = lax.broadcasted_iota(jnp.int32, (1, LANES), 1)
    short = jnp.zeros((1, LANES), F32)
    for s in range(3):
        g = jnp.where(is_mine, grad_mixed[s], 0.0)
        gp32[0:outer, :] = raw[:, :, s].astype(F32).reshape(outer, LANES)
        for j in range(3):
            x = gp32[mine, :] if j == 0 else shifts[s, j - 1, mine, :]
            total = jnp.sum(jnp.sum(g * x, axis=0, keepdims=True), axis=1, keepdims=True)
            short = jnp.where(lane1 == s * 3 + j, total, short)
    s_own[...] = short
    sib_short = remote(s_own, s_sib, sib_send.at[2], sib_recv.at[2], {"seq": sib})
    sib_short.start()

    red_core.wait()
    r_z[zi] = r_own[core] + r_sib[...]

    def to_z(r, carry):
        device = seq_dev(xi * Z_SIZE + lax.rem(zi + r, Z_SIZE))
        remote(r_z.at[zi], r_z.at[zi], red_send.at[1], red_recv.at[1], device).start()
        return carry

    lax.fori_loop(1, Z_SIZE, to_z, 0)


    sib_short.wait()
    s_all[q] = s_own[...] + s_sib[...]
    to_chips(
        lambda chip: remote(s_all.at[q], s_all.at[q], red_send.at[4], red_recv.at[4], seq_dev(chip)).start()
    )
    send_half(gp_send, gp_ret, 1, chips // 2, chips)

    z_rest = r_z.at[pl.ds(0, Z_SIZE - 1)]
    wait_bytes(z_rest, red_recv.at[1])
    total = r_z[0]
    for i in range(1, Z_SIZE):
        total = total + r_z[i]
    here = xi * y_size + yi
    r_x[core, xi] = total[0]
    r_xy[core, here] = total[1]

    def to_cross(r, carry):
        remote(r_xy.at[core, here], r_xy.at[core, here], red_send.at[2], red_recv.at[2], cross(r)).start()
        return carry

    def to_x(r, carry):
        remote(r_x.at[core, xi], r_x.at[core, xi], red_send.at[3], red_recv.at[3], cross(r * y_size)).start()
        return carry

    lax.fori_loop(1, 2 * x_size * y_size, to_cross, 0)
    lax.fori_loop(1, 2 * x_size, to_x, 0)

    wait_bytes(gp_send, ret_recv.at[1])
    gp32[...] = gp_ret[...].astype(F32).reshape(gp32.shape)
    for s in range(3):
        for cb in range(blocks):
            for j in range(ROWS):
                rows = pl.ds(cb * 8 * 3 * ROWS + s * ROWS + j, 8, stride=3 * ROWS)
                gp[s, cb * 8 : cb * 8 + 8, j * LANES : (j + 1) * LANES] = gp32[rows, :].astype(BF16)

    scale = 1.0 / math.sqrt(length)
    wait_bytes(s_all.at[pl.ds(0, chips - 1)], red_recv.at[4])
    shorts = s_all[...].reshape(channels, LANES) * scale
    for at in range(9):
        short_rows[at // 3, at % 3 : at % 3 + 1, :] = as_row(shorts[:, at : at + 1])

    group = 2 * x_size * y_size
    wait_bytes(gp32.at[pl.ds(0, (2 * x_size - 1) * (channels // 4))], red_recv.at[3])
    wait_bytes(gp32.at[pl.ds(0, (group - 1) * (channels // 4))], red_recv.at[2])
    for half_at in range(2):
        out_total = r_x[half_at, 0]
        for x in range(1, x_size):
            out_total = out_total + r_x[half_at, x]
        in_total = r_xy[half_at, 0]
        for at in range(1, x_size * y_size):
            in_total = in_total + r_xy[half_at, at]
        first = half_at * (channels // 2)
        middle, end = first + channels // 4, first + channels // 2
        for out, part in ((fout_out, out_total * scale), (fin_out, in_total * scale)):
            out[first:middle, :] = part[:, :units]
            out[middle:end, :] = part[:, units:]

    wait_bytes(raw_send.at[pl.ds(0, chips - 1)], in_send.at[0])
    wait_bytes(k_send.at[pl.ds(0, (chips - 1) * ROWS)], in_send.at[1])
    for slot, buf in ((0, kg_send), (1, gp_send)):
        wait_bytes(buf.at[pl.ds(0, chips - 1)], ret_send.at[slot])

        @pl.when(jnp.logical_not(is_local))
        def _():
            wait_bytes(buf.at[0], ret_send.at[slot])

    wait_bytes(raw_send, sib_send.at[0])
    wait_bytes(z_rest, red_send.at[1])
    wait_bytes(gp32.at[pl.ds(0, (2 * x_size - 1) * (channels // 4))], red_send.at[3])
    wait_bytes(gp32.at[pl.ds(0, (group - 1) * (channels // 4))], red_send.at[2])
    wait_bytes(s_all.at[pl.ds(0, chips - 1)], red_send.at[4])


def move_outputs(*refs):
    count = (len(refs) - 1) // 2
    copies = [pltpu.make_async_copy(refs[i], refs[count + i], refs[-1].at[i]) for i in range(count)]
    for copy in copies:
        copy.start()
    for copy in copies:
        copy.wait()


def shards(devices, y_size, tables, proj, cotangent, short_w, filter_in, filter_out, rates):
    channels = cotangent.shape[0]
    feats, order = filter_in.shape
    chips = devices // 2
    outer = devices * ROWS
    half = outer // 2
    hbm = pl.BlockSpec(memory_space=pltpu.HBM)
    dma = pltpu.SemaphoreType.DMA

    def f32(*shape):
        return pltpu.VMEM(shape, F32)

    def bf16(*shape):
        return pltpu.VMEM(shape, BF16)

    operands = (
        proj, cotangent, short_w.transpose(0, 2, 1), filter_in, filter_out.T, rates.reshape(1, channels), *tables
    )
    shapes = (
        jax.ShapeDtypeStruct(proj.shape, BF16),
        jax.ShapeDtypeStruct((3, 3, channels), F32),
        jax.ShapeDtypeStruct((channels, order), F32),
        jax.ShapeDtypeStruct((feats, order), F32),
    )
    results = pl.pallas_call(
        functools.partial(kernel, devices, y_size),
        out_shape=shapes,
        in_specs=[hbm] * 11,
        out_specs=(pl.BlockSpec(memory_space=pltpu.VMEM),) * 4,
        scratch_shapes=[
            bf16(*proj.shape),
            bf16(*cotangent.shape),
            f32(3, 3, channels),
            f32(feats, order),
            f32(channels, order),
            f32(1, channels),
            bf16(2, outer, outer),
            bf16(2, outer + 2 * EXTRA, outer),
            f32(2, half, LANES),
            bf16(2, 2 * LANES, 2 * LANES),
            bf16(2, 2 * LANES, 2 * LANES),
            f32(feats, TOKENS),
            f32(order, TOKENS),
            f32(channels, TOKENS),
            f32(chips * 4 * ROWS, LANES),
            bf16(chips, 4, ROWS, LANES),
            bf16(chips, 2, 4, ROWS, LANES),
            f32(chips * ROWS, LANES),
            f32(chips, 2, ROWS, LANES),
            f32(3, 2, outer, LANES),
            f32(2, outer, LANES),
            f32(3, half, 2 * LANES),
            f32(3, half + EXTRA, LANES),
            f32(3, half + EXTRA, LANES),
            f32(3, half + EXTRA, LANES),
            f32(chips, ROWS, LANES),
            f32(chips, ROWS, LANES),
            f32(3, half + EXTRA, LANES),
            bf16(chips, 3, ROWS, LANES),
            bf16(chips, 3, ROWS, LANES),
            f32(chips * 3 * ROWS, LANES),
            bf16(2, order, TOKENS),
            bf16(2, feats, TOKENS),
            f32(2, 2, channels // 4, LANES),
            f32(2, channels // 4, LANES),
            f32(Z_SIZE, 2, channels // 4, LANES),
            f32(2, chips // Z_SIZE, channels // 4, LANES),
            f32(2, chips // Z_SIZE * y_size, channels // 4, LANES),
            f32(1, LANES),
            f32(1, LANES),
            f32(chips, 1, LANES),
            dma((11,)), dma((2,)), dma((2,)), dma((chips,)), dma((3,)), dma((3,)), dma((2,)), dma((2,)),
            dma((2,)), dma((2,)), dma((5,)), dma((5,)),
        ],
        compiler_params=pltpu.CompilerParams(
            collective_id=0, has_side_effects=True, vmem_limit_bytes=32 << 20
        ),
    )(*[pltpu.with_memory_space_constraint(x, pltpu.HBM) for x in operands])
    grad_proj, grad_short, grad_out, grad_in = pl.pallas_call(
        move_outputs,
        out_shape=shapes,
        in_specs=[pl.BlockSpec(memory_space=pl.ANY)] * 4,
        out_specs=(hbm,) * 4,
        scratch_shapes=[dma((4,))],
        compiler_params=pltpu.CompilerParams(vmem_limit_bytes=1 << 20),
    )(*results)
    return grad_proj, grad_short.transpose(0, 2, 1), grad_out.T, grad_in


def solution(mesh):
    devices, y_size = mesh.shape["seq"], mesh.shape["ch"]
    tables = make_tables(devices)

    def run(*args):
        return shards(devices, y_size, [jnp.asarray(t) for t in tables], *args)

    return jax.shard_map(
        run,
        mesh=mesh,
        in_specs=(
            P(None, "ch", "seq"),
            P("ch", "seq"),
            P(None, "ch", None),
            P(),
            P(None, "ch"),
            P("ch"),
        ),
        out_specs=(P(None, "ch", "seq"), P(None, "ch", None), P(None, "ch"), P()),
        check_vma=False,
    )
```

```python
import functools
import math

import jax
import jax.numpy as jnp
import ml_dtypes
import numpy as np
from jax import lax
from jax.experimental import pallas as pl
from jax.experimental.pallas import tpu as pltpu
from jax.sharding import PartitionSpec as P

MESH = pl.DeviceIdType.MESH
F32 = jnp.float32
BF16 = jnp.bfloat16
PRECISE = lax.Precision.HIGHEST
LANES = 128
ROWS = 8
TOKENS = ROWS * LANES
Z_SIZE = 8
EXTRA = 16


def bf16_pair(table):
    high = table.astype(ml_dtypes.bfloat16)
    low = (table - high.astype(np.float64)).astype(ml_dtypes.bfloat16)
    return np.stack([high, low])


def make_tables(devices):
    outer = devices * ROWS
    length = outer * LANES
    half = outer // 2
    a = np.arange(outer)
    fwd, back, twiddle = [], [], []
    for core in range(2):
        k1 = core * half + np.arange(half)
        num = (a[None, :] * (4 * k1[:, None] + 1)) % (4 * outer)
        angle = num * (2.0 * np.pi / (4 * outer))
        matrix = np.concatenate([np.cos(angle), -np.sin(angle)], 0)
        fwd.append(bf16_pair(matrix))
        starts = [(1 - core) * (half - EXTRA), core * (half - EXTRA)]
        rows = np.concatenate([start + np.arange(half + EXTRA) for start in starts])
        back.append(bf16_pair(np.ascontiguousarray(matrix.T[rows])))
        num = (np.arange(LANES)[None, :] * (4 * k1[:, None] + 1)) % (4 * length)
        angle = num * (2.0 * np.pi / (4 * length))
        twiddle.append(np.stack([np.cos(angle), -np.sin(angle)]).astype(np.float32))
    b = np.arange(LANES)
    angle = (b[:, None] * b[None, :] % LANES) * (2.0 * np.pi / LANES)
    c, s = np.cos(angle), np.sin(angle)
    inner = np.block([[c, -s], [s, c]])
    return (
        np.stack(fwd),
        np.stack(back),
        np.stack(twiddle),
        bf16_pair(inner),
        bf16_pair(np.ascontiguousarray(inner.T)),
    )


def sin_small(x):
    y = x * x
    p = 1.0 / 6227020800.0
    p = p * y - 1.0 / 39916800.0
    p = p * y + 1.0 / 362880.0
    p = p * y - 1.0 / 5040.0
    p = p * y + 1.0 / 120.0
    p = p * y - 1.0 / 6.0
    return x + x * y * p


def minus_pi_times(x, n):
    return ((x - n * 3.140625) - n * 9.67502593994140625e-4) - n * 1.509957990978376e-7


def parity_sign(n):
    return 1.0 - 2.0 * (n - 2.0 * jnp.floor(n * 0.5))


def sin_cos(x):
    scaled = x * (1.0 / math.pi)
    n = jnp.floor(scaled + 0.5)
    sine = parity_sign(n) * sin_small(minus_pi_times(x, n))
    m = jnp.floor(scaled) + 1.0
    cosine = parity_sign(m) * sin_small(minus_pi_times(x, m - 0.5))
    return sine, cosine


def diagonal(n):
    return lax.broadcasted_iota(jnp.int32, (n, n), 0) == lax.broadcasted_iota(jnp.int32, (n, n), 1)


def column(row):
    return jnp.sum(jnp.where(diagonal(row.shape[1]), row, 0.0), axis=1, keepdims=True)


def as_row(col):
    return jnp.sum(jnp.where(diagonal(col.shape[0]), col, 0.0), axis=0, keepdims=True)


def inverse_spread(rate, length):
    y = rate * (2.0 / length)
    p = 1.0 / 5040.0
    for k in (720.0, 120.0, 24.0, 6.0, 2.0, 1.0):
        p = 1.0 / k - y * p
    return jnp.sqrt(y * p / (1.0 - jnp.exp(-2.0 * rate)))


def split(x):
    high = x.astype(BF16)
    return high, (x - high.astype(F32)).astype(BF16)


def dot_one(a, b, da=1, db=0):
    return lax.dot_general(a, b, (((da,), (db,)), ((), ())), preferred_element_type=F32)


def dot3(a, b, da=1, db=0):
    return dot_one(
        jnp.concatenate([a[0], a[0], a[1]], da), jnp.concatenate([b[0], b[1], b[0]], db), da, db
    )


def dot_exact(a, b, dims):
    return lax.dot_general(a, b, (dims, ((), ())), precision=PRECISE, preferred_element_type=F32)


def kernel(
    devices, y_size,
    proj_hbm, cot_hbm, sw_hbm, fin_hbm, fout_hbm, rates_hbm, f1_hbm, f1t_hbm, tw_hbm, f2_hbm, f2t_hbm,
    gp, short_rows, fout_out, fin_out,
    proj, cot, sw, fin, fout, rates, f1, f1t, tw, f2, f2t,
    feat, hcos, env, raw32, raw_send, raw, k_send, kbuf, shifts, kv, spec, ybuf, yown, xb, kg_send, kg_ret,
    res, gp_send, gp_ret, gp32, hid2, feat2, r_own, r_sib, r_z, r_x, r_xy, s_own, s_sib, s_all,
    load_sem, in_send, in_recv, raw_recv, sib_send, sib_recv, x_send, x_recv, ret_send, ret_recv,
    red_send, red_recv,
):
    chips = devices // 2
    channels = cot.shape[0]
    length = devices * TOKENS
    outer = devices * ROWS
    half = outer // 2
    local = half + EXTRA
    blocks = channels // 8
    units = hcos.shape[0]
    me = lax.axis_index("seq")
    yi = lax.axis_index("ch")
    q = lax.div(me, 2)
    core = lax.rem(me, 2)
    sib = me + 1 - 2 * core

    def seq_dev(chip):
        return {"seq": 2 * chip + core}

    barrier = pltpu.get_barrier_semaphore()

    order = (3, 4, 0, 1, 2, 5, 6, 7, 8, 9, 10)
    moves = (
        (fin_hbm, fin), (rates_hbm, rates), (fout_hbm, fout), (proj_hbm, proj), (cot_hbm, cot), (sw_hbm, sw),
        (f1_hbm.at[core], f1), (tw_hbm.at[core], tw), (f2_hbm, f2), (f2t_hbm, f2t), (f1t_hbm.at[core], f1t),
    )
    loads = [pltpu.make_async_copy(src, dst, load_sem.at[i]) for i, (src, dst) in enumerate(moves)]
    x_size = chips // Z_SIZE
    xi = lax.div(q, Z_SIZE)
    zi = lax.rem(q, Z_SIZE)

    def cross(r):
        x = lax.rem(xi + lax.rem(lax.div(r, y_size), x_size), x_size)
        other = lax.rem(core + lax.div(r, x_size * y_size), 2)
        return {"ch": lax.rem(yi + lax.rem(r, y_size), y_size), "seq": 2 * (x * Z_SIZE + zi) + other}

    def ring_offset(k):
        return Z_SIZE // 2 + jnp.where(lax.rem(k, 2) == 1, -lax.div(k + 1, 2), lax.div(k, 2))

    def greet_cross(r, carry):
        pl.semaphore_signal(barrier, inc=1, device_id=cross(r), device_id_type=MESH)
        return carry

    def greet_far(k, carry):
        z = lax.rem(zi + ring_offset(k), Z_SIZE)
        for dx in (2, 1, 3, 0):
            chip = lax.rem(xi + dx, x_size) * Z_SIZE + z
            pl.semaphore_signal(barrier, inc=1, device_id=seq_dev(chip), device_id_type=MESH)
        return carry

    lax.fori_loop(0, Z_SIZE - 1, greet_far, 0)
    for dx in range(1, x_size):
        chip = lax.rem(xi + dx, x_size) * Z_SIZE + zi
        pl.semaphore_signal(barrier, inc=1, device_id=seq_dev(chip), device_id_type=MESH)
    lax.fori_loop(1, 2 * x_size * y_size, greet_cross, 0)
    for i in order:
        loads[i].start()

    def remote(src, dst, send_sem, recv_sem, device):
        return pltpu.make_async_remote_copy(
            src, dst, send_sem, recv_sem, device_id=device, device_id_type=MESH
        )

    def wait_bytes(part, sem):
        pltpu.make_async_copy(part, part, sem).wait()

    for copy in loads[3:5]:
        copy.wait()

    for s in range(4):
        value = cot[...].astype(F32) if s == 3 else proj[s].astype(F32)
        for cb in range(blocks):
            for j in range(ROWS):
                rows = pl.ds(cb * 8 * 4 * ROWS + s * ROWS + j, 8, stride=4 * ROWS)
                raw32[rows, :] = value[cb * 8 : cb * 8 + 8, j * LANES : (j + 1) * LANES]
    raw_send[...] = raw32[...].reshape(raw_send.shape).astype(BF16)

    pl.semaphore_wait(barrier, chips - 1 + 2 * x_size * y_size - 1)

    def rows_of(chip):
        return pl.ds(pl.multiple_of(chip * ROWS, ROWS), ROWS)

    def to_chips(start):
        def far(k, carry):
            z = lax.rem(zi + ring_offset(k), Z_SIZE)
            for dx in (2, 1, 3, 0):
                start(lax.rem(xi + dx, x_size) * Z_SIZE + z)
            return carry

        lax.fori_loop(0, Z_SIZE - 1, far, 0)
        for dx in (2, 1, 3):
            start(lax.rem(xi + dx, x_size) * Z_SIZE + zi)

    def send_raw(chip):
        remote(raw_send.at[chip], raw.at[q, core], in_send.at[0], raw_recv.at[q], seq_dev(chip)).start()

    to_chips(send_raw)
    raw[q, core] = raw_send[q]

    row = lax.broadcasted_iota(jnp.int32, feat.shape, 0)
    position = me * TOKENS + lax.broadcasted_iota(jnp.int32, feat.shape, 1)
    odd = row & 1
    phase = position * (1 + (row >> 1) * 499) - odd * (length // 4) + length // 2
    phase = (phase & (length - 1)) - length // 2
    feat[...] = sin_small((length // 4 - jnp.abs(phase)).astype(F32) * (2.0 * math.pi / length))
    for copy in loads[:3]:
        copy.wait()

    preact = dot_exact(fin[...], feat[...], ((0,), (0,)))
    sine, cosine = sin_cos(preact)
    hid2[0], hid2[1] = split(sine)
    feat2[0], feat2[1] = split(feat[...])
    hcos[...] = cosine
    relative = (me * TOKENS + lax.broadcasted_iota(jnp.int32, env.shape, 1)).astype(F32) * (1.0 / length)
    rate = column(rates[...])
    env[...] = jnp.exp(-rate * relative) * inverse_spread(rate, length)
    filt = env[...] * dot3(split(fout[...]), (hid2[0], hid2[1]))
    for cb in range(blocks):
        for j in range(ROWS):
            k_send[pl.ds(cb * 64 + j, 8, stride=8), :] = filt[cb * 8 : cb * 8 + 8, j * LANES : (j + 1) * LANES]

    for copy in loads[5:]:
        copy.wait()
    lane9 = lax.broadcasted_iota(jnp.int32, (1, channels), 1)
    taps = [
        [jnp.sum(jnp.where(lane9 == q, sw[s, j : j + 1, :], 0.0), axis=1, keepdims=True) for j in range(3)]
        for s in range(3)
    ]

    def hand_on(chip):
        remote(raw.at[chip, core], raw.at[chip, core], sib_send.at[0], sib_recv.at[0], {"seq": sib}).start()

    def arrived(chip):
        pltpu.make_async_copy(raw.at[chip, core], raw.at[chip, core], raw_recv.at[chip]).wait()
        hand_on(chip)

    def arrived_far(k, carry):
        z = lax.rem(zi + Z_SIZE - ring_offset(k), Z_SIZE)
        for dx in (2, 3, 1, 0):
            arrived(lax.rem(xi + dx, x_size) * Z_SIZE + z)
        return carry

    hand_on(q)
    lax.fori_loop(0, Z_SIZE // 2, arrived_far, 0)
    to_chips(
        lambda chip: remote(
            k_send.at[rows_of(chip)], kbuf.at[q, core], in_send.at[1], in_recv.at[1], seq_dev(chip)
        ).start()
    )
    kbuf[q, core] = k_send[rows_of(q)]
    lax.fori_loop(Z_SIZE // 2, Z_SIZE - 1, arrived_far, 0)
    for dx in (2, 3, 1):
        arrived(lax.rem(xi + dx, x_size) * Z_SIZE + zi)
    wait_bytes(raw_send, sib_recv.at[0])

    lane = lax.broadcasted_iota(jnp.int32, (outer, LANES), 1)
    line = lax.broadcasted_iota(jnp.int32, (outer, LANES), 0)
    mixed = []
    for s in range(3):
        x = raw[:, :, s].astype(F32).reshape(outer, LANES)
        total = taps[s][0] * x
        for j in range(1, 3):
            turned = pltpu.roll(x, j, 1)
            before = jnp.where(line == 0, 0.0, pltpu.roll(turned, 1, 0))
            moved = jnp.where(lane < j, before, turned)
            shifts[s, j - 1] = moved
            total = total + taps[s][j] * moved
        mixed.append(total)
    kv[0] = mixed[1]
    kv[1] = mixed[2]
    gated = mixed[1] * mixed[2]
    grad_conv = raw[:, :, 3].astype(F32).reshape(outer, LANES) * mixed[0]

    def forward(values, slots):
        right = split(jnp.concatenate(values, 1) if len(values) > 1 else values[0])
        step = half // 4
        for first in range(0, half, step):
            ours = slice(first, first + step)
            rows = (ours, slice(half + first, half + first + step))
            left = [jnp.concatenate([f1[part, r, :] for r in rows], 0) for part in range(2)]
            u = dot3(left, right)
            for at, s in enumerate(slots):
                ur = u[:step, at * LANES : (at + 1) * LANES]
                ui = u[step:, at * LANES : (at + 1) * LANES]
                tr, ti = tw[0, ours, :], tw[1, ours, :]
                v = jnp.concatenate([ur * tr - ui * ti, ur * ti + ui * tr], 1)
                spec[s, ours, :] = dot3(split(v), (f2[0], f2[1]))

    def parts(s):
        return spec[s, :, :LANES], spec[s, :, LANES:]

    def inverse_rows(re, im):
        z = dot3(split(jnp.concatenate([re, im], 1)), (f2t[0], f2t[1]))
        zr, zi = z[:, :LANES], z[:, LANES:]
        return jnp.concatenate([zr * tw[0] + zi * tw[1], zi * tw[0] - zr * tw[1]], 0)

    mine = pl.ds(pl.multiple_of(core * (half - EXTRA), ROWS), local)

    def finish(slots, columns, exchange):
        right = split(jnp.concatenate(columns, 1) if len(columns) > 1 else columns[0])
        for own in (False, True):
            rows = slice(local, 2 * local) if own else slice(0, local)
            y = dot3((f1t[0, rows, :], f1t[1, rows, :]), right)
            for at, s in enumerate(slots):
                (yown if own else ybuf)[s] = y[:, at * LANES : (at + 1) * LANES]
            if not own:
                exchange.start()

    def swap(lo, hi, slot):
        return remote(
            ybuf.at[lo:hi], xb.at[lo:hi], x_send.at[slot], x_recv.at[slot], {"seq": sib}
        )

    forward([gated, grad_conv], [1, 2])
    gr, gi = parts(1)
    dr, di = parts(2)
    swap_k = swap(0, 1, 0)
    finish([0], [inverse_rows(dr * gr + di * gi, di * gr - dr * gi)], swap_k)

    is_local = lax.div(me, chips) == core

    def send_half(src, dst, slot, first, end):
        at = lax.rem(me, chips)

        def one(r, carry):
            d = lax.rem(at + r, chips)
            device = {"seq": core * chips + d}
            remote(src.at[d], dst.at[q], ret_send.at[slot], ret_recv.at[slot], device).start()
            return carry

        lax.fori_loop(max(first, 1), end, one, 0)
        if first == 0:

            @pl.when(is_local)
            def _():
                pltpu.make_async_copy(src.at[at], dst.at[q], ret_recv.at[slot]).start()

            @pl.when(jnp.logical_not(is_local))
            def _():
                one(0, 0)

    swap_k.wait()
    own_rows = pl.ds(pl.multiple_of(core * EXTRA, ROWS), half)
    kg = (yown[0, own_rows, :] + xb[0, own_rows, :]) * (1.0 / length)
    kg_send[...] = kg.reshape(kg_send.shape)

    def kg_push(d):
        device = {"seq": core * chips + d}
        remote(kg_send.at[d], kg_ret.at[q], ret_send.at[0], ret_recv.at[0], device).start()

    def kg_blocks(k):
        z = lax.rem(zi + ring_offset(k), Z_SIZE)
        return [x * 2 * Z_SIZE + 2 * z + c for x in range(x_size // 2) for c in range(2)]

    def kg_far(k, carry):
        for d in kg_blocks(k):
            kg_push(d)
        return carry

    lax.fori_loop(0, Z_SIZE - 1, kg_far, 0)
    for d in kg_blocks(jnp.int32(Z_SIZE - 1)):
        is_me = core * chips + d == me

        @pl.when(is_me)
        def _():
            pltpu.make_async_copy(kg_send.at[d], kg_ret.at[q], ret_recv.at[0]).start()

        @pl.when(jnp.logical_not(is_me))
        def _():
            kg_push(d)


    wait_bytes(k_send.at[pl.ds(0, (chips - 1) * ROWS)], in_recv.at[1])
    sib_k = remote(kbuf.at[:, core], kbuf.at[:, core], sib_send.at[1], sib_recv.at[1], {"seq": sib})
    sib_k.start()

    sib_k.wait()
    forward([kbuf[...].reshape(outer, LANES)], [0])
    kr, ki = parts(0)
    swap_c = swap(1, 3, 1)
    finish(
        [1, 2],
        [
            inverse_rows(gr * kr - gi * ki, gr * ki + gi * kr),
            inverse_rows(dr * kr + di * ki, di * kr - dr * ki),
        ],
        swap_c,
    )
    swap_c.wait()

    conv_out = (yown[1] + xb[1]) * (1.0 / length)
    grad_gated = (yown[2] + xb[2]) * (1.0 / length)
    lane = lax.broadcasted_iota(jnp.int32, (local, LANES), 1)
    line = lax.broadcasted_iota(jnp.int32, (local, LANES), 0)
    is_mine = (line >= core * EXTRA) & (line < core * EXTRA + half)
    cot_all = raw[:, :, 3].astype(F32).reshape(outer, LANES)
    gp32[0:outer, :] = cot_all
    cot_mine = gp32[mine, :]
    grad_mixed = [cot_mine * conv_out, grad_gated * kv[1, mine, :], grad_gated * kv[0, mine, :]]
    for s in range(3):
        g = grad_mixed[s]
        total = taps[s][0] * g
        for j in range(1, 3):
            turned = pltpu.roll(g, LANES - j, 1)
            after = jnp.where(line == local - 1, 0.0, pltpu.roll(turned, local - 1, 0))
            total = total + taps[s][j] * jnp.where(lane >= LANES - j, after, turned)
        res[s] = total
        gp_send[:, s] = res[s, own_rows, :].reshape(chips, ROWS, LANES).astype(BF16)
    send_half(gp_send, gp_ret, 1, 0, chips // 2)

    wait_bytes(kg_send, ret_recv.at[0])
    weighted = env[...] * jnp.concatenate(
        [
            jnp.concatenate(
                [
                    kg_ret.at[pl.ds(cb * 8, 8)][:, j, :] for j in range(ROWS)
                ], 1,
            )
            for cb in range(blocks)
        ], 0,
    )
    pair = split(weighted)
    out_part = dot3(pair, (hid2[0], hid2[1]), 1, 1)
    grad_hidden = dot3(split(fout[...]), pair, 0, 0) * hcos[...]
    in_part = dot3((feat2[0], feat2[1]), split(grad_hidden), 1, 1)
    for half_at in range(2):
        for at, part in enumerate((out_part, in_part)):
            first = half_at * (channels // 2)
            middle, end = first + channels // 4, first + channels // 2
            r_own[half_at, at] = jnp.concatenate([part[first:middle], part[middle:end]], 1)
    red_core = remote(r_own.at[1 - core], r_sib, red_send.at[0], red_recv.at[0], {"seq": sib})
    red_core.start()
    lane1 = lax.broadcasted_iota(jnp.int32, (1, LANES), 1)
    short = jnp.zeros((1, LANES), F32)
    for s in range(3):
        g = jnp.where(is_mine, grad_mixed[s], 0.0)
        gp32[0:outer, :] = raw[:, :, s].astype(F32).reshape(outer, LANES)
        for j in range(3):
            x = gp32[mine, :] if j == 0 else shifts[s, j - 1, mine, :]
            total = jnp.sum(jnp.sum(g * x, axis=0, keepdims=True), axis=1, keepdims=True)
            short = jnp.where(lane1 == s * 3 + j, total, short)
    s_own[...] = short
    sib_short = remote(s_own, s_sib, sib_send.at[2], sib_recv.at[2], {"seq": sib})
    sib_short.start()

    red_core.wait()
    r_z[zi] = r_own[core] + r_sib[...]

    for dz in (4, 3, 5, 2, 6, 1, 7):
        device = seq_dev(xi * Z_SIZE + lax.rem(zi + dz, Z_SIZE))
        remote(r_z.at[zi], r_z.at[zi], red_send.at[1], red_recv.at[1], device).start()

    sib_short.wait()
    s_all[q] = s_own[...] + s_sib[...]
    to_chips(
        lambda chip: remote(s_all.at[q], s_all.at[q], red_send.at[4], red_recv.at[4], seq_dev(chip)).start()
    )
    send_half(gp_send, gp_ret, 1, chips // 2, chips)

    z_rest = r_z.at[pl.ds(0, Z_SIZE - 1)]
    wait_bytes(z_rest, red_recv.at[1])
    total = r_z[0]
    for i in range(1, Z_SIZE):
        total = total + r_z[i]
    here = xi * y_size + yi
    r_x[core, xi] = total[0]
    r_xy[core, here] = total[1]

    def around(dx, dy, other):
        x = lax.rem(xi + dx, x_size)
        return {"ch": lax.rem(yi + dy, y_size), "seq": 2 * (x * Z_SIZE + zi) + (1 - core if other else core)}

    def sum_in(dx, dy, other):
        remote(
            r_xy.at[core, here], r_xy.at[core, here], red_send.at[2], red_recv.at[2], around(dx, dy, other)
        ).start()

    def sum_in_far(k, carry):
        dx = 2 + jnp.where(k == 0, 0, jnp.where(k == 1, -1, 1))
        for other in (True, False):
            for dy in (2, 1, 3, 0):
                sum_in(dx, dy, other)
        return carry

    lax.fori_loop(0, x_size - 1, sum_in_far, 0)
    for dy, other in ((2, True), (2, False), (1, True), (3, True), (1, False), (3, False), (0, True)):
        sum_in(0, dy, other)
    for dx, other in ((2, True), (2, False), (1, True), (3, True), (1, False), (3, False), (0, True)):
        remote(
            r_x.at[core, xi], r_x.at[core, xi], red_send.at[3], red_recv.at[3], around(dx, 0, other)
        ).start()

    wait_bytes(gp_send, ret_recv.at[1])
    gp32[...] = gp_ret[...].astype(F32).reshape(gp32.shape)
    for s in range(3):
        for cb in range(blocks):
            for j in range(ROWS):
                rows = pl.ds(cb * 8 * 3 * ROWS + s * ROWS + j, 8, stride=3 * ROWS)
                gp[s, cb * 8 : cb * 8 + 8, j * LANES : (j + 1) * LANES] = gp32[rows, :].astype(BF16)

    scale = 1.0 / math.sqrt(length)
    wait_bytes(s_all.at[pl.ds(0, chips - 1)], red_recv.at[4])
    shorts = s_all[...].reshape(channels, LANES) * scale
    for at in range(9):
        short_rows[at // 3, at % 3 : at % 3 + 1, :] = as_row(shorts[:, at : at + 1])

    group = 2 * x_size * y_size
    wait_bytes(gp32.at[pl.ds(0, (2 * x_size - 1) * (channels // 4))], red_recv.at[3])
    wait_bytes(gp32.at[pl.ds(0, (group - 1) * (channels // 4))], red_recv.at[2])
    for half_at in range(2):
        out_total = r_x[half_at, 0]
        for x in range(1, x_size):
            out_total = out_total + r_x[half_at, x]
        in_total = r_xy[half_at, 0]
        for at in range(1, x_size * y_size):
            in_total = in_total + r_xy[half_at, at]
        first = half_at * (channels // 2)
        middle, end = first + channels // 4, first + channels // 2
        for out, part in ((fout_out, out_total * scale), (fin_out, in_total * scale)):
            out[first:middle, :] = part[:, :units]
            out[middle:end, :] = part[:, units:]

    wait_bytes(raw_send.at[pl.ds(0, chips - 1)], in_send.at[0])
    wait_bytes(k_send.at[pl.ds(0, (chips - 1) * ROWS)], in_send.at[1])
    for slot, buf in ((0, kg_send), (1, gp_send)):
        wait_bytes(buf.at[pl.ds(0, chips - 1)], ret_send.at[slot])

        @pl.when(jnp.logical_not(is_local))
        def _():
            wait_bytes(buf.at[0], ret_send.at[slot])

    wait_bytes(raw_send, sib_send.at[0])
    wait_bytes(z_rest, red_send.at[1])
    wait_bytes(gp32.at[pl.ds(0, (2 * x_size - 1) * (channels // 4))], red_send.at[3])
    wait_bytes(gp32.at[pl.ds(0, (group - 1) * (channels // 4))], red_send.at[2])
    wait_bytes(s_all.at[pl.ds(0, chips - 1)], red_send.at[4])


def move_outputs(*refs):
    count = (len(refs) - 1) // 2
    copies = [pltpu.make_async_copy(refs[i], refs[count + i], refs[-1].at[i]) for i in range(count)]
    for copy in copies:
        copy.start()
    for copy in copies:
        copy.wait()


def shards(devices, y_size, tables, proj, cotangent, short_w, filter_in, filter_out, rates):
    channels = cotangent.shape[0]
    feats, order = filter_in.shape
    chips = devices // 2
    outer = devices * ROWS
    half = outer // 2
    hbm = pl.BlockSpec(memory_space=pltpu.HBM)
    dma = pltpu.SemaphoreType.DMA

    def f32(*shape):
        return pltpu.VMEM(shape, F32)

    def bf16(*shape):
        return pltpu.VMEM(shape, BF16)

    operands = (
        proj, cotangent, short_w.transpose(0, 2, 1), filter_in, filter_out.T, rates.reshape(1, channels), *tables
    )
    shapes = (
        jax.ShapeDtypeStruct(proj.shape, BF16),
        jax.ShapeDtypeStruct((3, 3, channels), F32),
        jax.ShapeDtypeStruct((channels, order), F32),
        jax.ShapeDtypeStruct((feats, order), F32),
    )
    results = pl.pallas_call(
        functools.partial(kernel, devices, y_size),
        out_shape=shapes,
        in_specs=[hbm] * 11,
        out_specs=(pl.BlockSpec(memory_space=pltpu.VMEM),) * 4,
        scratch_shapes=[
            bf16(*proj.shape),
            bf16(*cotangent.shape),
            f32(3, 3, channels),
            f32(feats, order),
            f32(channels, order),
            f32(1, channels),
            bf16(2, outer, outer),
            bf16(2, outer + 2 * EXTRA, outer),
            f32(2, half, LANES),
            bf16(2, 2 * LANES, 2 * LANES),
            bf16(2, 2 * LANES, 2 * LANES),
            f32(feats, TOKENS),
            f32(order, TOKENS),
            f32(channels, TOKENS),
            f32(chips * 4 * ROWS, LANES),
            bf16(chips, 4, ROWS, LANES),
            bf16(chips, 2, 4, ROWS, LANES),
            f32(chips * ROWS, LANES),
            f32(chips, 2, ROWS, LANES),
            f32(3, 2, outer, LANES),
            f32(2, outer, LANES),
            f32(3, half, 2 * LANES),
            f32(3, half + EXTRA, LANES),
            f32(3, half + EXTRA, LANES),
            f32(3, half + EXTRA, LANES),
            f32(chips, ROWS, LANES),
            f32(chips, ROWS, LANES),
            f32(3, half + EXTRA, LANES),
            bf16(chips, 3, ROWS, LANES),
            bf16(chips, 3, ROWS, LANES),
            f32(chips * 3 * ROWS, LANES),
            bf16(2, order, TOKENS),
            bf16(2, feats, TOKENS),
            f32(2, 2, channels // 4, LANES),
            f32(2, channels // 4, LANES),
            f32(Z_SIZE, 2, channels // 4, LANES),
            f32(2, chips // Z_SIZE, channels // 4, LANES),
            f32(2, chips // Z_SIZE * y_size, channels // 4, LANES),
            f32(1, LANES),
            f32(1, LANES),
            f32(chips, 1, LANES),
            dma((11,)), dma((2,)), dma((2,)), dma((chips,)), dma((3,)), dma((3,)), dma((2,)), dma((2,)),
            dma((2,)), dma((2,)), dma((5,)), dma((5,)),
        ],
        compiler_params=pltpu.CompilerParams(
            collective_id=0, has_side_effects=True, vmem_limit_bytes=32 << 20
        ),
    )(*[pltpu.with_memory_space_constraint(x, pltpu.HBM) for x in operands])
    grad_proj, grad_short, grad_out, grad_in = pl.pallas_call(
        move_outputs,
        out_shape=shapes,
        in_specs=[pl.BlockSpec(memory_space=pl.ANY)] * 4,
        out_specs=(hbm,) * 4,
        scratch_shapes=[dma((4,))],
        compiler_params=pltpu.CompilerParams(vmem_limit_bytes=1 << 20),
    )(*results)
    return grad_proj, grad_short.transpose(0, 2, 1), grad_out.T, grad_in


def solution(mesh):
    devices, y_size = mesh.shape["seq"], mesh.shape["ch"]
    tables = make_tables(devices)

    def run(*args):
        return shards(devices, y_size, [jnp.asarray(t) for t in tables], *args)

    return jax.shard_map(
        run,
        mesh=mesh,
        in_specs=(
            P(None, "ch", "seq"),
            P("ch", "seq"),
            P(None, "ch", None),
            P(),
            P(None, "ch"),
            P("ch"),
        ),
        out_specs=(P(None, "ch", "seq"), P(None, "ch", None), P(None, "ch"), P()),
        check_vma=False,
    )
```

```python
import functools
import math

import jax
import jax.numpy as jnp
import ml_dtypes
import numpy as np
from jax import lax
from jax.experimental import pallas as pl
from jax.experimental.pallas import tpu as pltpu
from jax.sharding import PartitionSpec as P

MESH = pl.DeviceIdType.MESH
F32 = jnp.float32
BF16 = jnp.bfloat16
PRECISE = lax.Precision.HIGHEST
LANES = 128
ROWS = 8
TOKENS = ROWS * LANES
Z_SIZE = 8
EXTRA = 16


def bf16_pair(table):
    high = table.astype(ml_dtypes.bfloat16)
    low = (table - high.astype(np.float64)).astype(ml_dtypes.bfloat16)
    return np.stack([high, low])


def make_tables(devices):
    outer = devices * ROWS
    length = outer * LANES
    half = outer // 2
    a = np.arange(outer)
    fwd, back, twiddle = [], [], []
    for core in range(2):
        k1 = core * half + np.arange(half)
        num = (a[None, :] * (4 * k1[:, None] + 1)) % (4 * outer)
        angle = num * (2.0 * np.pi / (4 * outer))
        matrix = np.concatenate([np.cos(angle), -np.sin(angle)], 0)
        fwd.append(bf16_pair(matrix))
        starts = [(1 - core) * (half - EXTRA), core * (half - EXTRA)]
        rows = np.concatenate([start + np.arange(half + EXTRA) for start in starts])
        back.append(bf16_pair(np.ascontiguousarray(matrix.T[rows])))
        num = (np.arange(LANES)[None, :] * (4 * k1[:, None] + 1)) % (4 * length)
        angle = num * (2.0 * np.pi / (4 * length))
        twiddle.append(np.stack([np.cos(angle), -np.sin(angle)]).astype(np.float32))
    b = np.arange(LANES)
    angle = (b[:, None] * b[None, :] % LANES) * (2.0 * np.pi / LANES)
    c, s = np.cos(angle), np.sin(angle)
    inner = np.block([[c, -s], [s, c]])
    return (
        np.stack(fwd),
        np.stack(back),
        np.stack(twiddle),
        bf16_pair(inner),
        bf16_pair(np.ascontiguousarray(inner.T)),
    )


def sin_small(x):
    y = x * x
    p = 1.0 / 6227020800.0
    p = p * y - 1.0 / 39916800.0
    p = p * y + 1.0 / 362880.0
    p = p * y - 1.0 / 5040.0
    p = p * y + 1.0 / 120.0
    p = p * y - 1.0 / 6.0
    return x + x * y * p


def minus_pi_times(x, n):
    return ((x - n * 3.140625) - n * 9.67502593994140625e-4) - n * 1.509957990978376e-7


def parity_sign(n):
    return 1.0 - 2.0 * (n - 2.0 * jnp.floor(n * 0.5))


def sin_cos(x):
    scaled = x * (1.0 / math.pi)
    n = jnp.floor(scaled + 0.5)
    sine = parity_sign(n) * sin_small(minus_pi_times(x, n))
    m = jnp.floor(scaled) + 1.0
    cosine = parity_sign(m) * sin_small(minus_pi_times(x, m - 0.5))
    return sine, cosine


def diagonal(n):
    return lax.broadcasted_iota(jnp.int32, (n, n), 0) == lax.broadcasted_iota(jnp.int32, (n, n), 1)


def column(row):
    return jnp.sum(jnp.where(diagonal(row.shape[1]), row, 0.0), axis=1, keepdims=True)


def as_row(col):
    return jnp.sum(jnp.where(diagonal(col.shape[0]), col, 0.0), axis=0, keepdims=True)


def inverse_spread(rate, length):
    y = rate * (2.0 / length)
    p = 1.0 / 5040.0
    for k in (720.0, 120.0, 24.0, 6.0, 2.0, 1.0):
        p = 1.0 / k - y * p
    return jnp.sqrt(y * p / (1.0 - jnp.exp(-2.0 * rate)))


def split(x):
    high = x.astype(BF16)
    return high, (x - high.astype(F32)).astype(BF16)


def dot_one(a, b, da=1, db=0):
    return lax.dot_general(a, b, (((da,), (db,)), ((), ())), preferred_element_type=F32)


def dot3(a, b, da=1, db=0):
    return dot_one(
        jnp.concatenate([a[0], a[0], a[1]], da), jnp.concatenate([b[0], b[1], b[0]], db), da, db
    )


def dot_exact(a, b, dims):
    return lax.dot_general(a, b, (dims, ((), ())), precision=PRECISE, preferred_element_type=F32)


def kernel(
    devices, y_size,
    proj_hbm, cot_hbm, sw_hbm, fin_hbm, fout_hbm, rates_hbm, f1_hbm, f1t_hbm, tw_hbm, f2_hbm, f2t_hbm,
    gp, short_rows, fout_out, fin_out,
    proj, cot, sw, fin, fout, rates, f1, f1t, tw, f2, f2t,
    feat, hcos, env, raw32, raw_send, raw, k_send, kbuf, shifts, kv, spec, ybuf, yown, xb, kg_send, kg_ret,
    res, gp_send, gp_ret, gp32, hid2, feat2, r_own, r_sib, r_z, r_x, r_xy, s_own, s_sib, s_all,
    load_sem, in_send, in_recv, raw_recv, sib_send, sib_recv, x_send, x_recv, ret_send, ret_recv,
    red_send, red_recv,
):
    chips = devices // 2
    channels = cot.shape[0]
    length = devices * TOKENS
    outer = devices * ROWS
    half = outer // 2
    local = half + EXTRA
    blocks = channels // 8
    units = hcos.shape[0]
    me = lax.axis_index("seq")
    yi = lax.axis_index("ch")
    q = lax.div(me, 2)
    core = lax.rem(me, 2)
    sib = me + 1 - 2 * core

    def seq_dev(chip):
        return {"seq": 2 * chip + core}

    barrier = pltpu.get_barrier_semaphore()

    order = (3, 4, 0, 1, 2, 5, 6, 7, 8, 9, 10)
    moves = (
        (fin_hbm, fin), (rates_hbm, rates), (fout_hbm, fout), (proj_hbm, proj), (cot_hbm, cot), (sw_hbm, sw),
        (f1_hbm.at[core], f1), (tw_hbm.at[core], tw), (f2_hbm, f2), (f2t_hbm, f2t), (f1t_hbm.at[core], f1t),
    )
    loads = [pltpu.make_async_copy(src, dst, load_sem.at[i]) for i, (src, dst) in enumerate(moves)]
    x_size = chips // Z_SIZE
    xi = lax.div(q, Z_SIZE)
    zi = lax.rem(q, Z_SIZE)

    def around(dx, dy, other):
        x = lax.rem(xi + dx, x_size)
        return {"ch": lax.rem(yi + dy, y_size), "seq": 2 * (x * Z_SIZE + zi) + (1 - core if other else core)}

    def ring_offset(k):
        return Z_SIZE // 2 + jnp.where(lax.rem(k, 2) == 1, -lax.div(k + 1, 2), lax.div(k, 2))

    def over_group(act):
        def far(k, carry):
            dx = 2 + jnp.where(k == 0, 0, jnp.where(k == 1, -1, 1))
            for other in (True, False):
                for dy in (2, 1, 3, 0):
                    act(dx, dy, other)
            return carry

        lax.fori_loop(0, x_size - 1, far, 0)
        for dy, other in ((2, True), (2, False), (1, True), (3, True), (1, False), (3, False), (0, True)):
            act(0, dy, other)

    def greet_far(k, carry):
        z = lax.rem(zi + ring_offset(k), Z_SIZE)
        for dx in (2, 1, 3, 0):
            chip = lax.rem(xi + dx, x_size) * Z_SIZE + z
            pl.semaphore_signal(barrier, inc=1, device_id=seq_dev(chip), device_id_type=MESH)
        return carry

    for i in order[:2]:
        loads[i].start()
    lax.fori_loop(0, Z_SIZE - 1, greet_far, 0)
    for dx in range(1, x_size):
        chip = lax.rem(xi + dx, x_size) * Z_SIZE + zi
        pl.semaphore_signal(barrier, inc=1, device_id=seq_dev(chip), device_id_type=MESH)
    over_group(
        lambda dx, dy, other: pl.semaphore_signal(
            barrier, inc=1, device_id=around(dx, dy, other), device_id_type=MESH
        )
    )
    for i in order[2:]:
        loads[i].start()

    def remote(src, dst, send_sem, recv_sem, device):
        return pltpu.make_async_remote_copy(
            src, dst, send_sem, recv_sem, device_id=device, device_id_type=MESH
        )

    def wait_bytes(part, sem):
        pltpu.make_async_copy(part, part, sem).wait()

    for copy in loads[3:5]:
        copy.wait()

    for s in range(4):
        value = cot[...].astype(F32) if s == 3 else proj[s].astype(F32)
        for cb in range(blocks):
            for j in range(ROWS):
                rows = pl.ds(cb * 8 * 4 * ROWS + s * ROWS + j, 8, stride=4 * ROWS)
                raw32[rows, :] = value[cb * 8 : cb * 8 + 8, j * LANES : (j + 1) * LANES]
    raw_send[...] = raw32[...].reshape(raw_send.shape).astype(BF16)

    pl.semaphore_wait(barrier, chips - 1 + 2 * x_size * y_size - 1)

    def rows_of(chip):
        return pl.ds(pl.multiple_of(chip * ROWS, ROWS), ROWS)

    def to_chips(start):
        def far(k, carry):
            z = lax.rem(zi + ring_offset(k), Z_SIZE)
            for dx in (2, 1, 3, 0):
                start(lax.rem(xi + dx, x_size) * Z_SIZE + z)
            return carry

        lax.fori_loop(0, Z_SIZE - 1, far, 0)
        for dx in (2, 1, 3):
            start(lax.rem(xi + dx, x_size) * Z_SIZE + zi)

    def send_raw(chip):
        remote(raw_send.at[chip], raw.at[q, core], in_send.at[0], raw_recv.at[q], seq_dev(chip)).start()

    to_chips(send_raw)
    raw[q, core] = raw_send[q]

    row = lax.broadcasted_iota(jnp.int32, feat.shape, 0)
    position = me * TOKENS + lax.broadcasted_iota(jnp.int32, feat.shape, 1)
    odd = row & 1
    phase = position * (1 + (row >> 1) * 499) - odd * (length // 4) + length // 2
    phase = (phase & (length - 1)) - length // 2
    feat[...] = sin_small((length // 4 - jnp.abs(phase)).astype(F32) * (2.0 * math.pi / length))
    for copy in loads[:3]:
        copy.wait()

    preact = dot_exact(fin[...], feat[...], ((0,), (0,)))
    sine, cosine = sin_cos(preact)
    hid2[0], hid2[1] = split(sine)
    feat2[0], feat2[1] = split(feat[...])
    hcos[...] = cosine
    relative = (me * TOKENS + lax.broadcasted_iota(jnp.int32, env.shape, 1)).astype(F32) * (1.0 / length)
    rate = column(rates[...])
    env[...] = jnp.exp(-rate * relative) * inverse_spread(rate, length)
    filt = env[...] * dot3(split(fout[...]), (hid2[0], hid2[1]))
    for cb in range(blocks):
        for j in range(ROWS):
            k_send[pl.ds(cb * 64 + j, 8, stride=8), :] = filt[cb * 8 : cb * 8 + 8, j * LANES : (j + 1) * LANES]

    for copy in loads[5:]:
        copy.wait()
    lane9 = lax.broadcasted_iota(jnp.int32, (1, channels), 1)
    taps = [
        [jnp.sum(jnp.where(lane9 == q, sw[s, j : j + 1, :], 0.0), axis=1, keepdims=True) for j in range(3)]
        for s in range(3)
    ]

    def hand_on(chip):
        remote(raw.at[chip, core], raw.at[chip, core], sib_send.at[0], sib_recv.at[0], {"seq": sib}).start()

    def arrived(chip):
        pltpu.make_async_copy(raw.at[chip, core], raw.at[chip, core], raw_recv.at[chip]).wait()
        hand_on(chip)

    def arrived_far(k, carry):
        z = lax.rem(zi + Z_SIZE - ring_offset(k), Z_SIZE)
        for dx in (2, 3, 1, 0):
            arrived(lax.rem(xi + dx, x_size) * Z_SIZE + z)
        return carry

    hand_on(q)
    lax.fori_loop(0, Z_SIZE - 2, arrived_far, 0)
    to_chips(
        lambda chip: remote(
            k_send.at[rows_of(chip)], kbuf.at[q, core], in_send.at[1], in_recv.at[1], seq_dev(chip)
        ).start()
    )
    kbuf[q, core] = k_send[rows_of(q)]
    lax.fori_loop(Z_SIZE - 2, Z_SIZE - 1, arrived_far, 0)
    for dx in (2, 3, 1):
        arrived(lax.rem(xi + dx, x_size) * Z_SIZE + zi)
    wait_bytes(raw_send, sib_recv.at[0])

    lane = lax.broadcasted_iota(jnp.int32, (outer, LANES), 1)
    line = lax.broadcasted_iota(jnp.int32, (outer, LANES), 0)
    mixed = []
    for s in range(3):
        x = raw[:, :, s].astype(F32).reshape(outer, LANES)
        total = taps[s][0] * x
        for j in range(1, 3):
            turned = pltpu.roll(x, j, 1)
            before = jnp.where(line == 0, 0.0, pltpu.roll(turned, 1, 0))
            moved = jnp.where(lane < j, before, turned)
            shifts[s, j - 1] = moved
            total = total + taps[s][j] * moved
        mixed.append(total)
    kv[0] = mixed[1]
    kv[1] = mixed[2]
    gated = mixed[1] * mixed[2]
    grad_conv = raw[:, :, 3].astype(F32).reshape(outer, LANES) * mixed[0]

    def forward(values, slots):
        right = split(jnp.concatenate(values, 1) if len(values) > 1 else values[0])
        step = half // 4
        for first in range(0, half, step):
            ours = slice(first, first + step)
            rows = (ours, slice(half + first, half + first + step))
            left = [jnp.concatenate([f1[part, r, :] for r in rows], 0) for part in range(2)]
            u = dot3(left, right)
            for at, s in enumerate(slots):
                ur = u[:step, at * LANES : (at + 1) * LANES]
                ui = u[step:, at * LANES : (at + 1) * LANES]
                tr, ti = tw[0, ours, :], tw[1, ours, :]
                v = jnp.concatenate([ur * tr - ui * ti, ur * ti + ui * tr], 1)
                spec[s, ours, :] = dot3(split(v), (f2[0], f2[1]))

    def parts(s):
        return spec[s, :, :LANES], spec[s, :, LANES:]

    def inverse_rows(re, im):
        z = dot3(split(jnp.concatenate([re, im], 1)), (f2t[0], f2t[1]))
        zr, zi = z[:, :LANES], z[:, LANES:]
        return jnp.concatenate([zr * tw[0] + zi * tw[1], zi * tw[0] - zr * tw[1]], 0)

    mine = pl.ds(pl.multiple_of(core * (half - EXTRA), ROWS), local)

    def finish(slots, columns, exchange):
        right = split(jnp.concatenate(columns, 1) if len(columns) > 1 else columns[0])
        for own in (False, True):
            rows = slice(local, 2 * local) if own else slice(0, local)
            y = dot3((f1t[0, rows, :], f1t[1, rows, :]), right)
            for at, s in enumerate(slots):
                (yown if own else ybuf)[s] = y[:, at * LANES : (at + 1) * LANES]
            if not own:
                exchange.start()

    def swap(lo, hi, slot):
        return remote(
            ybuf.at[lo:hi], xb.at[lo:hi], x_send.at[slot], x_recv.at[slot], {"seq": sib}
        )

    forward([gated, grad_conv], [1, 2])
    gr, gi = parts(1)
    dr, di = parts(2)
    swap_k = swap(0, 1, 0)
    finish([0], [inverse_rows(dr * gr + di * gi, di * gr - dr * gi)], swap_k)

    is_local = lax.div(me, chips) == core

    def send_half(src, dst, slot, first, end):
        at = lax.rem(me, chips)

        def one(r, carry):
            d = lax.rem(at + r, chips)
            device = {"seq": core * chips + d}
            remote(src.at[d], dst.at[q], ret_send.at[slot], ret_recv.at[slot], device).start()
            return carry

        lax.fori_loop(max(first, 1), end, one, 0)
        if first == 0:

            @pl.when(is_local)
            def _():
                pltpu.make_async_copy(src.at[at], dst.at[q], ret_recv.at[slot]).start()

            @pl.when(jnp.logical_not(is_local))
            def _():
                one(0, 0)

    swap_k.wait()
    own_rows = pl.ds(pl.multiple_of(core * EXTRA, ROWS), half)
    kg = (yown[0, own_rows, :] + xb[0, own_rows, :]) * (1.0 / length)
    kg_send[...] = kg.reshape(kg_send.shape)

    def kg_push(d):
        device = {"seq": core * chips + d}
        remote(kg_send.at[d], kg_ret.at[q], ret_send.at[0], ret_recv.at[0], device).start()

    def kg_blocks(k):
        z = lax.rem(zi + ring_offset(k), Z_SIZE)
        return [x * 2 * Z_SIZE + 2 * z + c for x in range(x_size // 2) for c in range(2)]

    def kg_far(k, carry):
        for d in kg_blocks(k):
            kg_push(d)
        return carry

    lax.fori_loop(0, Z_SIZE - 1, kg_far, 0)
    for d in kg_blocks(jnp.int32(Z_SIZE - 1)):
        is_me = core * chips + d == me

        @pl.when(is_me)
        def _():
            pltpu.make_async_copy(kg_send.at[d], kg_ret.at[q], ret_recv.at[0]).start()

        @pl.when(jnp.logical_not(is_me))
        def _():
            kg_push(d)


    wait_bytes(k_send.at[pl.ds(0, (chips - 1) * ROWS)], in_recv.at[1])
    sib_k = remote(kbuf.at[:, core], kbuf.at[:, core], sib_send.at[1], sib_recv.at[1], {"seq": sib})
    sib_k.start()

    sib_k.wait()
    forward([kbuf[...].reshape(outer, LANES)], [0])
    kr, ki = parts(0)
    swap_c = swap(1, 3, 1)
    finish(
        [1, 2],
        [
            inverse_rows(gr * kr - gi * ki, gr * ki + gi * kr),
            inverse_rows(dr * kr + di * ki, di * kr - dr * ki),
        ],
        swap_c,
    )
    swap_c.wait()

    conv_out = (yown[1] + xb[1]) * (1.0 / length)
    grad_gated = (yown[2] + xb[2]) * (1.0 / length)
    lane = lax.broadcasted_iota(jnp.int32, (local, LANES), 1)
    line = lax.broadcasted_iota(jnp.int32, (local, LANES), 0)
    is_mine = (line >= core * EXTRA) & (line < core * EXTRA + half)
    cot_all = raw[:, :, 3].astype(F32).reshape(outer, LANES)
    gp32[0:outer, :] = cot_all
    cot_mine = gp32[mine, :]
    grad_mixed = [cot_mine * conv_out, grad_gated * kv[1, mine, :], grad_gated * kv[0, mine, :]]
    for s in range(3):
        g = grad_mixed[s]
        total = taps[s][0] * g
        for j in range(1, 3):
            turned = pltpu.roll(g, LANES - j, 1)
            after = jnp.where(line == local - 1, 0.0, pltpu.roll(turned, local - 1, 0))
            total = total + taps[s][j] * jnp.where(lane >= LANES - j, after, turned)
        res[s] = total
        gp_send[:, s] = res[s, own_rows, :].reshape(chips, ROWS, LANES).astype(BF16)
    send_half(gp_send, gp_ret, 1, 0, chips // 2)

    wait_bytes(kg_send, ret_recv.at[0])
    weighted = env[...] * jnp.concatenate(
        [
            jnp.concatenate(
                [
                    kg_ret.at[pl.ds(cb * 8, 8)][:, j, :] for j in range(ROWS)
                ], 1,
            )
            for cb in range(blocks)
        ], 0,
    )
    pair = split(weighted)
    out_part = dot3(pair, (hid2[0], hid2[1]), 1, 1)
    grad_hidden = dot3(split(fout[...]), pair, 0, 0) * hcos[...]
    in_part = dot3((feat2[0], feat2[1]), split(grad_hidden), 1, 1)
    for half_at in range(2):
        for at, part in enumerate((out_part, in_part)):
            first = half_at * (channels // 2)
            middle, end = first + channels // 4, first + channels // 2
            r_own[half_at, at] = jnp.concatenate([part[first:middle], part[middle:end]], 1)
    red_core = remote(r_own.at[1 - core], r_sib, red_send.at[0], red_recv.at[0], {"seq": sib})
    red_core.start()
    lane1 = lax.broadcasted_iota(jnp.int32, (1, LANES), 1)
    short = jnp.zeros((1, LANES), F32)
    for s in range(3):
        g = jnp.where(is_mine, grad_mixed[s], 0.0)
        gp32[0:outer, :] = raw[:, :, s].astype(F32).reshape(outer, LANES)
        for j in range(3):
            x = gp32[mine, :] if j == 0 else shifts[s, j - 1, mine, :]
            total = jnp.sum(jnp.sum(g * x, axis=0, keepdims=True), axis=1, keepdims=True)
            short = jnp.where(lane1 == s * 3 + j, total, short)
    s_own[...] = short
    sib_short = remote(s_own, s_sib, sib_send.at[2], sib_recv.at[2], {"seq": sib})
    sib_short.start()

    red_core.wait()
    r_z[zi] = r_own[core] + r_sib[...]

    for dz in (4, 3, 5, 2, 6, 1, 7):
        device = seq_dev(xi * Z_SIZE + lax.rem(zi + dz, Z_SIZE))
        remote(r_z.at[zi], r_z.at[zi], red_send.at[1], red_recv.at[1], device).start()

    sib_short.wait()
    s_all[q] = s_own[...] + s_sib[...]
    to_chips(
        lambda chip: remote(s_all.at[q], s_all.at[q], red_send.at[4], red_recv.at[4], seq_dev(chip)).start()
    )
    send_half(gp_send, gp_ret, 1, chips // 2, chips)

    z_rest = r_z.at[pl.ds(0, Z_SIZE - 1)]
    wait_bytes(z_rest, red_recv.at[1])
    total = r_z[0]
    for i in range(1, Z_SIZE):
        total = total + r_z[i]
    here = xi * y_size + yi
    r_x[core, xi] = total[0]
    r_xy[core, here] = total[1]

    def sum_in(dx, dy, other):
        remote(
            r_xy.at[core, here], r_xy.at[core, here], red_send.at[2], red_recv.at[2], around(dx, dy, other)
        ).start()

    over_group(sum_in)
    for dx, other in ((2, True), (2, False), (1, True), (3, True), (1, False), (3, False), (0, True)):
        remote(
            r_x.at[core, xi], r_x.at[core, xi], red_send.at[3], red_recv.at[3], around(dx, 0, other)
        ).start()

    wait_bytes(gp_send, ret_recv.at[1])
    gp32[...] = gp_ret[...].astype(F32).reshape(gp32.shape)
    for s in range(3):
        for cb in range(blocks):
            for j in range(ROWS):
                rows = pl.ds(cb * 8 * 3 * ROWS + s * ROWS + j, 8, stride=3 * ROWS)
                gp[s, cb * 8 : cb * 8 + 8, j * LANES : (j + 1) * LANES] = gp32[rows, :].astype(BF16)

    scale = 1.0 / math.sqrt(length)
    wait_bytes(s_all.at[pl.ds(0, chips - 1)], red_recv.at[4])
    shorts = s_all[...].reshape(channels, LANES) * scale
    for at in range(9):
        short_rows[at // 3, at % 3 : at % 3 + 1, :] = as_row(shorts[:, at : at + 1])

    group = 2 * x_size * y_size
    wait_bytes(gp32.at[pl.ds(0, (2 * x_size - 1) * (channels // 4))], red_recv.at[3])
    wait_bytes(gp32.at[pl.ds(0, (group - 1) * (channels // 4))], red_recv.at[2])
    for half_at in range(2):
        out_total = r_x[half_at, 0]
        for x in range(1, x_size):
            out_total = out_total + r_x[half_at, x]
        in_total = r_xy[half_at, 0]
        for at in range(1, x_size * y_size):
            in_total = in_total + r_xy[half_at, at]
        first = half_at * (channels // 2)
        middle, end = first + channels // 4, first + channels // 2
        for out, part in ((fout_out, out_total * scale), (fin_out, in_total * scale)):
            out[first:middle, :] = part[:, :units]
            out[middle:end, :] = part[:, units:]

    wait_bytes(raw_send.at[pl.ds(0, chips - 1)], in_send.at[0])
    wait_bytes(k_send.at[pl.ds(0, (chips - 1) * ROWS)], in_send.at[1])
    for slot, buf in ((0, kg_send), (1, gp_send)):
        wait_bytes(buf.at[pl.ds(0, chips - 1)], ret_send.at[slot])

        @pl.when(jnp.logical_not(is_local))
        def _():
            wait_bytes(buf.at[0], ret_send.at[slot])

    wait_bytes(raw_send, sib_send.at[0])
    wait_bytes(z_rest, red_send.at[1])
    wait_bytes(gp32.at[pl.ds(0, (2 * x_size - 1) * (channels // 4))], red_send.at[3])
    wait_bytes(gp32.at[pl.ds(0, (group - 1) * (channels // 4))], red_send.at[2])
    wait_bytes(s_all.at[pl.ds(0, chips - 1)], red_send.at[4])


def move_outputs(*refs):
    count = (len(refs) - 1) // 2
    copies = [pltpu.make_async_copy(refs[i], refs[count + i], refs[-1].at[i]) for i in range(count)]
    for copy in copies:
        copy.start()
    for copy in copies:
        copy.wait()


def shards(devices, y_size, tables, proj, cotangent, short_w, filter_in, filter_out, rates):
    channels = cotangent.shape[0]
    feats, order = filter_in.shape
    chips = devices // 2
    outer = devices * ROWS
    half = outer // 2
    hbm = pl.BlockSpec(memory_space=pltpu.HBM)
    dma = pltpu.SemaphoreType.DMA

    def f32(*shape):
        return pltpu.VMEM(shape, F32)

    def bf16(*shape):
        return pltpu.VMEM(shape, BF16)

    operands = (
        proj, cotangent, short_w.transpose(0, 2, 1), filter_in, filter_out.T, rates.reshape(1, channels), *tables
    )
    shapes = (
        jax.ShapeDtypeStruct(proj.shape, BF16),
        jax.ShapeDtypeStruct((3, 3, channels), F32),
        jax.ShapeDtypeStruct((channels, order), F32),
        jax.ShapeDtypeStruct((feats, order), F32),
    )
    results = pl.pallas_call(
        functools.partial(kernel, devices, y_size),
        out_shape=shapes,
        in_specs=[hbm] * 11,
        out_specs=(pl.BlockSpec(memory_space=pltpu.VMEM),) * 4,
        scratch_shapes=[
            bf16(*proj.shape),
            bf16(*cotangent.shape),
            f32(3, 3, channels),
            f32(feats, order),
            f32(channels, order),
            f32(1, channels),
            bf16(2, outer, outer),
            bf16(2, outer + 2 * EXTRA, outer),
            f32(2, half, LANES),
            bf16(2, 2 * LANES, 2 * LANES),
            bf16(2, 2 * LANES, 2 * LANES),
            f32(feats, TOKENS),
            f32(order, TOKENS),
            f32(channels, TOKENS),
            f32(chips * 4 * ROWS, LANES),
            bf16(chips, 4, ROWS, LANES),
            bf16(chips, 2, 4, ROWS, LANES),
            f32(chips * ROWS, LANES),
            f32(chips, 2, ROWS, LANES),
            f32(3, 2, outer, LANES),
            f32(2, outer, LANES),
            f32(3, half, 2 * LANES),
            f32(3, half + EXTRA, LANES),
            f32(3, half + EXTRA, LANES),
            f32(3, half + EXTRA, LANES),
            f32(chips, ROWS, LANES),
            f32(chips, ROWS, LANES),
            f32(3, half + EXTRA, LANES),
            bf16(chips, 3, ROWS, LANES),
            bf16(chips, 3, ROWS, LANES),
            f32(chips * 3 * ROWS, LANES),
            bf16(2, order, TOKENS),
            bf16(2, feats, TOKENS),
            f32(2, 2, channels // 4, LANES),
            f32(2, channels // 4, LANES),
            f32(Z_SIZE, 2, channels // 4, LANES),
            f32(2, chips // Z_SIZE, channels // 4, LANES),
            f32(2, chips // Z_SIZE * y_size, channels // 4, LANES),
            f32(1, LANES),
            f32(1, LANES),
            f32(chips, 1, LANES),
            dma((11,)), dma((2,)), dma((2,)), dma((chips,)), dma((3,)), dma((3,)), dma((2,)), dma((2,)),
            dma((2,)), dma((2,)), dma((5,)), dma((5,)),
        ],
        compiler_params=pltpu.CompilerParams(
            collective_id=0, has_side_effects=True, vmem_limit_bytes=32 << 20
        ),
    )(*[pltpu.with_memory_space_constraint(x, pltpu.HBM) for x in operands])
    grad_proj, grad_short, grad_out, grad_in = pl.pallas_call(
        move_outputs,
        out_shape=shapes,
        in_specs=[pl.BlockSpec(memory_space=pl.ANY)] * 4,
        out_specs=(hbm,) * 4,
        scratch_shapes=[dma((4,))],
        compiler_params=pltpu.CompilerParams(vmem_limit_bytes=1 << 20),
    )(*results)
    return grad_proj, grad_short.transpose(0, 2, 1), grad_out.T, grad_in


def solution(mesh):
    devices, y_size = mesh.shape["seq"], mesh.shape["ch"]
    tables = make_tables(devices)

    def run(*args):
        return shards(devices, y_size, [jnp.asarray(t) for t in tables], *args)

    return jax.shard_map(
        run,
        mesh=mesh,
        in_specs=(
            P(None, "ch", "seq"),
            P("ch", "seq"),
            P(None, "ch", None),
            P(),
            P(None, "ch"),
            P("ch"),
        ),
        out_specs=(P(None, "ch", "seq"), P(None, "ch", None), P(None, "ch"), P()),
        check_vma=False,
    )
```
